32 devices in a mesh: dp: 8 (over z, y), seq: 4 (over x, core).
Axes of the slice: x: 2, y: 2, z: 4, core: 2. Of those that a mesh axis runs over, the one named last changes fastest.
Arguments:
- tokens: bfloat16 [8, 512, 768], P('dp', 'seq'), may hold values from -6 to 6
- cotangent: bfloat16 [8, 512, 768], P('dp', 'seq'), may hold values from -6 to 6
- segment_ids: int32 [8, 512], P('dp', 'seq'), may hold values from 0 to 7, never falling along the last dimension, each value on 1 to 256 neighbouring positions
- pad_mask: int32 [8, 512], P('dp', 'seq'), may hold values 0 or 1
- routes: int32 [8, 512, 2], P('dp', 'seq'), may hold values from 0 to 3, all different within a row; in each aligned block of 128 rows (0 to 127, 128 to 255, ..., all dimensions but the last counted through in order) at most 96 rows name the same one
- gate_weights: float32 [8, 512, 2], P('dp', 'seq'), may hold values from 0.25 to 1
- gain_one: float32 [768], replicated, may hold values from 0.5 to 1.5
- w_qkv: bfloat16 [768, 2304], P(('dp', 'seq')), may hold values from -0.21875 to 0.21875
- w_attn: bfloat16 [768, 768], P(('dp', 'seq')), may hold values from -1.75 to 1.75
- rel_table: bfloat16 [12, 32], replicated, may hold values from -4 to 4
- gain_two: float32 [768], replicated, may hold values from 0.5 to 1.5
- w_expert_in: bfloat16 [4, 768, 3072], P(None, ('dp', 'seq')), may hold values from -0.21875 to 0.21875
- w_expert_out: bfloat16 [4, 3072, 768], P(None, ('dp', 'seq')), may hold values from -0.109375 to 0.109375
Outputs:
- output: bfloat16 [8, 512, 768], P('dp', 'seq')
- grad_tokens: float32 [8, 512, 768], P('dp', 'seq')
- grad_gain_one: float32 [768], replicated
- grad_w_qkv: float32 [768, 2304], P(('dp', 'seq'))
- grad_w_attn: float32 [768, 768], P(('dp', 'seq'))
- grad_rel_table: float32 [12, 32], replicated
- grad_gain_two: float32 [768], replicated
- grad_expert_in: float32 [4, 768, 3072], P(None, ('dp', 'seq'))
- grad_expert_out: float32 [4, 3072, 768], P(None, ('dp', 'seq'))
The draws below stay inside these ranges and needn't reach their ends.
Inputs may be any that keep to these rules, and one draw needn't show every extreme that they name: `routes`: the two experts of a token differ. Among the rows of one device no expert is named more than 96 times, and in some device's rows one expert is named exactly 96 times. `segment_ids`: ids never fall along a sequence; a document has 1 to 256 positions, and one has exactly that many.
All inputs are finite; a program needn't handle non-finite values. No bound on the sum of `pad_mask` on one device may be relied on, other than what follows from the above.
Results may differ from the reference program's by a relative error of at most 0.011.
Values may be sent and summed in bfloat16 or wider, within the bound.
No kernel may reach another device: no remote copies, remote signals or barrier semaphores. Data moves between devices by JAX's collectives and lax.ppermute only.
A program may use at most 320 MiB of HBM per device.

```python
import math
import jax
import jax.numpy as jnp
import numpy as np
from jax import lax

D = 768
HEADS = 12
FF = 3072
EXPERTS = 4
TOP = 2
BUCKETS = 32
MAX_DIST = 128
TOK_DEV = 128
CAP = 96
LENGTH = 512
SEQS = 8
N_SEQ = 4


def set_ends(entries, key, low, high):
    extent = entries.shape
    spot = [jax.random.randint(jax.random.fold_in(key, axis), (), 0, extent[axis]) for axis in range(len(extent))]
    entries = entries.at[tuple(spot)].set(low)
    longest = extent.index(max(extent))
    spot[longest] = (spot[longest] + 1) % extent[longest]
    return entries.at[tuple(spot)].set(high)


def shard_levels(stream_key, dims, split, low, top_value):
    loudness = 1.0
    for dim, parts in split:
        draws = jax.random.uniform(jax.random.fold_in(jax.random.fold_in(stream_key, 6), dim), (parts,), jnp.float32, low / len(split), top_value / len(split))
        loudness = loudness * jnp.repeat(jnp.exp(draws), dims[dim] // parts).reshape((-1,) + (1,) * (len(dims) - 1 - dim))
    return loudness


def length_profile(count, total, bound, skew):
    loads = [(1 << 20) // math.isqrt(standing ** skew) + 1 for standing in range(2, count + 1)]
    spare, given = total - bound - (count - 1), [1] * (count - 1)
    while spare > 0:
        free = [i for i in range(count - 1) if given[i] < bound]
        pool, budget = sum([loads[i] for i in free]), spare
        for i in free:
            addition = min(bound - given[i], max(1, budget * loads[i] // pool), spare)
            given[i] = given[i] + addition
            spare = spare - addition
    return np.array([bound] + given)


def uneven_parts(rng, amount, total, most, lean):
    if amount == 2:
        one = jax.random.randint(rng, (), max(1, total - most), min(most, total - 1) + 1)
        return jnp.stack([one, total - one])
    tallies = jnp.asarray(length_profile(amount, total, most, lean), jnp.int32)
    twos = (amount - 1) // 2
    giver, sink = tallies[1:1 + 2 * twos:2], tallies[2:2 + 2 * twos:2]
    room = jnp.minimum(giver - 1, most - sink)
    passed = jax.random.randint(jax.random.fold_in(rng, 1), (twos,), 0, 1 << 20) % (room + 1)
    tallies = tallies.at[1:1 + 2 * twos:2].set(giver - passed).at[2:2 + 2 * twos:2].set(sink + passed)
    return tallies[jax.random.permutation(jax.random.fold_in(rng, 2), amount)]


def shared_out(rng, own, number, rows, amount, top, most, lean):
    ranking = jax.random.permutation(rng, amount)
    crowded, ordinary = load_shares(amount, rows * top, most, lean, True), load_shares(amount, rows * top, most, lean, False)
    places = jnp.arange(amount)

    def named(tallies, rotation):
        used = int((tallies > 0).sum())
        fixed = max(1, used // 4)
        shifted = fixed + (places - fixed + rotation * (used - fixed)) % max(1, amount - fixed)
        return jnp.zeros((amount,), jnp.int32).at[ranking[jnp.where(places < fixed, places, shifted)]].set(jnp.asarray(tallies, jnp.int32))

    tallies = jnp.where(number % 4 == 0, named(crowded, number // 4), named(ordinary, number - number // 4 - 1))
    mixed = jax.random.permutation(jax.random.fold_in(own, 3), amount)
    source_of, receiver = mixed[0:amount // 2 * 2:2], mixed[1:amount // 2 * 2:2]
    margin = jnp.minimum(tallies[source_of] - 1, most - tallies[receiver]) // 2
    margin = jnp.where((source_of == ranking[0]) | (receiver == ranking[0]) | (tallies[receiver] == 0), 0, jnp.maximum(margin, 0))
    shifted = jax.random.randint(jax.random.fold_in(own, 4), (amount // 2,), 0, 1 << 20) % (margin + 1)
    tallies = tallies.at[source_of].add(-shifted).at[receiver].add(shifted)
    members = jnp.searchsorted(jnp.cumsum(tallies), jnp.arange(rows * top), side="right").astype(jnp.int32)
    listing = members.reshape(top, rows).T
    listing = listing[jax.random.permutation(jax.random.fold_in(own, 1), rows)]
    rotation = jax.random.randint(jax.random.fold_in(own, 2), (rows, 1), 0, top)
    return jnp.take_along_axis(listing, (jnp.arange(top)[None, :] + rotation) % top, axis=1)


def load_shares(amount, total, limit, lean, full):
    loads = [(1 << 20) // math.isqrt(grade ** lean) + 1 for grade in range(1, amount + 1)]
    largest = limit if full else min(limit, max(-(-total // amount), total * loads[0] // sum(loads)))
    least = 1 if total - largest >= amount - 1 else 0
    holding, rest = [largest] + [least] * (amount - 1), total - largest - least * (amount - 1)
    while rest > 0:
        free = [i for i in range(1, amount) if holding[i] < largest] or [i for i in range(1, amount) if holding[i] < limit]
        mass, budget = sum([loads[i] for i in free]), rest
        for i in free:
            addition = min(limit - holding[i], max(1, budget * loads[i] // mass), rest)
            holding[i] = holding[i] + addition
            rest = rest - addition
    return np.array(holding)


def gaussian(key, dims, width, limit, cuts=(), kind=jnp.bfloat16):
    gain = shard_levels(key, dims, cuts, -0.22, 0.18) if cuts else 1.0
    drawn = jax.random.normal(key, dims, jnp.float32) * width * gain
    return jnp.minimum(jnp.maximum(drawn, -limit), limit).astype(kind)


def setup_inputs(seed: int = 0) -> dict:
    splits = jax.random.split(jax.random.key(seed), 14)
    tokens = gaussian(splits[0], (SEQS, LENGTH, D), 1.0, 6.0, ((0, 8), (1, 4)))
    cotangent = gaussian(splits[1], (SEQS, LENGTH, D), 1.0, 6.0, ((0, 8), (1, 4)))
    segment_ids = jax.vmap(lambda own: jnp.searchsorted(jnp.cumsum(uneven_parts(own, 2 * N_SEQ, LENGTH, LENGTH // 2, 2)), jnp.arange(LENGTH), side="right"))(jax.random.split(splits[2], SEQS)).reshape((SEQS, LENGTH)).astype(jnp.int32)
    pad_mask = set_ends((jax.random.randint(splits[3], (SEQS, LENGTH), 0, 8) < 7).astype(jnp.int32), jax.random.fold_in(splits[3], 1), 0, 1)
    routes_keys = jax.random.split(jax.random.fold_in(splits[4], 1), SEQS * LENGTH // TOK_DEV)
    routes_turns = jax.random.permutation(jax.random.fold_in(splits[4], 3), SEQS * LENGTH // TOK_DEV)
    routes = jax.vmap(lambda own, number: shared_out(jax.random.fold_in(splits[4], 2), own, number, TOK_DEV, EXPERTS, TOP, CAP, 1))(routes_keys, routes_turns).reshape((SEQS, LENGTH, TOP))
    gate_weights = jnp.clip(0.25 + 0.75 * jax.random.uniform(splits[5], (SEQS, LENGTH, TOP), jnp.float32) ** shard_levels(splits[5], (SEQS, LENGTH, TOP), ((0, 8), (1, 4)), -0.2, 0.2), 0.25, 1.0)
    gain_one = jnp.clip(1.0 + 0.1 * jax.random.normal(splits[6], (D,), jnp.float32), 0.5, 1.5)
    w_qkv = gaussian(splits[7], (D, 3 * D), D ** -0.5, 0.21875, ((0, 32),))
    w_attn = gaussian(splits[8], (D, D), (D // 64) ** -0.5, 1.75, ((0, 32),))
    rel_table = gaussian(splits[9], (HEADS, BUCKETS), 1.0, 4.0)
    gain_two = jnp.clip(1.0 + 0.1 * jax.random.normal(splits[10], (D,), jnp.float32), 0.5, 1.5)
    w_expert_in = gaussian(splits[11], (EXPERTS, D, FF), D ** -0.5, 0.21875, ((1, 32),))
    w_expert_out = gaussian(splits[12], (EXPERTS, FF, D), FF ** -0.5, 0.109375, ((1, 32),))
    return {"tokens": tokens, "cotangent": cotangent, "segment_ids": segment_ids, "pad_mask": pad_mask, "routes": routes, "gate_weights": gate_weights, "gain_one": gain_one, "w_qkv": w_qkv, "w_attn": w_attn, "rel_table": rel_table, "gain_two": gain_two, "w_expert_in": w_expert_in, "w_expert_out": w_expert_out}


HIGHEST = lax.Precision.HIGHEST

@jax.custom_vjp
def low(v):
    return lax.optimization_barrier(v.astype(jnp.bfloat16)).astype(jnp.float32)

@jax.custom_vjp
def low_back(v):
    return v

def low_keep(v):
    return (low(v), None)

def low_pass(kept, grad):
    return (grad,)

def back_keep(v):
    return (v, None)

def back_low(kept, grad):
    return (low(grad),)
low.defvjp(low_keep, low_pass)
low_back.defvjp(back_keep, back_low)

def bucket_edges():
    exact_span = BUCKETS // 2
    distance = np.arange(1, 8 * MAX_DIST + 1)
    widened = np.maximum(distance, exact_span) / exact_span
    spread = exact_span + (np.log(widened) / np.log(MAX_DIST / exact_span) * exact_span).astype(np.int64)
    bucket_of = np.where(distance < exact_span, distance, np.minimum(spread, BUCKETS - 1))
    return np.array([distance[np.argmax(bucket_of >= target)] for target in range(1, BUCKETS)], dtype=np.int32)

def norm_rows(values, gain_vec):
    factor = lax.rsqrt(lax.optimization_barrier(jnp.mean(values * values, axis=-1, keepdims=True)) + 1e-06)
    return values * factor * gain_vec

def sequence_forward(weights, inputs, segment, padding, route_ids, gate_vals):
    gain_first, w_proj, w_mix, rel_bias, gain_second, w_first, w_second = weights
    length = inputs.shape[0]
    model_width = inputs.shape[1]
    head_count = rel_bias.shape[0]
    head_size = model_width // head_count
    normed_one = low(norm_rows(inputs, gain_first))
    project = jnp.dot(normed_one, w_proj, precision=HIGHEST)
    queries = low_back(low(project[:, :model_width])).reshape(length, head_count, head_size)
    keys_all = low_back(low(project[:, model_width:2 * model_width])).reshape(length, head_count, head_size)
    values_all = low_back(low(project[:, 2 * model_width:])).reshape(length, head_count, head_size)
    positions = jnp.arange(length, dtype=jnp.int32)
    key_info = jnp.where(padding == 1, segment, -1)
    edges = jnp.asarray(bucket_edges(), dtype=jnp.int32)
    query_block = math.gcd(length, 512)

    def attend(block_start):
        query_pos = block_start + jnp.arange(query_block, dtype=jnp.int32)
        query_heads = lax.dynamic_slice_in_dim(queries, block_start, query_block, 0)
        query_seg = lax.dynamic_slice_in_dim(segment, block_start, query_block, 0)
        distance = query_pos[:, None] - positions[None, :]
        bucket_of = jnp.searchsorted(edges, distance, side='right').astype(jnp.int32)
        scores = jnp.einsum('qhd,khd->hqk', query_heads, keys_all, precision=HIGHEST) * head_size ** (-0.5)
        scores = low_back(scores + rel_bias[:, bucket_of])
        allowed = (distance >= 0) & ((key_info[None, :] == query_seg[:, None]) | (distance == 0))
        weights_p = low(jax.nn.softmax(jnp.where(allowed[None], scores, -1e+30), axis=-1))
        return jnp.einsum('hqk,khd->qhd', weights_p, values_all, precision=HIGHEST)
    starts = jnp.arange(0, length, query_block, dtype=jnp.int32)
    mixed = lax.map(jax.checkpoint(attend), starts).reshape(length, model_width)
    attn_out = low_back(jnp.dot(low_back(low(mixed)), w_mix, precision=HIGHEST))
    hidden_one = inputs + attn_out
    normed_two = low(norm_rows(hidden_one, gain_second))
    expert_ids = jnp.arange(w_first.shape[0], dtype=jnp.int32)
    choose = lax.optimization_barrier(jnp.sum(gate_vals[:, :, None] * (route_ids[:, :, None] == expert_ids).astype(jnp.float32), axis=1))

    def expert_step(running, pieces):
        first_w, second_w, weight_col = pieces
        entered = low_back(normed_two)
        pre_act = low_back(jnp.dot(entered, first_w, precision=HIGHEST))
        active = low(jax.nn.gelu(pre_act))
        result = low_back(jnp.dot(active, second_w, precision=HIGHEST))
        return (running + low(weight_col[:, None] * result), None)
    moe_sum, unused_out = lax.scan(jax.checkpoint(expert_step), jnp.zeros_like(inputs), (w_first, w_second, choose.T))
    return hidden_one + moe_sum

def reference(tokens, cotangent, segment_ids, pad_mask, routes, gate_weights, gain_one, w_qkv, w_attn, rel_table, gain_two, w_expert_in, w_expert_out):
    params = (gain_one.astype(jnp.float32), w_qkv.astype(jnp.float32), w_attn.astype(jnp.float32), rel_table.astype(jnp.float32), gain_two.astype(jnp.float32), w_expert_in.astype(jnp.float32), w_expert_out.astype(jnp.float32))
    inputs = tokens.astype(jnp.float32)

    def forward(values, weights):

        def per_sequence(pieces):
            return sequence_forward(weights, pieces[0], pieces[1], pieces[2], pieces[3], pieces[4])
        return lax.map(jax.checkpoint(per_sequence), (values, segment_ids, pad_mask, routes, gate_weights))
    outputs, pullback = jax.vjp(forward, inputs, params)
    grad_inputs, grads = pullback(cotangent.astype(jnp.float32))
    return (outputs.astype(jnp.bfloat16), grad_inputs, grads[0], grads[1], grads[2], grads[3], grads[4], grads[5], grads[6])
```

```python
import math

import jax
import jax.numpy as jnp
import numpy as np
from jax import lax
from jax.experimental import pallas as pl
from jax.experimental.pallas import tpu as pltpu
from jax.sharding import Mesh
from jax.sharding import PartitionSpec as P

BUCKETS = 32
MAX_DIST = 128
CAP = 96


def bucket_edges():
    exact_span = BUCKETS // 2
    distance = np.arange(1, 8 * MAX_DIST + 1)
    widened = np.maximum(distance, exact_span) / exact_span
    spread = exact_span + (np.log(widened) / np.log(MAX_DIST / exact_span) * exact_span).astype(
        np.int64
    )
    bucket_of = np.where(distance < exact_span, distance, np.minimum(spread, BUCKETS - 1))
    return np.array(
        [distance[np.argmax(bucket_of >= target)] for target in range(1, BUCKETS)], dtype=np.int32
    )


def norm_stats(values):
    factor = lax.rsqrt(jnp.mean(values * values, axis=-1, keepdims=True) + 1e-06)
    return (values * factor, factor)


def norm_back(grad_normed, scaled, factor, gain_vec):
    grad_scaled = grad_normed * gain_vec
    inner_mean = jnp.mean(grad_scaled * scaled, axis=-1, keepdims=True)
    return (factor * (grad_scaled - scaled * inner_mean), jnp.sum(grad_normed * scaled, axis=0))


def make_onehot(distance, edges_np):
    bucket_of = jnp.sum((distance[:, :, None] >= edges_np).astype(jnp.int32), axis=-1)
    return (bucket_of[:, :, None] == jnp.arange(BUCKETS, dtype=jnp.int32)).astype(jnp.bfloat16)


def block_bias(table_low, edges_np, distance):
    far_away = jnp.min(distance) >= int(edges_np[-1])

    def block_detailed(unused):
        return jnp.einsum(
            "qkb,hb->hqk",
            make_onehot(distance, edges_np),
            table_low,
            preferred_element_type=jnp.float32,
        )

    def block_constant(unused):
        last_col = table_low[:, BUCKETS - 1].astype(jnp.float32)
        return jnp.broadcast_to(last_col[:, None, None], (table_low.shape[0],) + distance.shape)

    return lax.cond(far_away, block_constant, block_detailed, 0)


def table_part(grad_low, edges_np, distance):
    far_away = jnp.min(distance) >= int(edges_np[-1])

    def table_detailed(unused):
        return jnp.einsum(
            "hqk,qkb->hb",
            grad_low,
            make_onehot(distance, edges_np),
            preferred_element_type=jnp.float32,
        )

    def table_constant(unused):
        totals = jnp.sum(grad_low, axis=(1, 2), dtype=jnp.float32)
        return totals[:, None] * (jnp.arange(BUCKETS) == BUCKETS - 1).astype(jnp.float32)

    return lax.cond(far_away, table_constant, table_detailed, 0)


def body(
    tokens,
    cotangent,
    segment_ids,
    pad_mask,
    routes,
    gate_weights,
    gain_one,
    w_qkv,
    w_attn,
    rel_table,
    gain_two,
    w_expert_in,
    w_expert_out,
):
    gathered = (
        lax.all_gather(w_qkv, ("dp", "seq"), axis=0, tiled=True),
        lax.all_gather(w_attn, ("dp", "seq"), axis=0, tiled=True),
        lax.all_gather(w_expert_in, ("dp", "seq"), axis=1, tiled=True),
        lax.all_gather(w_expert_out, ("dp", "seq"), axis=1, tiled=True),
    )
    full_qkv, full_attn, full_in, full_out = gathered
    inputs = tokens[0].astype(jnp.float32)
    row_count, model_width = inputs.shape
    head_count = rel_table.shape[0]
    head_size = model_width // head_count
    score_scale = head_size ** (-0.5)
    seg_local = segment_ids[0]
    seq_index = lax.axis_index("seq")
    length = row_count * lax.axis_size("seq")
    key_block = math.gcd(length, 512)
    query_pos = seq_index * row_count + jnp.arange(row_count, dtype=jnp.int32)
    block_count = ((seq_index + 1) * row_count + key_block - 1) // key_block
    edges_np = bucket_edges()
    scaled_one, factor_one = norm_stats(inputs)
    normed_one = (scaled_one * gain_one).astype(jnp.bfloat16)
    project = jnp.dot(normed_one, full_qkv, preferred_element_type=jnp.float32)
    queries = project[:, :model_width].astype(jnp.bfloat16)
    keys_local = project[:, model_width : 2 * model_width].astype(jnp.bfloat16)
    values_local = project[:, 2 * model_width :].astype(jnp.bfloat16)
    info_local = jnp.where(pad_mask[0] == 1, seg_local, -1)
    keys_all, values_all, info_all, seg_all = (
        lax.all_gather(keys_local, "seq", axis=0, tiled=True),
        lax.all_gather(values_local, "seq", axis=0, tiled=True),
        lax.all_gather(info_local, "seq", axis=0, tiled=True),
        lax.all_gather(seg_local, "seq", axis=0, tiled=True),
    )
    query_heads = queries.reshape(row_count, head_count, head_size)

    def block_scores(block_index):
        key_start = block_index * key_block
        key_heads = lax.dynamic_slice_in_dim(keys_all, key_start, key_block, 0).reshape(
            key_block, head_count, head_size
        )
        value_heads = lax.dynamic_slice_in_dim(values_all, key_start, key_block, 0).reshape(
            key_block, head_count, head_size
        )
        info_block = lax.dynamic_slice_in_dim(info_all, key_start, key_block, 0)
        key_pos = key_start + jnp.arange(key_block, dtype=jnp.int32)
        distance = query_pos[:, None] - key_pos[None, :]
        allowed = (distance >= 0) & ((info_block[None, :] == seg_local[:, None]) | (distance == 0))
        raw_scores = (
            jnp.einsum("qhd,khd->hqk", query_heads, key_heads, preferred_element_type=jnp.float32)
            * score_scale
        )
        raw_scores = raw_scores + block_bias(rel_table, edges_np, distance)
        return (
            jnp.where(allowed[None], raw_scores, -1e30),
            allowed[None],
            key_heads,
            value_heads,
            distance,
            key_start,
        )

    def max_step(block_index, running):
        top_score, row_total = running
        pieces = block_scores(block_index)
        new_top = jnp.maximum(top_score, jnp.max(pieces[0], axis=-1))
        exponent = jnp.where(pieces[1], jnp.exp(pieces[0] - new_top[:, :, None]), 0.0)
        return (new_top, row_total * jnp.exp(top_score - new_top) + jnp.sum(exponent, axis=-1))

    start_top = jnp.full((head_count, row_count), -1e30, jnp.float32)
    start_total = jnp.zeros((head_count, row_count), jnp.float32)
    top_score, row_total = lax.fori_loop(0, block_count, max_step, (start_top, start_total))
    log_total = top_score + jnp.log(row_total)

    def out_step(block_index, mixed_acc):
        pieces = block_scores(block_index)
        prob_low = jnp.where(pieces[1], jnp.exp(pieces[0] - log_total[:, :, None]), 0.0).astype(
            jnp.bfloat16
        )
        return mixed_acc + jnp.einsum(
            "hqk,khd->qhd", prob_low, pieces[3], preferred_element_type=jnp.float32
        )

    mixed_full = lax.fori_loop(
        0, block_count, out_step, jnp.zeros((row_count, head_count, head_size), jnp.float32)
    )
    mixed_low = mixed_full.reshape(row_count, model_width).astype(jnp.bfloat16)
    hidden_one = inputs + jnp.dot(mixed_low, full_attn, preferred_element_type=jnp.float32)
    scaled_two, factor_two = norm_stats(hidden_one)
    normed_two = (scaled_two * gain_two).astype(jnp.bfloat16)
    route_local = routes[0]
    expert_count = w_expert_in.shape[0]
    top_count = route_local.shape[1]
    flat_routes = route_local.reshape(-1)
    expert_hot = (flat_routes[:, None] == jnp.arange(expert_count, dtype=jnp.int32)).astype(
        jnp.int32
    )
    earlier = jnp.cumsum(expert_hot, axis=0) - expert_hot
    slot_index = jnp.sum(earlier * expert_hot, axis=1)
    slot_float = (
        (slot_index[:, None] == jnp.arange(CAP, dtype=jnp.int32))
        .astype(jnp.float32)
        .reshape(row_count, top_count, CAP)
    )
    expert_float = expert_hot.astype(jnp.float32).reshape(row_count, top_count, expert_count)
    dispatch = jnp.einsum(
        "tke,tkc->ect",
        expert_float.astype(jnp.bfloat16),
        slot_float.astype(jnp.bfloat16),
        preferred_element_type=jnp.float32,
    ).astype(jnp.bfloat16)
    slot_gate = jnp.einsum(
        "tke,tkc,tk->ec", expert_float, slot_float, gate_weights[0], precision=lax.Precision.HIGHEST
    )
    entered = jnp.einsum(
        "ect,td->ecd", dispatch, normed_two, preferred_element_type=jnp.float32
    ).astype(jnp.bfloat16)
    pre_act = jnp.einsum("ecd,edf->ecf", entered, full_in, preferred_element_type=jnp.float32)
    active = jax.nn.gelu(pre_act).astype(jnp.bfloat16)
    result = jnp.einsum("ecf,efd->ecd", active, full_out, preferred_element_type=jnp.float32)
    expert_low = (slot_gate[:, :, None] * result).astype(jnp.bfloat16)
    combined = jnp.einsum("ect,ecd->td", dispatch, expert_low, preferred_element_type=jnp.float32)
    output = (hidden_one + combined).astype(jnp.bfloat16)
    regathered = (
        lax.all_gather(w_qkv, ("dp", "seq"), axis=0, tiled=True),
        lax.all_gather(w_attn, ("dp", "seq"), axis=0, tiled=True),
        lax.all_gather(w_expert_in, ("dp", "seq"), axis=1, tiled=True),
        lax.all_gather(w_expert_out, ("dp", "seq"), axis=1, tiled=True),
    )
    back_qkv, back_attn, back_in, back_out = regathered
    grad_out_low = cotangent[0]
    grad_slots = jnp.einsum(
        "ect,td->ecd", dispatch, grad_out_low, preferred_element_type=jnp.float32
    )
    grad_result = (slot_gate[:, :, None] * grad_slots).astype(jnp.bfloat16)
    grad_w_out = jnp.einsum("ecf,ecd->efd", active, grad_result, preferred_element_type=jnp.float32)
    grad_active = jnp.einsum(
        "ecd,efd->ecf", grad_result, back_out, preferred_element_type=jnp.float32
    )
    unused_value, gelu_pull = jax.vjp(jax.nn.gelu, pre_act)
    grad_pre = gelu_pull(grad_active)[0].astype(jnp.bfloat16)
    grad_w_in = jnp.einsum("ecd,ecf->edf", entered, grad_pre, preferred_element_type=jnp.float32)
    grad_entered = jnp.einsum(
        "ecf,edf->ecd", grad_pre, back_in, preferred_element_type=jnp.float32
    ).astype(jnp.bfloat16)
    grad_normed_two = jnp.einsum(
        "ect,ecd->td", dispatch, grad_entered, preferred_element_type=jnp.float32
    )
    grad_hidden_norm, grad_gain_two = norm_back(grad_normed_two, scaled_two, factor_two, gain_two)
    grad_hidden = grad_out_low.astype(jnp.float32) + grad_hidden_norm
    branch_low = grad_hidden.astype(jnp.bfloat16)
    grad_w_attn = lax.dot_general(
        mixed_low, branch_low, (((0,), (0,)), ((), ())), preferred_element_type=jnp.float32
    )
    grad_mixed = lax.dot_general(
        branch_low, back_attn, (((1,), (1,)), ((), ())), preferred_element_type=jnp.float32
    ).astype(jnp.bfloat16)
    grad_mixed_heads = grad_mixed.reshape(row_count, head_count, head_size)
    row_delta = jnp.sum(grad_mixed_heads.astype(jnp.float32) * mixed_full, axis=-1).T

    def score_grads(pieces):
        prob_full = jnp.where(pieces[1], jnp.exp(pieces[0] - log_total[:, :, None]), 0.0)
        grad_prob = jnp.einsum(
            "qhd,khd->hqk", grad_mixed_heads, pieces[3], preferred_element_type=jnp.float32
        )
        grad_score = (prob_full * (grad_prob - row_delta[:, :, None])).astype(jnp.bfloat16)
        return (prob_full.astype(jnp.bfloat16), grad_score)

    start_query = jnp.zeros((row_count, head_count, head_size), jnp.float32)
    start_table = jnp.zeros((head_count, BUCKETS), jnp.float32)

    def back_step(block_index, running):
        grad_query, grad_key_all, grad_value_all, grad_table = running
        pieces = block_scores(block_index)
        prob_low, grad_score = score_grads(pieces)
        grad_query = (
            grad_query
            + jnp.einsum("hqk,khd->qhd", grad_score, pieces[2], preferred_element_type=jnp.float32)
            * score_scale
        )
        key_part = (
            jnp.einsum("hqk,qhd->khd", grad_score, query_heads, preferred_element_type=jnp.float32)
            * score_scale
        ).reshape(key_block, model_width)
        value_part = jnp.einsum(
            "hqk,qhd->khd", prob_low, grad_mixed_heads, preferred_element_type=jnp.float32
        ).reshape(key_block, model_width)
        grad_key_all = lax.dynamic_update_slice_in_dim(grad_key_all, key_part, pieces[5], 0)
        grad_value_all = lax.dynamic_update_slice_in_dim(grad_value_all, value_part, pieces[5], 0)
        grad_table = grad_table + table_part(grad_score, edges_np, pieces[4])
        return (grad_query, grad_key_all, grad_value_all, grad_table)

    start_back = (
        start_query,
        jnp.zeros((length, model_width), jnp.float32),
        jnp.zeros((length, model_width), jnp.float32),
        start_table,
    )
    grad_query, grad_key_all, grad_value_all, grad_table = lax.fori_loop(
        0, block_count, back_step, start_back
    )
    grad_keys, grad_values = (
        lax.psum_scatter(
            grad_key_all.astype(jnp.bfloat16), "seq", scatter_dimension=0, tiled=True
        ).astype(jnp.float32),
        lax.psum_scatter(
            grad_value_all.astype(jnp.bfloat16), "seq", scatter_dimension=0, tiled=True
        ).astype(jnp.float32),
    )
    grad_proj = jnp.concatenate(
        [
            grad_query.reshape(row_count, model_width).astype(jnp.bfloat16),
            grad_keys.astype(jnp.bfloat16),
            grad_values.astype(jnp.bfloat16),
        ],
        axis=1,
    )
    grad_w_qkv = lax.dot_general(
        normed_one, grad_proj, (((0,), (0,)), ((), ())), preferred_element_type=jnp.float32
    )
    grad_normed_one = lax.dot_general(
        grad_proj, back_qkv, (((1,), (1,)), ((), ())), preferred_element_type=jnp.float32
    )
    grad_input_norm, grad_gain_one = norm_back(grad_normed_one, scaled_one, factor_one, gain_one)
    grad_inputs = grad_hidden + grad_input_norm
    table_total, gain_one_total, gain_two_total = lax.psum(
        (grad_table, grad_gain_one, grad_gain_two), ("dp", "seq")
    )
    shares = (
        lax.psum_scatter(grad_w_qkv, ("dp", "seq"), scatter_dimension=0, tiled=True),
        lax.psum_scatter(grad_w_attn, ("dp", "seq"), scatter_dimension=0, tiled=True),
        lax.psum_scatter(grad_w_in, ("dp", "seq"), scatter_dimension=1, tiled=True),
        lax.psum_scatter(grad_w_out, ("dp", "seq"), scatter_dimension=1, tiled=True),
    )
    return (
        output[None],
        grad_inputs[None],
        gain_one_total,
        shares[0],
        shares[1],
        table_total,
        gain_two_total,
        shares[2],
        shares[3],
    )


def rows_solution(mesh):
    return jax.shard_map(
        body,
        mesh=mesh,
        in_specs=(
            P("dp", "seq", None),
            P("dp", "seq", None),
            P("dp", "seq"),
            P("dp", "seq"),
            P("dp", "seq", None),
            P("dp", "seq", None),
            P(),
            P(("dp", "seq"), None),
            P(("dp", "seq"), None),
            P(),
            P(),
            P(None, ("dp", "seq"), None),
            P(None, ("dp", "seq"), None),
        ),
        out_specs=(
            P("dp", "seq", None),
            P("dp", "seq", None),
            P(),
            P(("dp", "seq"), None),
            P(("dp", "seq"), None),
            P(),
            P(),
            P(None, ("dp", "seq"), None),
            P(None, ("dp", "seq"), None),
        ),
        check_vma=False,
    )


F32 = jnp.float32
BF16 = jnp.bfloat16
ROWS = 128
EXT = 128
AXES = ("z", "y", "x", "c")
VMEM_BYTES = 48 * 1024 * 1024


def swap(value, axis, step=1):
    size = lax.axis_size(axis)
    return lax.ppermute(value, axis, [(i, i ^ step) for i in range(size)])


def gather_seq(value):
    pair = jnp.concatenate([value, swap(value, "x")], axis=0)
    return jnp.concatenate([pair, swap(pair, "c")], axis=0)


def reduce_seq(part):
    half = part.shape[0] // 2
    quarter = half // 2
    got = swap(part[half:].astype(BF16), "c")
    pair = part[:half].astype(F32) + got.astype(F32)
    got_pair = swap(pair[quarter:].astype(BF16), "x")
    return pair[:quarter] + got_pair.astype(F32)


def mm(a, b):
    return lax.dot_general(a, b, (((1,), (0,)), ((), ())), preferred_element_type=F32)


def mm_t(a, b):
    return lax.dot_general(a, b, (((1,), (1,)), ((), ())), preferred_element_type=F32)


def t_mm(a, b):
    return lax.dot_general(a, b, (((0,), (0,)), ((), ())), preferred_element_type=F32)


def slot_rows(block, me):
    mask = jnp.bitwise_xor(me, block)
    slot = jnp.right_shift(mask, 1) + 2 * jnp.bitwise_and(mask, 1)
    return pl.ds(pl.multiple_of(slot * ROWS, ROWS), ROWS)


def tile_distance(offset):
    row = lax.broadcasted_iota(jnp.int32, (ROWS, ROWS), 0)
    col = lax.broadcasted_iota(jnp.int32, (ROWS, ROWS), 1)
    return offset + row - col


def fill_bias(bias_ref, tab_ref, heads):
    edges = [int(e) for e in bucket_edges()]
    for near in range(2):
        distance = tile_distance(near * ROWS)
        tiles = [jnp.full((ROWS, ROWS), tab_ref[h, 0], F32) for h in range(heads)]
        for b, edge in enumerate(edges):
            above = distance >= edge
            tiles = [jnp.where(above, tab_ref[h, b + 1], tiles[h]) for h in range(heads)]
        for h in range(heads):
            bias_ref[near * heads + h] = tiles[h]


def read_marks(xs_ref, me, width, blocks):
    seg_cols, info_rows = [], []
    for i in range(blocks):
        marks = xs_ref[slot_rows(i, me), width : width + EXT].astype(F32)
        seg_cols.append(marks[:, 0:1])
        info_rows.append(marks.T[1:2, :])
    return seg_cols, info_rows


def mask_tiles(i, seg_cols, info_rows):
    tiles = []
    for j in range(i + 1):
        seen = info_rows[j] == seg_cols[i]
        if j == i:
            distance = tile_distance(0)
            seen = (distance == 0) | ((distance > 0) & seen)
        tiles.append(jnp.where(seen, 0.0, -1e30))
    return tiles


def add_tiles(i, h, heads, masks, bias_ref, tab_ref):
    tiles = []
    for j in range(i + 1):
        if i - j < 2:
            tiles.append(masks[j] + bias_ref[(i - j) * heads + h])
        else:
            tiles.append(masks[j] + tab_ref[h, BUCKETS - 1])
    return jnp.concatenate(tiles, axis=1) if len(tiles) > 1 else tiles[0]


def attend_kernel(
    me_ref, tab_ref, xs_ref, gain_ref, wq_ref, n1_ref, qkv_ref, mixed_ref, lse_ref, bias_ref
):
    me = me_ref[0]
    width = gain_ref.shape[1]
    third = wq_ref.shape[1] // 3
    heads = tab_ref.shape[0]
    size = third // heads
    blocks = xs_ref.shape[0] // ROWS
    scale = size ** (-0.5)
    fill_bias(bias_ref, tab_ref, heads)
    for i in range(blocks):
        x = xs_ref[slot_rows(i, me), :width].astype(F32)
        factor = lax.rsqrt(jnp.mean(x * x, axis=-1, keepdims=True) + 1e-06)
        n1_ref[i * ROWS : (i + 1) * ROWS, :] = (x * factor * gain_ref[...]).astype(BF16)
    qkv_ref[...] = mm(n1_ref[...], wq_ref[...]).astype(BF16)
    seg_cols, info_rows = read_marks(xs_ref, me, width, blocks)
    lane = lax.broadcasted_iota(jnp.int32, (ROWS, EXT), 1)
    for i in range(blocks):
        masks = mask_tiles(i, seg_cols, info_rows)
        span = (i + 1) * ROWS
        rows = slice(i * ROWS, span)
        outs = []
        lse = jnp.zeros((ROWS, EXT), F32)
        for h in range(heads):
            q = qkv_ref[rows, h * size : (h + 1) * size]
            k = qkv_ref[0:span, third + h * size : third + (h + 1) * size]
            v = qkv_ref[0:span, 2 * third + h * size : 2 * third + (h + 1) * size]
            scores = mm_t(q, k) * scale + add_tiles(i, h, heads, masks, bias_ref, tab_ref)
            top = jnp.max(scores, axis=-1, keepdims=True)
            weight = jnp.exp(scores - top)
            total = jnp.sum(weight, axis=-1, keepdims=True)
            prob = (weight * (1.0 / total)).astype(BF16)
            outs.append(mm(prob, v))
            lse = jnp.where(lane == h, top + jnp.log(total), lse)
        mixed_ref[slot_rows(i, me), :] = jnp.concatenate(outs, axis=1).astype(BF16)
        lse_ref[rows, :] = lse


def attend_back_kernel(
    me_ref,
    tab_ref,
    branch_ref,
    watt_ref,
    qkv_ref,
    n1_ref,
    lse_ref,
    xs_ref,
    wq_ref,
    mixed_ref,
    gwq_ref,
    gno_ref,
    gain_ref,
    gtab_ref,
    gwatt_ref,
    bias_ref,
    dk_ref,
    dv_ref,
    proj_ref,
):
    me = me_ref[0]
    width = watt_ref.shape[1]
    third = wq_ref.shape[1] // 3
    heads = tab_ref.shape[0]
    size = third // heads
    blocks = xs_ref.shape[0] // ROWS
    scale = size ** (-0.5)
    fill_bias(bias_ref, tab_ref, heads)
    seg_cols, info_rows = read_marks(xs_ref, me, width, blocks)
    dk_ref[...] = jnp.zeros_like(dk_ref)
    dv_ref[...] = jnp.zeros_like(dv_ref)
    near = [[jnp.zeros((ROWS, ROWS), F32) for _ in range(heads)] for _ in range(2)]
    far = [jnp.zeros((1, ROWS), F32) for _ in range(heads)]
    for i in range(blocks):
        masks = mask_tiles(i, seg_cols, info_rows)
        span = (i + 1) * ROWS
        rows = slice(i * ROWS, span)
        grad_mixed = mm_t(branch_ref[slot_rows(i, me), :], watt_ref[...]).astype(BF16)
        for h in range(heads):
            own = slice(h * size, (h + 1) * size)
            q = qkv_ref[rows, own]
            k = qkv_ref[0:span, third + h * size : third + (h + 1) * size]
            v = qkv_ref[0:span, 2 * third + h * size : 2 * third + (h + 1) * size]
            dm = grad_mixed[:, own]
            scores = mm_t(q, k) * scale + add_tiles(i, h, heads, masks, bias_ref, tab_ref)
            prob = jnp.exp(scores - lse_ref[rows, h : h + 1])
            grad_prob = mm_t(dm, v)
            delta = jnp.sum(prob * grad_prob, axis=-1, keepdims=True)
            grad_score = (prob * (grad_prob - delta)).astype(BF16)
            proj_ref[rows, own] = (mm(grad_score, k) * scale).astype(BF16)
            dk_ref[0:span, own] += t_mm(grad_score, q)
            dv_ref[0:span, own] += t_mm(prob.astype(BF16), dm)
            for j in range(i + 1):
                tile = grad_score[:, j * ROWS : (j + 1) * ROWS].astype(F32)
                if i - j < 2:
                    near[i - j][h] = near[i - j][h] + tile
                else:
                    far[h] = far[h] + jnp.sum(tile, axis=0, keepdims=True)
    proj_ref[:, third : 2 * third] = (dk_ref[...] * scale).astype(BF16)
    proj_ref[:, 2 * third :] = dv_ref[...].astype(BF16)
    edges = [int(e) for e in bucket_edges()]
    buckets = []
    for n in range(2):
        distance = tile_distance(n * ROWS)
        count = jnp.zeros((ROWS, ROWS), jnp.int32)
        for edge in edges:
            count = count + (distance >= edge).astype(jnp.int32)
        buckets.append(count)
    for b in range(BUCKETS):
        picks = [buckets[n] == b for n in range(2)]
        for h in range(heads):
            line = jnp.sum(
                jnp.where(picks[0], near[0][h], 0.0) + jnp.where(picks[1], near[1][h], 0.0),
                axis=0,
                keepdims=True,
            )
            if b == BUCKETS - 1:
                line = line + far[h]
            gtab_ref[h * BUCKETS + b : h * BUCKETS + b + 1, :] = line
    gwq_ref[...] = t_mm(n1_ref[...], proj_ref[...]).astype(BF16)
    gain = jnp.zeros((1, width), F32)
    for i in range(blocks):
        x = xs_ref[slot_rows(i, me), :width].astype(F32)
        factor = lax.rsqrt(jnp.mean(x * x, axis=-1, keepdims=True) + 1e-06)
        part = mm_t(proj_ref[i * ROWS : (i + 1) * ROWS, :], wq_ref[...])
        gno_ref[slot_rows(i, me), :] = part.astype(BF16)
        gain = gain + jnp.sum(part * (x * factor), axis=0, keepdims=True)
    gain_ref[...] = jnp.broadcast_to(gain, gain_ref.shape)
    gwatt_ref[...] = t_mm(mixed_ref[...], branch_ref[...]).astype(BF16)


def expert_kernel(x_ref, g_ref, w1_ref, w2_ref, pick_ref, dx_ref, act_ref, pre_ref, out_ref):
    width = x_ref.shape[1]
    step = 256
    root = math.sqrt(2.0 / math.pi)

    def tile(t, carry):
        rows = pl.ds(pl.multiple_of(t * step, step), step)
        choose = mm(g_ref[rows, width:], pick_ref[...])
        v = mm(x_ref[rows, :], w1_ref[...])
        square = v * v
        curve = jnp.tanh(root * v * (1.0 + 0.044715 * square))
        half = 0.5 * (1.0 + curve)
        slope = half + 0.5 * v * (1.0 - curve * curve) * (root * (1.0 + 3 * 0.044715 * square))
        act = (choose * (v * half)).astype(BF16)
        act_ref[rows, :] = act
        grad_act = mm_t(g_ref[rows, :width], w2_ref[...])
        grad_pre = (choose * grad_act * slope).astype(BF16)
        pre_ref[rows, :] = grad_pre
        dx_ref[rows, :] = mm_t(grad_pre, w1_ref[...]).astype(BF16)
        out_ref[rows, :] = mm(act, w2_ref[...]).astype(BF16)
        return carry

    lax.fori_loop(0, x_ref.shape[0] // step, tile, 0)


def weight_grad_kernel(count, *refs):
    xs, gs, acts, pres = (refs[n * count : (n + 1) * count] for n in range(4))
    own1_ref, far1_ref, own2_ref, far2_ref = refs[4 * count :]
    width = xs[0].shape[1]
    half = own1_ref.shape[1]
    own1, far1, own2, far2 = 0.0, 0.0, 0.0, 0.0
    for x, pre in zip(xs, pres):
        own1 = own1 + t_mm(x[...], pre[:, :half])
    own1_ref[...] = own1
    for x, pre in zip(xs, pres):
        far1 = far1 + t_mm(x[...], pre[:, half:])
    far1_ref[...] = far1.astype(BF16)
    for act, g in zip(acts, gs):
        own2 = own2 + t_mm(act[:, :half], g[:, :width])
    own2_ref[...] = own2
    for act, g in zip(acts, gs):
        far2 = far2 + t_mm(act[:, half:], g[:, :width])
    far2_ref[...] = far2.astype(BF16)


def call(kernel, outs, args, scratch=(), scalars=0, flops=0, moved=0, exps=0):
    smem = pl.BlockSpec(memory_space=pltpu.SMEM)
    vmem = pl.BlockSpec(memory_space=pltpu.VMEM)
    return pl.pallas_call(
        kernel,
        out_shape=[jax.ShapeDtypeStruct(shape, dtype) for shape, dtype in outs],
        in_specs=[smem] * scalars + [vmem] * (len(args) - scalars),
        out_specs=[vmem] * len(outs),
        scratch_shapes=list(scratch),
        compiler_params=pltpu.CompilerParams(vmem_limit_bytes=VMEM_BYTES),
        cost_estimate=pl.CostEstimate(flops=flops, bytes_accessed=moved, transcendentals=exps),
    )(*args)


def head_body(
    tokens,
    cotangent,
    segment_ids,
    pad_mask,
    routes,
    gate_weights,
    gain_one,
    w_qkv,
    w_attn,
    rel_table,
    gain_two,
    w_expert_in,
    w_expert_out,
):
    x_low = tokens[0]
    g_low = cotangent[0]
    rows, width = x_low.shape
    size_z, size_y, size_x, size_c = (lax.axis_size(a) for a in AXES)
    parts = size_x * size_c
    devices = size_z * size_y * parts
    me = lax.axis_index(("x", "c"))
    head_count = rel_table.shape[0]
    heads = head_count // parts
    third = width // parts
    length = rows * parts
    experts, shard, ff = w_expert_in.shape
    ff_own = ff // devices
    me_arr = me.astype(jnp.int32).reshape(1)

    seg = segment_ids[0]
    info = jnp.where(pad_mask[0] == 1, seg, -1)
    marks = jnp.stack([seg, info], axis=1).astype(BF16)
    x_ext = jnp.concatenate([x_low, jnp.pad(marks, ((0, 0), (0, EXT - 2)))], axis=1)
    xs = gather_seq(x_ext)

    by_part = w_qkv.reshape(shard, 3, parts, third).transpose(2, 0, 1, 3)
    by_part = by_part.reshape(1, parts, shard, 3 * third)
    qkv_send = jnp.broadcast_to(by_part, (devices // parts, parts, shard, 3 * third))
    wq = lax.all_to_all(
        qkv_send.reshape(devices, shard, 3 * third), AXES, 0, 0, tiled=True
    ).reshape(width, 3 * third)

    in_send = w_expert_in.reshape(experts, shard, devices, ff_own).transpose(2, 1, 0, 3)
    in_send = in_send.reshape(devices, shard, experts * ff_own)
    in_send, wq = lax.optimization_barrier((in_send, wq))
    w1_own = lax.all_to_all(in_send, AXES, 0, 0, tiled=True).reshape(width, experts * ff_own)
    w2_own = w_expert_out.reshape(experts * ff_own, width)
    w1 = jnp.concatenate([w1_own, swap(w1_own, "y")], axis=1)
    w2 = jnp.concatenate([w2_own, swap(w2_own, "y")], axis=0)

    groups = devices // parts
    to_part = [((i % groups) * parts + i // groups) for i in range(devices)]
    att_one = lax.ppermute(w_attn, AXES, [(i, to_part[i]) for i in range(devices)])
    watt = lax.all_gather(att_one, ("z", "y"), axis=0, tiled=True)

    expert_ids = jnp.arange(experts, dtype=jnp.int32)
    choose = jnp.sum(
        gate_weights[0][:, :, None] * (routes[0][:, :, None] == expert_ids).astype(F32), axis=1
    )
    choose_hi = choose.astype(BF16)
    choose_lo = (choose - choose_hi.astype(F32)).astype(BF16)
    g_ext = jnp.concatenate(
        [g_low, choose_hi, choose_lo, jnp.zeros((rows, EXT - 2 * experts), BF16)], axis=1
    )
    g_ext, wq = lax.optimization_barrier((g_ext, wq))
    g_z = jnp.stack([g_ext] + [swap(g_ext, "z", k) for k in range(1, size_z)])
    g_x = swap(g_z, "x")
    g_zx = jnp.concatenate([g_z, g_x], axis=1)
    g_c = swap(g_zx, "c")
    g_all = jnp.concatenate([g_zx, g_c], axis=1)

    table = lax.dynamic_slice_in_dim(rel_table, me * heads, heads, 0).astype(F32)
    n1, qkv, mixed, lse = call(
        attend_kernel,
        [
            ((length, width), BF16),
            ((length, 3 * third), BF16),
            ((length, third), BF16),
            ((length, EXT), F32),
        ],
        [me_arr, table, xs, gain_one.reshape(1, width), wq],
        scratch=[pltpu.VMEM((2 * heads, ROWS, ROWS), F32)],
        scalars=2,
        flops=2 * length * width * 3 * third + 4 * length * length * third,
        moved=2 * length * width * 4,
        exps=heads * length * length,
    )
    branch_part = mm(mixed, watt)
    inputs = x_low.astype(F32)
    hidden_one = inputs + reduce_seq(branch_part)
    scaled_two, factor_two = norm_stats(hidden_one)
    normed_two = (scaled_two * gain_two).astype(BF16)

    pick_np = np.zeros((EXT, 2 * experts * ff_own), np.float32)
    for e in range(experts):
        for y in range(2):
            start = (y * experts + e) * ff_own
            pick_np[[e, experts + e], start : start + ff_own] = 1.0
    pick = jnp.asarray(pick_np, BF16)
    ff_two = 2 * experts * ff_own
    x_blocks, g_blocks, act_blocks, pre_blocks, out_blocks = [], [], [], [], []
    grad_normed_two = None
    for k in range(size_z):
        x_block = gather_seq(normed_two if k == 0 else swap(normed_two, "z", k))
        g_block = g_all[k]
        dx, act, pre, out = call(
            expert_kernel,
            [
                ((length, width), BF16),
                ((length, ff_two), BF16),
                ((length, ff_two), BF16),
                ((length, width), BF16),
            ],
            [x_block, g_block, w1, w2, pick],
            flops=8 * length * width * ff_two,
            moved=2 * (6 * length * width + 2 * width * ff_two),
            exps=length * ff_two,
        )
        x_blocks.append(x_block)
        g_blocks.append(g_block)
        act_blocks.append(act)
        pre_blocks.append(pre)
        out_blocks.append(out)
        back = reduce_seq(dx)
        if k:
            back = swap(back.astype(BF16), "z", k).astype(F32)
        grad_normed_two = back if grad_normed_two is None else grad_normed_two + back

    outs = jnp.stack(out_blocks)
    half = length // 2
    out_c = outs[:, :half].astype(F32) + swap(outs[:, half:], "c").astype(F32)
    out_x = out_c[:, :rows] + swap(out_c[:, rows:].astype(BF16), "x").astype(F32)
    combined = out_x[0]
    for k in range(1, size_z):
        combined = combined + swap(out_x[k].astype(BF16), "z", k).astype(F32)
    output = (hidden_one + combined).astype(BF16)

    ff_half = experts * ff_own
    own1, far1, own2, far2 = call(
        lambda *refs: weight_grad_kernel(size_z, *refs),
        [
            ((width, ff_half), F32),
            ((width, ff_half), BF16),
            ((ff_half, width), F32),
            ((ff_half, width), BF16),
        ],
        [*x_blocks, *g_blocks, *act_blocks, *pre_blocks],
        flops=4 * size_z * length * width * ff_two,
        moved=2 * 4 * size_z * length * width,
    )
    grad_w_out = (own2 + swap(far2, "y").astype(F32)).reshape(experts, ff_own, width)
    in_sum = (own1 + swap(far1, "y").astype(F32)).astype(BF16)
    in_got = lax.all_to_all(
        in_sum.reshape(devices, shard, ff_half), AXES, 0, 0, tiled=True
    )
    grad_w_in = (
        in_got.reshape(devices, shard, experts, ff_own)
        .transpose(2, 1, 0, 3)
        .reshape(experts, shard, ff)
        .astype(F32)
    )

    grad_hidden_norm, gain_two_part = norm_back(grad_normed_two, scaled_two, factor_two, gain_two)
    grad_hidden = g_low.astype(F32) + grad_hidden_norm
    branch = gather_seq(grad_hidden.astype(BF16))
    gwq, gno, gain_one_part, table_part, gwatt = call(
        attend_back_kernel,
        [
            ((width, 3 * third), BF16),
            ((length, width), BF16),
            ((8, width), F32),
            ((heads * BUCKETS, ROWS), F32),
            ((third, width), BF16),
        ],
        [me_arr, table, branch, watt, qkv, n1, lse, xs, wq, mixed],
        scratch=[
            pltpu.VMEM((2 * heads, ROWS, ROWS), F32),
            pltpu.VMEM((length, third), F32),
            pltpu.VMEM((length, third), F32),
            pltpu.VMEM((length, 3 * third), BF16),
        ],
        scalars=2,
        flops=6 * length * width * 3 * third + 10 * length * length * third,
        moved=2 * length * width * 6,
        exps=heads * length * length,
    )
    grad_normed_one = reduce_seq(gno)
    scaled_one, factor_one = norm_stats(inputs)
    grad_input_norm, unused_gain = norm_back(grad_normed_one, scaled_one, factor_one, gain_one)
    grad_inputs = grad_hidden + grad_input_norm

    att_share = lax.psum_scatter(gwatt, ("z", "y"), scatter_dimension=0, tiled=True)
    grad_w_attn = lax.ppermute(
        att_share, AXES, [(to_part[i], i) for i in range(devices)]
    ).astype(F32)

    small_table = lax.dynamic_update_slice_in_dim(
        jnp.zeros((head_count, BUCKETS), F32),
        jnp.sum(table_part, axis=1).reshape(heads, BUCKETS),
        me * heads,
        0,
    )
    small = jnp.concatenate([gain_one_part[0], gain_two_part, small_table.reshape(-1)])
    small_hi = small.astype(BF16)
    small_lo = (small - small_hi.astype(F32)).astype(BF16)
    count = small.shape[0]
    extra = -(-2 * count // (3 * third * 8)) * 8
    small_rows = jnp.pad(
        jnp.concatenate([small_hi, small_lo]), (0, extra * 3 * third - 2 * count)
    ).reshape(1, extra, 3 * third)
    last_send = jnp.concatenate(
        [
            gwq.reshape(devices, shard, 3 * third),
            jnp.broadcast_to(small_rows, (devices, extra, 3 * third)),
        ],
        axis=1,
    )
    last = lax.all_to_all(last_send, AXES, 0, 0, tiled=True).astype(F32)
    grad_w_qkv = (
        jnp.sum(last[:, :shard].reshape(groups, parts, shard, 3, third), axis=0)
        .transpose(1, 2, 0, 3)
        .reshape(shard, 3 * width)
    )
    small_sum = jnp.sum(last[:, shard:], axis=0).reshape(-1)
    totals = small_sum[:count] + small_sum[count : 2 * count]
    return (
        output[None],
        grad_inputs[None],
        totals[:width],
        grad_w_qkv,
        grad_w_attn,
        totals[2 * width :].reshape(head_count, BUCKETS),
        totals[width : 2 * width],
        grad_w_in,
        grad_w_out,
    )


def heads_fit(mesh):
    return mesh.shape["seq"] == 4 and mesh.shape["dp"] == 8


def solution(mesh):
    if not heads_fit(mesh):
        return rows_solution(mesh)
    grid = Mesh(mesh.devices.reshape(mesh.shape["dp"] // 2, 2, mesh.shape["seq"] // 2, 2), AXES)
    by_token = P(("z", "y"), ("x", "c"))
    by_row = P(AXES, None)
    by_second = P(None, AXES, None)
    return jax.shard_map(
        head_body,
        mesh=grid,
        in_specs=(
            by_token,
            by_token,
            by_token,
            by_token,
            by_token,
            by_token,
            P(),
            by_row,
            by_row,
            P(),
            P(),
            by_second,
            by_second,
        ),
        out_specs=(
            by_token,
            by_token,
            P(),
            by_row,
            by_row,
            P(),
            P(),
            by_second,
            by_second,
        ),
        check_vma=False,
    )
```

```python
import functools
import math

import jax
import jax.numpy as jnp
import numpy as np
from jax import lax
from jax.experimental import pallas as pl
from jax.experimental.pallas import tpu as pltpu
from jax.sharding import Mesh
from jax.sharding import PartitionSpec as P

BUCKETS = 32
MAX_DIST = 128
CAP = 96


def bucket_edges():
    exact_span = BUCKETS // 2
    distance = np.arange(1, 8 * MAX_DIST + 1)
    widened = np.maximum(distance, exact_span) / exact_span
    spread = exact_span + (np.log(widened) / np.log(MAX_DIST / exact_span) * exact_span).astype(
        np.int64
    )
    bucket_of = np.where(distance < exact_span, distance, np.minimum(spread, BUCKETS - 1))
    return np.array(
        [distance[np.argmax(bucket_of >= target)] for target in range(1, BUCKETS)], dtype=np.int32
    )


def norm_stats(values):
    factor = lax.rsqrt(jnp.mean(values * values, axis=-1, keepdims=True) + 1e-06)
    return (values * factor, factor)


def norm_back(grad_normed, scaled, factor, gain_vec):
    grad_scaled = grad_normed * gain_vec
    inner_mean = jnp.mean(grad_scaled * scaled, axis=-1, keepdims=True)
    return (factor * (grad_scaled - scaled * inner_mean), jnp.sum(grad_normed * scaled, axis=0))


def make_onehot(distance, edges_np):
    bucket_of = jnp.sum((distance[:, :, None] >= edges_np).astype(jnp.int32), axis=-1)
    return (bucket_of[:, :, None] == jnp.arange(BUCKETS, dtype=jnp.int32)).astype(jnp.bfloat16)


def block_bias(table_low, edges_np, distance):
    far_away = jnp.min(distance) >= int(edges_np[-1])

    def block_detailed(unused):
        return jnp.einsum(
            "qkb,hb->hqk",
            make_onehot(distance, edges_np),
            table_low,
            preferred_element_type=jnp.float32,
        )

    def block_constant(unused):
        last_col = table_low[:, BUCKETS - 1].astype(jnp.float32)
        return jnp.broadcast_to(last_col[:, None, None], (table_low.shape[0],) + distance.shape)

    return lax.cond(far_away, block_constant, block_detailed, 0)


def table_part(grad_low, edges_np, distance):
    far_away = jnp.min(distance) >= int(edges_np[-1])

    def table_detailed(unused):
        return jnp.einsum(
            "hqk,qkb->hb",
            grad_low,
            make_onehot(distance, edges_np),
            preferred_element_type=jnp.float32,
        )

    def table_constant(unused):
        totals = jnp.sum(grad_low, axis=(1, 2), dtype=jnp.float32)
        return totals[:, None] * (jnp.arange(BUCKETS) == BUCKETS - 1).astype(jnp.float32)

    return lax.cond(far_away, table_constant, table_detailed, 0)


def body(
    tokens,
    cotangent,
    segment_ids,
    pad_mask,
    routes,
    gate_weights,
    gain_one,
    w_qkv,
    w_attn,
    rel_table,
    gain_two,
    w_expert_in,
    w_expert_out,
):
    gathered = (
        lax.all_gather(w_qkv, ("dp", "seq"), axis=0, tiled=True),
        lax.all_gather(w_attn, ("dp", "seq"), axis=0, tiled=True),
        lax.all_gather(w_expert_in, ("dp", "seq"), axis=1, tiled=True),
        lax.all_gather(w_expert_out, ("dp", "seq"), axis=1, tiled=True),
    )
    full_qkv, full_attn, full_in, full_out = gathered
    inputs = tokens[0].astype(jnp.float32)
    row_count, model_width = inputs.shape
    head_count = rel_table.shape[0]
    head_size = model_width // head_count
    score_scale = head_size ** (-0.5)
    seg_local = segment_ids[0]
    seq_index = lax.axis_index("seq")
    length = row_count * lax.axis_size("seq")
    key_block = math.gcd(length, 512)
    query_pos = seq_index * row_count + jnp.arange(row_count, dtype=jnp.int32)
    block_count = ((seq_index + 1) * row_count + key_block - 1) // key_block
    edges_np = bucket_edges()
    scaled_one, factor_one = norm_stats(inputs)
    normed_one = (scaled_one * gain_one).astype(jnp.bfloat16)
    project = jnp.dot(normed_one, full_qkv, preferred_element_type=jnp.float32)
    queries = project[:, :model_width].astype(jnp.bfloat16)
    keys_local = project[:, model_width : 2 * model_width].astype(jnp.bfloat16)
    values_local = project[:, 2 * model_width :].astype(jnp.bfloat16)
    info_local = jnp.where(pad_mask[0] == 1, seg_local, -1)
    keys_all, values_all, info_all, seg_all = (
        lax.all_gather(keys_local, "seq", axis=0, tiled=True),
        lax.all_gather(values_local, "seq", axis=0, tiled=True),
        lax.all_gather(info_local, "seq", axis=0, tiled=True),
        lax.all_gather(seg_local, "seq", axis=0, tiled=True),
    )
    query_heads = queries.reshape(row_count, head_count, head_size)

    def block_scores(block_index):
        key_start = block_index * key_block
        key_heads = lax.dynamic_slice_in_dim(keys_all, key_start, key_block, 0).reshape(
            key_block, head_count, head_size
        )
        value_heads = lax.dynamic_slice_in_dim(values_all, key_start, key_block, 0).reshape(
            key_block, head_count, head_size
        )
        info_block = lax.dynamic_slice_in_dim(info_all, key_start, key_block, 0)
        key_pos = key_start + jnp.arange(key_block, dtype=jnp.int32)
        distance = query_pos[:, None] - key_pos[None, :]
        allowed = (distance >= 0) & ((info_block[None, :] == seg_local[:, None]) | (distance == 0))
        raw_scores = (
            jnp.einsum("qhd,khd->hqk", query_heads, key_heads, preferred_element_type=jnp.float32)
            * score_scale
        )
        raw_scores = raw_scores + block_bias(rel_table, edges_np, distance)
        return (
            jnp.where(allowed[None], raw_scores, -1e30),
            allowed[None],
            key_heads,
            value_heads,
            distance,
            key_start,
        )

    def max_step(block_index, running):
        top_score, row_total = running
        pieces = block_scores(block_index)
        new_top = jnp.maximum(top_score, jnp.max(pieces[0], axis=-1))
        exponent = jnp.where(pieces[1], jnp.exp(pieces[0] - new_top[:, :, None]), 0.0)
        return (new_top, row_total * jnp.exp(top_score - new_top) + jnp.sum(exponent, axis=-1))

    start_top = jnp.full((head_count, row_count), -1e30, jnp.float32)
    start_total = jnp.zeros((head_count, row_count), jnp.float32)
    top_score, row_total = lax.fori_loop(0, block_count, max_step, (start_top, start_total))
    log_total = top_score + jnp.log(row_total)

    def out_step(block_index, mixed_acc):
        pieces = block_scores(block_index)
        prob_low = jnp.where(pieces[1], jnp.exp(pieces[0] - log_total[:, :, None]), 0.0).astype(
            jnp.bfloat16
        )
        return mixed_acc + jnp.einsum(
            "hqk,khd->qhd", prob_low, pieces[3], preferred_element_type=jnp.float32
        )

    mixed_full = lax.fori_loop(
        0, block_count, out_step, jnp.zeros((row_count, head_count, head_size), jnp.float32)
    )
    mixed_low = mixed_full.reshape(row_count, model_width).astype(jnp.bfloat16)
    hidden_one = inputs + jnp.dot(mixed_low, full_attn, preferred_element_type=jnp.float32)
    scaled_two, factor_two = norm_stats(hidden_one)
    normed_two = (scaled_two * gain_two).astype(jnp.bfloat16)
    route_local = routes[0]
    expert_count = w_expert_in.shape[0]
    top_count = route_local.shape[1]
    flat_routes = route_local.reshape(-1)
    expert_hot = (flat_routes[:, None] == jnp.arange(expert_count, dtype=jnp.int32)).astype(
        jnp.int32
    )
    earlier = jnp.cumsum(expert_hot, axis=0) - expert_hot
    slot_index = jnp.sum(earlier * expert_hot, axis=1)
    slot_float = (
        (slot_index[:, None] == jnp.arange(CAP, dtype=jnp.int32))
        .astype(jnp.float32)
        .reshape(row_count, top_count, CAP)
    )
    expert_float = expert_hot.astype(jnp.float32).reshape(row_count, top_count, expert_count)
    dispatch = jnp.einsum(
        "tke,tkc->ect",
        expert_float.astype(jnp.bfloat16),
        slot_float.astype(jnp.bfloat16),
        preferred_element_type=jnp.float32,
    ).astype(jnp.bfloat16)
    slot_gate = jnp.einsum(
        "tke,tkc,tk->ec", expert_float, slot_float, gate_weights[0], precision=lax.Precision.HIGHEST
    )
    entered = jnp.einsum(
        "ect,td->ecd", dispatch, normed_two, preferred_element_type=jnp.float32
    ).astype(jnp.bfloat16)
    pre_act = jnp.einsum("ecd,edf->ecf", entered, full_in, preferred_element_type=jnp.float32)
    active = jax.nn.gelu(pre_act).astype(jnp.bfloat16)
    result = jnp.einsum("ecf,efd->ecd", active, full_out, preferred_element_type=jnp.float32)
    expert_low = (slot_gate[:, :, None] * result).astype(jnp.bfloat16)
    combined = jnp.einsum("ect,ecd->td", dispatch, expert_low, preferred_element_type=jnp.float32)
    output = (hidden_one + combined).astype(jnp.bfloat16)
    regathered = (
        lax.all_gather(w_qkv, ("dp", "seq"), axis=0, tiled=True),
        lax.all_gather(w_attn, ("dp", "seq"), axis=0, tiled=True),
        lax.all_gather(w_expert_in, ("dp", "seq"), axis=1, tiled=True),
        lax.all_gather(w_expert_out, ("dp", "seq"), axis=1, tiled=True),
    )
    back_qkv, back_attn, back_in, back_out = regathered
    grad_out_low = cotangent[0]
    grad_slots = jnp.einsum(
        "ect,td->ecd", dispatch, grad_out_low, preferred_element_type=jnp.float32
    )
    grad_result = (slot_gate[:, :, None] * grad_slots).astype(jnp.bfloat16)
    grad_w_out = jnp.einsum("ecf,ecd->efd", active, grad_result, preferred_element_type=jnp.float32)
    grad_active = jnp.einsum(
        "ecd,efd->ecf", grad_result, back_out, preferred_element_type=jnp.float32
    )
    unused_value, gelu_pull = jax.vjp(jax.nn.gelu, pre_act)
    grad_pre = gelu_pull(grad_active)[0].astype(jnp.bfloat16)
    grad_w_in = jnp.einsum("ecd,ecf->edf", entered, grad_pre, preferred_element_type=jnp.float32)
    grad_entered = jnp.einsum(
        "ecf,edf->ecd", grad_pre, back_in, preferred_element_type=jnp.float32
    ).astype(jnp.bfloat16)
    grad_normed_two = jnp.einsum(
        "ect,ecd->td", dispatch, grad_entered, preferred_element_type=jnp.float32
    )
    grad_hidden_norm, grad_gain_two = norm_back(grad_normed_two, scaled_two, factor_two, gain_two)
    grad_hidden = grad_out_low.astype(jnp.float32) + grad_hidden_norm
    branch_low = grad_hidden.astype(jnp.bfloat16)
    grad_w_attn = lax.dot_general(
        mixed_low, branch_low, (((0,), (0,)), ((), ())), preferred_element_type=jnp.float32
    )
    grad_mixed = lax.dot_general(
        branch_low, back_attn, (((1,), (1,)), ((), ())), preferred_element_type=jnp.float32
    ).astype(jnp.bfloat16)
    grad_mixed_heads = grad_mixed.reshape(row_count, head_count, head_size)
    row_delta = jnp.sum(grad_mixed_heads.astype(jnp.float32) * mixed_full, axis=-1).T

    def score_grads(pieces):
        prob_full = jnp.where(pieces[1], jnp.exp(pieces[0] - log_total[:, :, None]), 0.0)
        grad_prob = jnp.einsum(
            "qhd,khd->hqk", grad_mixed_heads, pieces[3], preferred_element_type=jnp.float32
        )
        grad_score = (prob_full * (grad_prob - row_delta[:, :, None])).astype(jnp.bfloat16)
        return (prob_full.astype(jnp.bfloat16), grad_score)

    start_query = jnp.zeros((row_count, head_count, head_size), jnp.float32)
    start_table = jnp.zeros((head_count, BUCKETS), jnp.float32)

    def back_step(block_index, running):
        grad_query, grad_key_all, grad_value_all, grad_table = running
        pieces = block_scores(block_index)
        prob_low, grad_score = score_grads(pieces)
        grad_query = (
            grad_query
            + jnp.einsum("hqk,khd->qhd", grad_score, pieces[2], preferred_element_type=jnp.float32)
            * score_scale
        )
        key_part = (
            jnp.einsum("hqk,qhd->khd", grad_score, query_heads, preferred_element_type=jnp.float32)
            * score_scale
        ).reshape(key_block, model_width)
        value_part = jnp.einsum(
            "hqk,qhd->khd", prob_low, grad_mixed_heads, preferred_element_type=jnp.float32
        ).reshape(key_block, model_width)
        grad_key_all = lax.dynamic_update_slice_in_dim(grad_key_all, key_part, pieces[5], 0)
        grad_value_all = lax.dynamic_update_slice_in_dim(grad_value_all, value_part, pieces[5], 0)
        grad_table = grad_table + table_part(grad_score, edges_np, pieces[4])
        return (grad_query, grad_key_all, grad_value_all, grad_table)

    start_back = (
        start_query,
        jnp.zeros((length, model_width), jnp.float32),
        jnp.zeros((length, model_width), jnp.float32),
        start_table,
    )
    grad_query, grad_key_all, grad_value_all, grad_table = lax.fori_loop(
        0, block_count, back_step, start_back
    )
    grad_keys, grad_values = (
        lax.psum_scatter(
            grad_key_all.astype(jnp.bfloat16), "seq", scatter_dimension=0, tiled=True
        ).astype(jnp.float32),
        lax.psum_scatter(
            grad_value_all.astype(jnp.bfloat16), "seq", scatter_dimension=0, tiled=True
        ).astype(jnp.float32),
    )
    grad_proj = jnp.concatenate(
        [
            grad_query.reshape(row_count, model_width).astype(jnp.bfloat16),
            grad_keys.astype(jnp.bfloat16),
            grad_values.astype(jnp.bfloat16),
        ],
        axis=1,
    )
    grad_w_qkv = lax.dot_general(
        normed_one, grad_proj, (((0,), (0,)), ((), ())), preferred_element_type=jnp.float32
    )
    grad_normed_one = lax.dot_general(
        grad_proj, back_qkv, (((1,), (1,)), ((), ())), preferred_element_type=jnp.float32
    )
    grad_input_norm, grad_gain_one = norm_back(grad_normed_one, scaled_one, factor_one, gain_one)
    grad_inputs = grad_hidden + grad_input_norm
    table_total, gain_one_total, gain_two_total = lax.psum(
        (grad_table, grad_gain_one, grad_gain_two), ("dp", "seq")
    )
    shares = (
        lax.psum_scatter(grad_w_qkv, ("dp", "seq"), scatter_dimension=0, tiled=True),
        lax.psum_scatter(grad_w_attn, ("dp", "seq"), scatter_dimension=0, tiled=True),
        lax.psum_scatter(grad_w_in, ("dp", "seq"), scatter_dimension=1, tiled=True),
        lax.psum_scatter(grad_w_out, ("dp", "seq"), scatter_dimension=1, tiled=True),
    )
    return (
        output[None],
        grad_inputs[None],
        gain_one_total,
        shares[0],
        shares[1],
        table_total,
        gain_two_total,
        shares[2],
        shares[3],
    )


def rows_solution(mesh):
    return jax.shard_map(
        body,
        mesh=mesh,
        in_specs=(
            P("dp", "seq", None),
            P("dp", "seq", None),
            P("dp", "seq"),
            P("dp", "seq"),
            P("dp", "seq", None),
            P("dp", "seq", None),
            P(),
            P(("dp", "seq"), None),
            P(("dp", "seq"), None),
            P(),
            P(),
            P(None, ("dp", "seq"), None),
            P(None, ("dp", "seq"), None),
        ),
        out_specs=(
            P("dp", "seq", None),
            P("dp", "seq", None),
            P(),
            P(("dp", "seq"), None),
            P(("dp", "seq"), None),
            P(),
            P(),
            P(None, ("dp", "seq"), None),
            P(None, ("dp", "seq"), None),
        ),
        check_vma=False,
    )


F32 = jnp.float32
BF16 = jnp.bfloat16
ROWS = 128
EXT = 128
TAB_AT = 256
AXES = ("z", "y", "x", "c")
MIB = 1024 * 1024
BYTES_US = 3690000


def swap(value, axis, step=1):
    size = lax.axis_size(axis)
    return lax.ppermute(value, axis, [(i, i ^ step) for i in range(size)])


def after(value, *earlier):
    return lax.optimization_barrier((value, earlier))[0]


def gather_seq(value):
    along_x = swap(value, "x")
    return value, along_x, swap(value, "c"), swap(along_x, "c")


def reduce_seq(keep, send):
    rows = keep.shape[0] // 2
    pair = keep + swap(send, "c").astype(F32)
    return pair[:rows] + swap(pair[rows:].astype(BF16), "x").astype(F32)


def mm(a, b):
    return lax.dot_general(a, b, (((1,), (0,)), ((), ())), preferred_element_type=F32)


def mm_t(a, b):
    return lax.dot_general(a, b, (((1,), (1,)), ((), ())), preferred_element_type=F32)


def t_mm(a, b):
    return lax.dot_general(a, b, (((0,), (0,)), ((), ())), preferred_element_type=F32)


SLOTS = (0, 2, 1, 3)


def slot_rows(slot, me):
    block = jnp.bitwise_xor(me, SLOTS[slot])
    return pl.ds(pl.multiple_of(block * ROWS, ROWS), ROWS)


def tile_distance(offset):
    row = lax.broadcasted_iota(jnp.int32, (ROWS, ROWS), 0)
    col = lax.broadcasted_iota(jnp.int32, (ROWS, ROWS), 1)
    return offset + row - col


def fill_bias(bias_ref, tab_ref, heads):
    edges = [int(e) for e in bucket_edges()]
    for near in range(2):
        distance = tile_distance(near * ROWS)
        tiles = [jnp.full((ROWS, ROWS), tab_ref[h, 0], F32) for h in range(heads)]
        for b, edge in enumerate(edges):
            above = distance >= edge
            tiles = [jnp.where(above, tab_ref[h, b + 1], tiles[h]) for h in range(heads)]
        for h in range(heads):
            bias_ref[near * heads + h] = tiles[h]


def read_marks(xs_ref, width, blocks):
    seg_cols, info_rows = [], []
    for i in range(blocks):
        marks = xs_ref[i * ROWS : (i + 1) * ROWS, width : width + EXT].astype(F32)
        seg_cols.append(marks[:, 0:1])
        info_rows.append(marks.T[1:2, :])
    return seg_cols, info_rows


def mask_tiles(i, seg_cols, info_rows):
    tiles = []
    for j in range(i + 1):
        seen = info_rows[j] == seg_cols[i]
        if j == i:
            distance = tile_distance(0)
            seen = (distance == 0) | ((distance > 0) & seen)
        tiles.append(jnp.where(seen, 0.0, -1e30))
    return tiles


def add_tiles(i, h, heads, masks, bias_ref, tab_ref):
    tiles = []
    for j in range(i + 1):
        if i - j < 2:
            tiles.append(masks[j] + bias_ref[(i - j) * heads + h])
        else:
            tiles.append(masks[j] + tab_ref[h, BUCKETS - 1])
    return jnp.concatenate(tiles, axis=1) if len(tiles) > 1 else tiles[0]


def copies(pairs, sem_ref):
    return [pltpu.make_async_copy(a, b, sem_ref.at[n]) for n, (a, b) in enumerate(pairs)]


def attend_kernel(
    me_ref,
    place_ref,
    tab_ref,
    x0_ref,
    x1_ref,
    x2_ref,
    x3_ref,
    gain_ref,
    *refs,
):
    w_refs = refs[:2]
    mixed_ref = refs[2]
    home = refs[3:8]
    kept = refs[8:13]
    blocks_ref, bias_ref, sem_ref = refs[13:]
    xs_ref, n1_ref, wq_ref, qkv_ref, lse_ref = kept
    out = copies(zip(kept, home), sem_ref)
    me, place = me_ref[0], place_ref[0]
    width = gain_ref.shape[1]
    third = wq_ref.shape[1] // 3
    heads = tab_ref.shape[0]
    size = third // heads
    blocks = xs_ref.shape[0] // ROWS
    devices, shard = blocks_ref.shape[0], blocks_ref.shape[1]
    scale = size ** (-0.5)
    fill_bias(bias_ref, tab_ref, heads)
    for slot, x_ref in enumerate((x0_ref, x1_ref, x2_ref, x3_ref)):
        rows = slot_rows(slot, me)
        xs_ref[rows, :] = x_ref[...]
        x = x_ref[:, :width].astype(F32)
        factor = lax.rsqrt(jnp.mean(x * x, axis=-1, keepdims=True) + 1e-06)
        n1_ref[rows, :] = (x * factor * gain_ref[...]).astype(BF16)
    out[0].start()
    out[1].start()
    for n, w_ref in enumerate(w_refs):
        y = jnp.bitwise_xor(jnp.bitwise_and(place, 1), n)
        for i in range(devices // 2):
            blocks_ref[(2 * (i // blocks) + y) * blocks + i % blocks] = w_ref[i]
    for i in range(devices):
        wq_ref[i * shard : (i + 1) * shard, :] = blocks_ref[i]
    out[2].start()
    qkv_ref[...] = mm(n1_ref[...], wq_ref[...]).astype(BF16)
    out[3].start()
    seg_cols, info_rows = read_marks(xs_ref, width, blocks)
    lane = lax.broadcasted_iota(jnp.int32, (ROWS, EXT), 1)
    for i in range(blocks):
        masks = mask_tiles(i, seg_cols, info_rows)
        span = (i + 1) * ROWS
        rows = slice(i * ROWS, span)
        outs = []
        lse = jnp.zeros((ROWS, EXT), F32)
        for h in range(heads):
            q = qkv_ref[rows, h * size : (h + 1) * size]
            k = qkv_ref[0:span, third + h * size : third + (h + 1) * size]
            v = qkv_ref[0:span, 2 * third + h * size : 2 * third + (h + 1) * size]
            scores = mm_t(q, k) * scale + add_tiles(i, h, heads, masks, bias_ref, tab_ref)
            top = jnp.max(scores, axis=-1, keepdims=True)
            weight = jnp.exp(scores - top)
            total = jnp.sum(weight, axis=-1, keepdims=True)
            prob = (weight * (1.0 / total)).astype(BF16)
            outs.append(mm(prob, v))
            lse = jnp.where(lane == h, top + jnp.log(total), lse)
        mixed_ref[rows, :] = jnp.concatenate(outs, axis=1).astype(BF16)
        lse_ref[rows, :] = lse
    out[4].start()
    for copy in out:
        copy.wait()


def project_kernel(me_ref, mixed_ref, watt_ref, keep_ref, send_ref):
    me = me_ref[0]
    for slot in range(len(SLOTS)):
        part = mm(mixed_ref[slot_rows(slot, me), :], watt_ref[...])
        if slot < 2:
            keep_ref[slot * ROWS : (slot + 1) * ROWS, :] = part
        else:
            send_ref[(slot - 2) * ROWS : (slot - 1) * ROWS, :] = part.astype(BF16)


def attend_back_kernel(
    me_ref,
    place_ref,
    tab_ref,
    b0_ref,
    b1_ref,
    b2_ref,
    b3_ref,
    watt_ref,
    gain_two_ref,
    *refs,
):
    home = refs[:6]
    wkeep_ref, wsend_ref, keep_ref, send_ref = refs[6:10]
    kept = refs[10:16]
    bias_ref, dm_ref, dk_ref, dv_ref, proj_ref, gtab_ref, small_ref, grad_ref, sem_ref = refs[16:]
    xs_ref, n1_ref, wq_ref, qkv_ref, lse_ref, mixed_ref = kept
    fetch = copies(zip(home, kept), sem_ref)
    for copy in fetch:
        copy.start()
    me = me_ref[0]
    width = watt_ref.shape[1]
    third = wq_ref.shape[1] // 3
    heads = tab_ref.shape[0]
    size = third // heads
    blocks = xs_ref.shape[0] // ROWS
    scale = size ** (-0.5)
    fill_bias(bias_ref, tab_ref, heads)
    for slot, b_ref in enumerate((b0_ref, b1_ref, b2_ref, b3_ref)):
        dm_ref[slot_rows(slot, me), :] = mm_t(b_ref[...], watt_ref[...]).astype(BF16)
    for copy in fetch:
        copy.wait()
    seg_cols, info_rows = read_marks(xs_ref, width, blocks)
    dk_ref[...] = jnp.zeros_like(dk_ref)
    dv_ref[...] = jnp.zeros_like(dv_ref)
    near = [[jnp.zeros((ROWS, ROWS), F32) for _ in range(heads)] for _ in range(2)]
    far = [jnp.zeros((1, ROWS), F32) for _ in range(heads)]
    for i in range(blocks):
        masks = mask_tiles(i, seg_cols, info_rows)
        span = (i + 1) * ROWS
        rows = slice(i * ROWS, span)
        for h in range(heads):
            own = slice(h * size, (h + 1) * size)
            q = qkv_ref[rows, own]
            k = qkv_ref[0:span, third + h * size : third + (h + 1) * size]
            v = qkv_ref[0:span, 2 * third + h * size : 2 * third + (h + 1) * size]
            dm = dm_ref[rows, own]
            scores = mm_t(q, k) * scale + add_tiles(i, h, heads, masks, bias_ref, tab_ref)
            prob = jnp.exp(scores - lse_ref[rows, h : h + 1])
            grad_prob = mm_t(dm, v)
            delta = jnp.sum(prob * grad_prob, axis=-1, keepdims=True)
            grad_score = (prob * (grad_prob - delta)).astype(BF16)
            proj_ref[rows, own] = (mm(grad_score, k) * scale).astype(BF16)
            dk_ref[0:span, own] += t_mm(grad_score, q)
            dv_ref[0:span, own] += t_mm(prob.astype(BF16), dm)
            for j in range(i + 1):
                tile = grad_score[:, j * ROWS : (j + 1) * ROWS].astype(F32)
                if i - j < 2:
                    near[i - j][h] = near[i - j][h] + tile
                else:
                    far[h] = far[h] + jnp.sum(tile, axis=0, keepdims=True)
    proj_ref[:, third : 2 * third] = (dk_ref[...] * scale).astype(BF16)
    proj_ref[:, 2 * third :] = dv_ref[...].astype(BF16)
    gtab_ref[...] = jnp.zeros_like(gtab_ref)
    edges = [int(e) for e in bucket_edges()]
    buckets = []
    for n in range(2):
        distance = tile_distance(n * ROWS)
        count = jnp.zeros((ROWS, ROWS), jnp.int32)
        for edge in edges:
            count = count + (distance >= edge).astype(jnp.int32)
        buckets.append(count)
    for b in range(BUCKETS):
        picks = [buckets[n] == b for n in range(2)]
        for h in range(heads):
            line = jnp.sum(
                jnp.where(picks[0], near[0][h], 0.0) + jnp.where(picks[1], near[1][h], 0.0),
                axis=0,
                keepdims=True,
            )
            if b == BUCKETS - 1:
                line = line + far[h]
            gtab_ref[h * BUCKETS + b : h * BUCKETS + b + 1, :] = line
    gain = jnp.zeros((1, width), F32)
    for slot in range(blocks):
        rows = slot_rows(slot, me)
        x = xs_ref[rows, :width].astype(F32)
        factor = lax.rsqrt(jnp.mean(x * x, axis=-1, keepdims=True) + 1e-06)
        part = mm_t(proj_ref[rows, :], wq_ref[...])
        if slot < 2:
            keep_ref[slot * ROWS : (slot + 1) * ROWS, :] = part
        else:
            send_ref[(slot - 2) * ROWS : (slot - 1) * ROWS, :] = part.astype(BF16)
        gain = gain + jnp.sum(part * (x * factor), axis=0, keepdims=True)
    wide = 3 * third
    table = jnp.sum(gtab_ref[...].T, axis=0, keepdims=True)
    small_ref[...] = jnp.zeros_like(small_ref)
    for n, value in enumerate((gain, gain_two_ref[...])):
        for m, piece in enumerate(halves(value)):
            small_ref[4 * n + 2 * m : 4 * n + 2 * m + 1, :] = piece[:, :wide]
            small_ref[4 * n + 2 * m + 1 : 4 * n + 2 * m + 2, : width - wide] = piece[:, wide:]
    for m, piece in enumerate(halves(table)):
        small_ref[2 * m + 1 : 2 * m + 2, TAB_AT : TAB_AT + EXT] = piece
    small = small_ref[...].astype(BF16)
    grad = t_mm(n1_ref[...], proj_ref[...])
    att = 0.0
    for slot, b_ref in enumerate((b0_ref, b1_ref, b2_ref, b3_ref)):
        att = att + t_mm(mixed_ref[slot_rows(slot, me), :], b_ref[...])
    groups, rows = grad_ref.shape[0], grad_ref.shape[1]
    shard = third // groups
    main = width // groups
    for n in range(groups):
        grad_ref[n, :main, :] = grad[n * main : (n + 1) * main, :]
        piece = att[n * shard : (n + 1) * shard, :]
        grad_ref[n, main : main + shard, :] = piece[:, :wide]
        for m in range(3):
            grad_ref[n, main + shard :, m * third : (m + 1) * third] = piece[
                m * 8 : (m + 1) * 8, wide:
            ]
    own = jnp.bitwise_and(place_ref[0], 1)
    for z in range(groups // 2):
        wkeep_ref[z * rows : (z + 1) * rows, :] = grad_ref[2 * z + own]
        wsend_ref[z * rows : (z + 1) * rows, :] = grad_ref[2 * z + 1 - own].astype(BF16)
    wkeep_ref[groups // 2 * rows :, :] = small.astype(F32)
    wsend_ref[groups // 2 * rows :, :] = small


def halves(value):
    high = value.astype(BF16).astype(F32)
    return high, value - high


def split_small(rows):
    pieces = []
    for n in range(2):
        pieces += halves(rows[4 * n : 4 * n + 2] + rows[4 * n + 2 : 4 * n + 4])
    return jnp.concatenate(pieces, axis=0).astype(BF16)


def fold_y_kernel(place_ref, keep_ref, got_ref, own_ref, *refs):
    sends, block_ref = refs[:-1], refs[-1]
    count, rows = block_ref.shape[0], block_ref.shape[1]
    total = keep_ref[...] + got_ref[...].astype(F32)
    for z in range(count):
        block_ref[z] = total[z * rows : (z + 1) * rows, :]
    small = split_small(total[count * rows :, :])
    me = jnp.right_shift(place_ref[0], 1)
    own_ref[:rows, :] = block_ref[me]
    own_ref[rows:, :] = small.astype(F32)
    for k, send_ref in enumerate(sends):
        send_ref[:rows, :] = block_ref[jnp.bitwise_xor(me, k + 1)].astype(BF16)
        send_ref[rows:, :] = small


def fold_z_kernel(me_ref, own_ref, *refs):
    gots, att_ref, keep_ref, sends, block_ref = refs[:3], refs[3], refs[4], refs[5:-1], refs[-1]
    count, shard, wide = block_ref.shape
    third = wide // 3
    total = (own_ref[...] + gots[0][...].astype(F32)) + (
        gots[1][...].astype(F32) + gots[2][...].astype(F32)
    )
    for s in range(count):
        block_ref[s] = total[s * shard : (s + 1) * shard, :]
    main = count * shard
    att_ref[:, :wide] = total[main : main + shard, :].astype(BF16)
    rest = total[main + shard : main + shard + 8, :]
    att_ref[:, wide:] = jnp.concatenate(
        [rest[:, m * third : (m + 1) * third] for m in range(3)], axis=0
    ).astype(BF16)
    small = split_small(total[main + shard + 8 :, :])
    keep_ref[:shard, :] = block_ref[me_ref[0]]
    keep_ref[shard:, :] = small.astype(F32)
    for k, send_ref in enumerate(sends):
        send_ref[:shard, :] = block_ref[jnp.bitwise_xor(me_ref[0], SLOTS[k + 1])].astype(BF16)
        send_ref[shard:, :] = small


def fold_seq_kernel(me_ref, *refs):
    pieces, gwq_ref, one_ref, two_ref, tab_ref, block_ref, table_ref = (
        refs[:4],
        *refs[4:],
    )
    parts, shard = block_ref.shape[0], block_ref.shape[1]
    wide = block_ref.shape[2]
    width = one_ref.shape[1]
    third = wide // 3
    values = [piece[...].astype(F32) for piece in pieces]
    for slot, value in enumerate(values):
        s = jnp.bitwise_xor(me_ref[0], SLOTS[slot])
        block_ref[s] = value[:shard]
        table_ref[s] = jnp.broadcast_to(
            (value[shard + 1 : shard + 2] + value[shard + 3 : shard + 4])[
                :, TAB_AT : TAB_AT + EXT
            ],
            (8, EXT),
        )
    for s in range(parts):
        for n in range(3):
            at = n * width + s * third
            gwq_ref[:, at : at + third] = block_ref[s, :, n * third : (n + 1) * third]
        tab_ref[s : s + 1, :] = table_ref[s, 0:1, :]
    small = (values[0][shard:] + values[1][shard:]) + (values[2][shard:] + values[3][shard:])
    for n, out_ref in enumerate((one_ref, two_ref)):
        out_ref[:, :wide] = small[4 * n : 4 * n + 1] + small[4 * n + 2 : 4 * n + 3]
        rest = small[4 * n + 1 : 4 * n + 2] + small[4 * n + 3 : 4 * n + 4]
        out_ref[:, wide:] = rest[:, : width - wide]


def qkv_send_kernel(w_ref, send_ref):
    count, shard, wide = send_ref.shape
    third = wide // 3
    width = w_ref.shape[1] // 3
    parts = width // third
    for p in range(parts):
        for n in range(3):
            at = n * width + p * third
            piece = w_ref[:, at : at + third]
            for i in range(p, count, parts):
                send_ref[i, :, n * third : (n + 1) * third] = piece


def in_send_kernel(w_ref, send_ref):
    devices, shard, wide = send_ref.shape
    experts = w_ref.shape[0]
    own = wide // experts
    for i in range(devices):
        for e in range(experts):
            send_ref[i, :, e * own : (e + 1) * own] = w_ref[e, :, i * own : (i + 1) * own]


def in_last_kernel(got_ref, grad_ref):
    devices, shard, wide = got_ref.shape
    experts = grad_ref.shape[0]
    own = wide // experts
    for i in range(devices):
        for e in range(experts):
            grad_ref[e, :, i * own : (i + 1) * own] = got_ref[
                i, :, e * own : (e + 1) * own
            ].astype(F32)


def expert_kernel(
    step,
    place_ref,
    xa_ref,
    xb_ref,
    g_all_ref,
    w1a_ref,
    w1b_ref,
    w2a_ref,
    w2b_ref,
    pick_ref,
    act_home,
    pre_home,
    keep_ref,
    send_ref,
    x_ref,
    g_ref,
    dx_ref,
    act_ref,
    pre_ref,
    sem_ref,
):
    rows, width = xa_ref.shape
    half = w1a_ref.shape[1]
    tile_cols = 256
    root = math.sqrt(2.0 / math.pi)
    own, far = g_rows(step, place_ref[0])
    fetch = copies(
        [
            (g_all_ref.at[own], g_ref.at[pl.ds(0, rows)]),
            (g_all_ref.at[far], g_ref.at[pl.ds(rows, rows)]),
        ],
        sem_ref,
    )
    for copy in fetch:
        copy.start()
    x_ref[:rows, :] = xa_ref[...]
    x_ref[rows:, :] = xb_ref[...]
    dx_ref[...] = jnp.zeros_like(dx_ref)
    for copy in fetch:
        copy.wait()

    def tile(t, carry):
        cols = pl.ds(pl.multiple_of(t * tile_cols, tile_cols), tile_cols)
        for side, (w1_ref, w2_ref) in enumerate(((w1a_ref, w2a_ref), (w1b_ref, w2b_ref))):
            out_cols = pl.ds(pl.multiple_of(side * half + t * tile_cols, tile_cols), tile_cols)
            choose = mm(g_ref[:, width:], pick_ref[:, cols])
            v = mm(x_ref[...], w1_ref[:, cols])
            square = v * v
            curve = jnp.tanh(root * v * (1.0 + 0.044715 * square))
            part = 0.5 * (1.0 + curve)
            slope = part + 0.5 * v * (1.0 - curve * curve) * (
                root * (1.0 + 3 * 0.044715 * square)
            )
            act_ref[:, out_cols] = (choose * (v * part)).astype(BF16)
            grad_act = mm_t(g_ref[:, :width], w2_ref[cols, :])
            grad_pre = (choose * grad_act * slope).astype(BF16)
            pre_ref[:, out_cols] = grad_pre
            dx_ref[...] += mm_t(grad_pre, w1_ref[:, cols])
        return carry

    lax.fori_loop(0, half // tile_cols, tile, 0)
    home = copies([(act_ref, act_home), (pre_ref, pre_home)], sem_ref)
    for copy in home:
        copy.start()
    keep_ref[...] = dx_ref[:rows, :]
    send_ref[...] = dx_ref[rows:, :].astype(BF16)
    for copy in home:
        copy.wait()


def g_rows(step, place):
    own = jnp.bitwise_xor(place, 2 * step)
    return own, jnp.bitwise_xor(own, 1)


def expert_out_kernel(count, place_ref, w2a_ref, w2b_ref, *refs):
    acts, keep_ref, send_ref, act_ref, sem_ref = refs[:count], *refs[count:]
    rows = keep_ref.shape[1]
    half = w2a_ref.shape[0]
    fetch = copies([(act, act_ref.at[k]) for k, act in enumerate(acts)], sem_ref)
    for copy in fetch:
        copy.start()
    for k in range(count):
        fetch[k].wait()
        out = mm(act_ref[k, :, :half], w2a_ref[...]) + mm(act_ref[k, :, half:], w2b_ref[...])
        keep_ref[k] = out[:rows]
        send_ref[k] = out[rows:].astype(BF16)


def in_grad_kernel(count, *refs):
    xs, pres = refs[: 2 * count], refs[2 * count : 3 * count]
    own_ref, far_ref, xt_ref, pre_ref, sem_ref = refs[3 * count :]
    rows = xs[0].shape[0]
    half = own_ref.shape[1]
    step = 256
    fetch = copies(
        [(p, pre_ref.at[pl.ds(k * 2 * rows, 2 * rows)]) for k, p in enumerate(pres)], sem_ref
    )
    for copy in fetch:
        copy.start()
    for k in range(2 * count):
        xt_ref[:, k * rows : (k + 1) * rows] = xs[k][...].T
    for copy in fetch:
        copy.wait()

    def tile(t, carry):
        cols = pl.ds(pl.multiple_of(t * step, step), step)
        cols_far = pl.ds(pl.multiple_of(half + t * step, step), step)
        far_ref[:, cols] = mm(xt_ref[...], pre_ref[:, cols_far]).astype(BF16)
        own_ref[:, cols] = mm(xt_ref[...], pre_ref[:, cols])
        return carry

    lax.fori_loop(0, half // step, tile, 0)


def out_grad_kernel(count, place_ref, g_all_ref, *refs):
    acts = refs[:count]
    own_ref, far_ref, g_ref, act_ref, sem_ref = refs[count:]
    rows = g_all_ref.shape[1]
    half, width = own_ref.shape
    step = 256
    pairs = [(a, act_ref.at[pl.ds(k * 2 * rows, 2 * rows)]) for k, a in enumerate(acts)]
    for k in range(count):
        for m, place in enumerate(g_rows(k, place_ref[0])):
            pairs.append((g_all_ref.at[place], g_ref.at[pl.ds((2 * k + m) * rows, rows)]))
    fetch = copies(pairs, sem_ref)
    for copy in fetch:
        copy.start()
    for copy in fetch:
        copy.wait()

    def tile(t, carry):
        cols = pl.ds(pl.multiple_of(t * step, step), step)
        cols_far = pl.ds(pl.multiple_of(half + t * step, step), step)
        far_ref[cols, :] = t_mm(act_ref[:, cols_far], g_ref[:, :width]).astype(BF16)
        own_ref[cols, :] = t_mm(act_ref[:, cols], g_ref[:, :width])
        return carry

    lax.fori_loop(0, half // step, tile, 0)


def call(kernel, outs, args, us, scratch=(), scalars=0, far=(), home=(), mib=60):
    smem = pl.BlockSpec(memory_space=pltpu.SMEM)
    vmem = pl.BlockSpec(memory_space=pltpu.VMEM)
    hbm = pl.BlockSpec(memory_space=pltpu.HBM)
    return pl.pallas_call(
        kernel,
        out_shape=[jax.ShapeDtypeStruct(shape, dtype) for shape, dtype in outs],
        in_specs=[smem] * scalars
        + [hbm if n in far else vmem for n in range(scalars, len(args))],
        out_specs=[hbm if n in home else vmem for n in range(len(outs))],
        scratch_shapes=list(scratch),
        compiler_params=pltpu.CompilerParams(vmem_limit_bytes=mib * MIB),
        cost_estimate=pl.CostEstimate(
            flops=0, bytes_accessed=int(us * BYTES_US), transcendentals=0
        ),
    )(*args)


def head_body(
    tokens,
    cotangent,
    segment_ids,
    pad_mask,
    routes,
    gate_weights,
    gain_one,
    w_qkv,
    w_attn,
    rel_table,
    gain_two,
    w_expert_in,
    w_expert_out,
):
    x_low = tokens[0]
    g_low = cotangent[0]
    rows, width = x_low.shape
    size_z, size_y, size_x, size_c = (lax.axis_size(a) for a in AXES)
    parts = size_x * size_c
    devices = size_z * size_y * parts
    me = lax.axis_index(("x", "c"))
    head_count = rel_table.shape[0]
    heads = head_count // parts
    third = width // parts
    length = rows * parts
    experts, shard, ff = w_expert_in.shape
    ff_own = ff // devices
    me_arr = me.astype(jnp.int32).reshape(1)

    seg = segment_ids[0]
    info = jnp.where(pad_mask[0] == 1, seg, -1)
    marks = jnp.stack([seg, info], axis=1).astype(BF16)
    x_ext = jnp.concatenate([x_low, jnp.pad(marks, ((0, 0), (0, EXT - 2)))], axis=1)
    x_slots = gather_seq(x_ext)

    groups = devices // parts
    across = [(i, i ^ 3) for i in range(parts)]
    to_part = [((i % groups) * parts + i // groups) for i in range(devices)]
    q_send = call(
        qkv_send_kernel,
        [((devices // 2, shard, 3 * third), BF16)],
        [w_qkv],
        us=1,
        mib=8,
    )[0]
    q_own = lax.all_to_all(q_send, ("z", "x", "c"), 0, 0, tiled=True)

    att_one = lax.ppermute(w_attn, AXES, [(i, to_part[i]) for i in range(devices)])
    z_index = lax.axis_index("z")
    y_index = lax.axis_index("y")
    att_z = jnp.zeros((size_z, shard, width), BF16)
    for k in range(size_z):
        piece = att_one if k == 0 else swap(att_one, "z", k)
        att_z = lax.dynamic_update_slice_in_dim(
            att_z, piece[None], jnp.bitwise_xor(z_index, k), 0
        )
    att_y = swap(att_z, "y")
    watt = jnp.where(
        y_index == 0, jnp.stack([att_z, att_y], axis=1), jnp.stack([att_y, att_z], axis=1)
    ).reshape(third, width)

    w2_own = w_expert_out.reshape(experts * ff_own, width)
    w2a = jnp.concatenate([w2_own, swap(w2_own, "x")], axis=0)
    w2b = swap(w2a, "c")
    q_own = after(q_own, watt, x_slots, w2a)
    q_far = swap(q_own, "y")

    in_send = call(
        in_send_kernel,
        [((devices, shard, experts * ff_own), BF16)],
        [w_expert_in],
        us=1.2,
        mib=16,
    )[0]
    in_send = after(in_send, q_own)
    w1_own = lax.all_to_all(in_send, AXES, 0, 0, tiled=True).reshape(width, experts * ff_own)

    w1_x = swap(w1_own, "x")

    expert_ids = jnp.arange(experts, dtype=jnp.int32)
    choose = jnp.sum(
        gate_weights[0][:, :, None] * (routes[0][:, :, None] == expert_ids).astype(F32), axis=1
    )
    choose_hi = choose.astype(BF16)
    choose_lo = (choose - choose_hi.astype(F32)).astype(BF16)
    g_ext = jnp.concatenate(
        [g_low, choose_hi, choose_lo, jnp.zeros((rows, EXT - 2 * experts), BF16)], axis=1
    )
    g_all = lax.all_gather(g_ext, ("z", "y"), axis=0)
    place_arr = lax.axis_index(("z", "y")).astype(jnp.int32).reshape(1)

    table = lax.dynamic_slice_in_dim(rel_table, me * heads, heads, 0).astype(F32)
    half = length // 2
    kept = [
        ((length, width + EXT), BF16),
        ((length, width), BF16),
        ((width, 3 * third), BF16),
        ((length, 3 * third), BF16),
        ((length, EXT), F32),
    ]
    kept_scratch = [pltpu.VMEM(shape, dtype) for shape, dtype in kept]
    mixed, *saved = call(
        attend_kernel,
        [((length, third), BF16), *kept],
        [me_arr, place_arr, table, *x_slots, gain_one.reshape(1, width), q_own, q_far],
        scratch=[
            *kept_scratch,
            pltpu.VMEM((devices, shard, 3 * third), BF16),
            pltpu.VMEM((2 * heads, ROWS, ROWS), F32),
            pltpu.SemaphoreType.DMA((5,)),
        ],
        scalars=3,
        home=range(1, 6),
        us=8,
        mib=60,
    )
    saved = [*saved, mixed]
    keep, send = call(
        project_kernel,
        [((half, width), F32), ((half, width), BF16)],
        [me_arr, mixed, watt],
        scalars=1,
        us=1,
        mib=16,
    )
    inputs = x_low.astype(F32)
    hidden_one = inputs + reduce_seq(keep, send)
    scaled_two, factor_two = norm_stats(hidden_one)
    normed_two = (scaled_two * gain_two).astype(BF16)

    w1a = jnp.concatenate([after(w1_own, normed_two), w1_x], axis=1)
    w1b = swap(w1a, "c")
    ff_two = parts * experts * ff_own
    pick_np = np.zeros((EXT, ff_two // 2), np.float32)
    for col in range(ff_two // 2):
        e = col // ff_own % experts
        pick_np[[e, experts + e], col] = 1.0
    pick = jnp.asarray(pick_np, BF16)
    pair = 2 * rows
    x_own = [normed_two] + [swap(normed_two, "z", k) for k in range(1, size_z)]
    x_far = [swap(x, "y") for x in x_own]
    acts, pres, keeps, gots, backs = [], [], [], [], []
    for k in range(size_z):
        x_here = x_own[k] if k < 2 else after(x_own[k], backs[k - 2])
        act, pre, dx_keep, dx_send = call(
            functools.partial(expert_kernel, k),
            [
                ((pair, ff_two), BF16),
                ((pair, ff_two), BF16),
                ((rows, width), F32),
                ((rows, width), BF16),
            ],
            [place_arr, x_here, x_far[k], g_all, w1a, w1b, w2a, w2b, pick],
            scratch=[
                pltpu.VMEM((pair, width), BF16),
                pltpu.VMEM((pair, width + EXT), BF16),
                pltpu.VMEM((pair, width), F32),
                pltpu.VMEM((pair, ff_two), BF16),
                pltpu.VMEM((pair, ff_two), BF16),
                pltpu.SemaphoreType.DMA((2,)),
            ],
            far=(3,),
            home=(0, 1),
            mib=20,
            scalars=1,
        us=5.5,
        )
        acts.append(act)
        pres.append(pre)
        keeps.append(dx_keep)
        gots.append(swap(dx_send, "y"))
        if k + 1 < size_z:
            backs.append(dx_keep + gots[k].astype(F32))

    ff_half = ff_two // 2
    backs.append(keeps[-1] + gots[-1].astype(F32))
    in_own, in_far = call(
        functools.partial(in_grad_kernel, size_z),
        [((width, ff_half), F32), ((width, ff_half), BF16)],
        [*[x for both in zip(x_own, x_far) for x in both], *pres[:-1], after(pres[-1], *backs)],
        scratch=[
            pltpu.VMEM((width, size_z * pair), BF16),
            pltpu.VMEM((size_z * pair, ff_two), BF16),
            pltpu.SemaphoreType.DMA((size_z,)),
        ],
        far=range(2 * size_z, 3 * size_z),
        us=6,
        mib=24,
    )
    out_keep, out_send = call(
        functools.partial(expert_out_kernel, size_z),
        [((size_z, rows, width), F32), ((size_z, rows, width), BF16)],
        [place_arr, w2a, w2b, after(acts[0], in_far), *acts[1:]],
        scratch=[
            pltpu.VMEM((size_z, pair, ff_two), BF16),
            pltpu.SemaphoreType.DMA((size_z,)),
        ],
        scalars=1,
        far=range(3, 3 + size_z),
        us=4.4,
        mib=24,
    )
    grad_normed_two = after(backs[0], out_send)
    for k in range(1, size_z):
        grad_normed_two = grad_normed_two + swap(backs[k].astype(BF16), "z", k).astype(F32)

    grad_hidden_norm, gain_two_part = norm_back(grad_normed_two, scaled_two, factor_two, gain_two)
    grad_hidden = g_low.astype(F32) + grad_hidden_norm
    branch_low = grad_hidden.astype(BF16)
    branch = gather_seq(branch_low)

    quarter = ff_half // 2
    in_c = after(in_own, out_send) + swap(in_far, "c").astype(F32)
    in_x_got = swap(in_c[:, quarter:].astype(BF16), "x")
    out_y = out_keep + swap(out_send, "y").astype(F32)
    extra = 8
    wide = 3 * third
    rows_y = parts * shard + shard * width // wide
    w_keep, w_send, gno_keep, gno_send = call(
        attend_back_kernel,
        [
            ((size_z * rows_y + extra, wide), F32),
            ((size_z * rows_y + extra, wide), BF16),
            ((half, width), F32),
            ((half, width), BF16),
        ],
        [
            me_arr,
            place_arr,
            table,
            *branch,
            watt,
            after(gain_two_part.reshape(1, width), out_y, in_c),
            *saved,
        ],
        scratch=[
            *kept_scratch,
            pltpu.VMEM((length, third), BF16),
            pltpu.VMEM((2 * heads, ROWS, ROWS), F32),
            pltpu.VMEM((length, third), BF16),
            pltpu.VMEM((length, third), F32),
            pltpu.VMEM((length, third), F32),
            pltpu.VMEM((length, wide), BF16),
            pltpu.VMEM((EXT, ROWS), F32),
            pltpu.VMEM((extra, wide), F32),
            pltpu.VMEM((groups, rows_y, wide), F32),
            pltpu.SemaphoreType.DMA((6,)),
        ],
        scalars=3,
        far=range(9, 15),
        us=10,
        mib=60,
    )
    in_x = after(in_c[:, :quarter], gno_send) + in_x_got.astype(F32)
    in_x_low = in_x.astype(BF16).reshape(devices, shard, quarter)
    in_got = lax.all_to_all(in_x_low, AXES, 0, 0, tiled=True)
    combined = after(out_y[0], gno_send)
    for k in range(1, size_z):
        combined = combined + swap(out_y[k].astype(BF16), "z", k).astype(F32)
    output = (hidden_one + combined).astype(BF16)
    first_act = after(acts[0], gno_send)
    out_own, out_far = call(
        functools.partial(out_grad_kernel, size_z),
        [((ff_half, width), F32), ((ff_half, width), BF16)],
        [place_arr, g_all, first_act, *acts[1:]],
        scratch=[
            pltpu.VMEM((size_z * pair, width + EXT), BF16),
            pltpu.VMEM((size_z * pair, ff_two), BF16),
            pltpu.SemaphoreType.DMA((3 * size_z,)),
        ],
        far=range(1, 2 + size_z),
        scalars=1,
        us=6.5,
        mib=24,
    )
    z_keep, *z_sends = call(
        fold_y_kernel,
        [((rows_y + extra, wide), F32)] + [((rows_y + extra, wide), BF16)] * (size_z - 1),
        [place_arr, after(w_keep, out_far), swap(after(w_send, in_x_low, combined), "y")],
        scratch=[pltpu.VMEM((size_z, rows_y, wide), F32)],
        scalars=1,
        mib=12,
        us=1,
    )
    out_c = after(out_own, z_keep) + swap(out_far, "c").astype(F32)
    out_x_got = swap(out_c[quarter:].astype(BF16), "x")
    att_share, s_keep, *s_sends = call(
        fold_z_kernel,
        [((shard, width), BF16), ((shard + extra, wide), F32)]
        + [((shard + extra, wide), BF16)] * (parts - 1),
        [me_arr, after(z_keep, in_got), *[swap(piece, "z", k + 1) for k, piece in enumerate(z_sends)]],
        scratch=[pltpu.VMEM((parts, shard, wide), F32)],
        scalars=1,
        mib=12,
        us=1,
    )
    grad_w_qkv, one_sum, two_sum, table_sum = call(
        fold_seq_kernel,
        [
            ((shard, 3 * width), F32),
            ((1, width), F32),
            ((1, width), F32),
            ((parts, EXT), F32),
        ],
        [
            me_arr,
            s_keep,
            swap(s_sends[0], "x"),
            swap(s_sends[1], "c"),
            lax.ppermute(s_sends[2], ("x", "c"), across),
        ],
        scratch=[
            pltpu.VMEM((parts, shard, wide), F32),
            pltpu.VMEM((parts, 8, EXT), F32),
        ],
        scalars=1,
        mib=12,
        us=1,
    )

    grad_normed_one = reduce_seq(after(gno_keep, z_keep), after(gno_send, z_keep))
    scaled_one, factor_one = norm_stats(inputs)
    grad_input_norm, unused_gain = norm_back(grad_normed_one, scaled_one, factor_one, gain_one)
    grad_inputs = grad_hidden + grad_input_norm

    grad_w_in = call(
        in_last_kernel, [((experts, shard, ff), F32)], [in_got], us=1.3, mib=16
    )[0]
    grad_w_out = (out_c[:quarter] + out_x_got.astype(F32)).reshape(experts, ff_own, width)

    grad_w_attn = lax.ppermute(
        att_share, AXES, [(to_part[i], i) for i in range(devices)]
    ).astype(F32)
    return (
        output[None],
        grad_inputs[None],
        one_sum[0],
        grad_w_qkv,
        grad_w_attn,
        table_sum[:, : heads * BUCKETS].reshape(head_count, BUCKETS),
        two_sum[0],
        grad_w_in,
        grad_w_out,
    )


def heads_fit(mesh):
    return mesh.shape["seq"] == 4 and mesh.shape["dp"] == 8


def solution(mesh):
    if not heads_fit(mesh):
        return rows_solution(mesh)
    grid = Mesh(mesh.devices.reshape(mesh.shape["dp"] // 2, 2, mesh.shape["seq"] // 2, 2), AXES)
    by_token = P(("z", "y"), ("x", "c"))
    by_row = P(AXES, None)
    by_second = P(None, AXES, None)
    return jax.shard_map(
        head_body,
        mesh=grid,
        in_specs=(
            by_token,
            by_token,
            by_token,
            by_token,
            by_token,
            by_token,
            P(),
            by_row,
            by_row,
            P(),
            P(),
            by_second,
            by_second,
        ),
        out_specs=(
            by_token,
            by_token,
            P(),
            by_row,
            by_row,
            P(),
            P(),
            by_second,
            by_second,
        ),
        check_vma=False,
    )
```

```python
import functools
import math

import jax
import jax.numpy as jnp
import numpy as np
from jax import lax
from jax.experimental import pallas as pl
from jax.experimental.pallas import tpu as pltpu
from jax.sharding import Mesh
from jax.sharding import PartitionSpec as P

BUCKETS = 32
MAX_DIST = 128
CAP = 96


def bucket_edges():
    exact_span = BUCKETS // 2
    distance = np.arange(1, 8 * MAX_DIST + 1)
    widened = np.maximum(distance, exact_span) / exact_span
    spread = exact_span + (np.log(widened) / np.log(MAX_DIST / exact_span) * exact_span).astype(
        np.int64
    )
    bucket_of = np.where(distance < exact_span, distance, np.minimum(spread, BUCKETS - 1))
    return np.array(
        [distance[np.argmax(bucket_of >= target)] for target in range(1, BUCKETS)], dtype=np.int32
    )


def norm_stats(values):
    factor = lax.rsqrt(jnp.mean(values * values, axis=-1, keepdims=True) + 1e-06)
    return (values * factor, factor)


def norm_back(grad_normed, scaled, factor, gain_vec):
    grad_scaled = grad_normed * gain_vec
    inner_mean = jnp.mean(grad_scaled * scaled, axis=-1, keepdims=True)
    return (factor * (grad_scaled - scaled * inner_mean), jnp.sum(grad_normed * scaled, axis=0))


def make_onehot(distance, edges_np):
    bucket_of = jnp.sum((distance[:, :, None] >= edges_np).astype(jnp.int32), axis=-1)
    return (bucket_of[:, :, None] == jnp.arange(BUCKETS, dtype=jnp.int32)).astype(jnp.bfloat16)


def block_bias(table_low, edges_np, distance):
    far_away = jnp.min(distance) >= int(edges_np[-1])

    def block_detailed(unused):
        return jnp.einsum(
            "qkb,hb->hqk",
            make_onehot(distance, edges_np),
            table_low,
            preferred_element_type=jnp.float32,
        )

    def block_constant(unused):
        last_col = table_low[:, BUCKETS - 1].astype(jnp.float32)
        return jnp.broadcast_to(last_col[:, None, None], (table_low.shape[0],) + distance.shape)

    return lax.cond(far_away, block_constant, block_detailed, 0)


def table_part(grad_low, edges_np, distance):
    far_away = jnp.min(distance) >= int(edges_np[-1])

    def table_detailed(unused):
        return jnp.einsum(
            "hqk,qkb->hb",
            grad_low,
            make_onehot(distance, edges_np),
            preferred_element_type=jnp.float32,
        )

    def table_constant(unused):
        totals = jnp.sum(grad_low, axis=(1, 2), dtype=jnp.float32)
        return totals[:, None] * (jnp.arange(BUCKETS) == BUCKETS - 1).astype(jnp.float32)

    return lax.cond(far_away, table_constant, table_detailed, 0)


def body(
    tokens,
    cotangent,
    segment_ids,
    pad_mask,
    routes,
    gate_weights,
    gain_one,
    w_qkv,
    w_attn,
    rel_table,
    gain_two,
    w_expert_in,
    w_expert_out,
):
    gathered = (
        lax.all_gather(w_qkv, ("dp", "seq"), axis=0, tiled=True),
        lax.all_gather(w_attn, ("dp", "seq"), axis=0, tiled=True),
        lax.all_gather(w_expert_in, ("dp", "seq"), axis=1, tiled=True),
        lax.all_gather(w_expert_out, ("dp", "seq"), axis=1, tiled=True),
    )
    full_qkv, full_attn, full_in, full_out = gathered
    inputs = tokens[0].astype(jnp.float32)
    row_count, model_width = inputs.shape
    head_count = rel_table.shape[0]
    head_size = model_width // head_count
    score_scale = head_size ** (-0.5)
    seg_local = segment_ids[0]
    seq_index = lax.axis_index("seq")
    length = row_count * lax.axis_size("seq")
    key_block = math.gcd(length, 512)
    query_pos = seq_index * row_count + jnp.arange(row_count, dtype=jnp.int32)
    block_count = ((seq_index + 1) * row_count + key_block - 1) // key_block
    edges_np = bucket_edges()
    scaled_one, factor_one = norm_stats(inputs)
    normed_one = (scaled_one * gain_one).astype(jnp.bfloat16)
    project = jnp.dot(normed_one, full_qkv, preferred_element_type=jnp.float32)
    queries = project[:, :model_width].astype(jnp.bfloat16)
    keys_local = project[:, model_width : 2 * model_width].astype(jnp.bfloat16)
    values_local = project[:, 2 * model_width :].astype(jnp.bfloat16)
    info_local = jnp.where(pad_mask[0] == 1, seg_local, -1)
    keys_all, values_all, info_all, seg_all = (
        lax.all_gather(keys_local, "seq", axis=0, tiled=True),
        lax.all_gather(values_local, "seq", axis=0, tiled=True),
        lax.all_gather(info_local, "seq", axis=0, tiled=True),
        lax.all_gather(seg_local, "seq", axis=0, tiled=True),
    )
    query_heads = queries.reshape(row_count, head_count, head_size)

    def block_scores(block_index):
        key_start = block_index * key_block
        key_heads = lax.dynamic_slice_in_dim(keys_all, key_start, key_block, 0).reshape(
            key_block, head_count, head_size
        )
        value_heads = lax.dynamic_slice_in_dim(values_all, key_start, key_block, 0).reshape(
            key_block, head_count, head_size
        )
        info_block = lax.dynamic_slice_in_dim(info_all, key_start, key_block, 0)
        key_pos = key_start + jnp.arange(key_block, dtype=jnp.int32)
        distance = query_pos[:, None] - key_pos[None, :]
        allowed = (distance >= 0) & ((info_block[None, :] == seg_local[:, None]) | (distance == 0))
        raw_scores = (
            jnp.einsum("qhd,khd->hqk", query_heads, key_heads, preferred_element_type=jnp.float32)
            * score_scale
        )
        raw_scores = raw_scores + block_bias(rel_table, edges_np, distance)
        return (
            jnp.where(allowed[None], raw_scores, -1e30),
            allowed[None],
            key_heads,
            value_heads,
            distance,
            key_start,
        )

    def max_step(block_index, running):
        top_score, row_total = running
        pieces = block_scores(block_index)
        new_top = jnp.maximum(top_score, jnp.max(pieces[0], axis=-1))
        exponent = jnp.where(pieces[1], jnp.exp(pieces[0] - new_top[:, :, None]), 0.0)
        return (new_top, row_total * jnp.exp(top_score - new_top) + jnp.sum(exponent, axis=-1))

    start_top = jnp.full((head_count, row_count), -1e30, jnp.float32)
    start_total = jnp.zeros((head_count, row_count), jnp.float32)
    top_score, row_total = lax.fori_loop(0, block_count, max_step, (start_top, start_total))
    log_total = top_score + jnp.log(row_total)

    def out_step(block_index, mixed_acc):
        pieces = block_scores(block_index)
        prob_low = jnp.where(pieces[1], jnp.exp(pieces[0] - log_total[:, :, None]), 0.0).astype(
            jnp.bfloat16
        )
        return mixed_acc + jnp.einsum(
            "hqk,khd->qhd", prob_low, pieces[3], preferred_element_type=jnp.float32
        )

    mixed_full = lax.fori_loop(
        0, block_count, out_step, jnp.zeros((row_count, head_count, head_size), jnp.float32)
    )
    mixed_low = mixed_full.reshape(row_count, model_width).astype(jnp.bfloat16)
    hidden_one = inputs + jnp.dot(mixed_low, full_attn, preferred_element_type=jnp.float32)
    scaled_two, factor_two = norm_stats(hidden_one)
    normed_two = (scaled_two * gain_two).astype(jnp.bfloat16)
    route_local = routes[0]
    expert_count = w_expert_in.shape[0]
    top_count = route_local.shape[1]
    flat_routes = route_local.reshape(-1)
    expert_hot = (flat_routes[:, None] == jnp.arange(expert_count, dtype=jnp.int32)).astype(
        jnp.int32
    )
    earlier = jnp.cumsum(expert_hot, axis=0) - expert_hot
    slot_index = jnp.sum(earlier * expert_hot, axis=1)
    slot_float = (
        (slot_index[:, None] == jnp.arange(CAP, dtype=jnp.int32))
        .astype(jnp.float32)
        .reshape(row_count, top_count, CAP)
    )
    expert_float = expert_hot.astype(jnp.float32).reshape(row_count, top_count, expert_count)
    dispatch = jnp.einsum(
        "tke,tkc->ect",
        expert_float.astype(jnp.bfloat16),
        slot_float.astype(jnp.bfloat16),
        preferred_element_type=jnp.float32,
    ).astype(jnp.bfloat16)
    slot_gate = jnp.einsum(
        "tke,tkc,tk->ec", expert_float, slot_float, gate_weights[0], precision=lax.Precision.HIGHEST
    )
    entered = jnp.einsum(
        "ect,td->ecd", dispatch, normed_two, preferred_element_type=jnp.float32
    ).astype(jnp.bfloat16)
    pre_act = jnp.einsum("ecd,edf->ecf", entered, full_in, preferred_element_type=jnp.float32)
    active = jax.nn.gelu(pre_act).astype(jnp.bfloat16)
    result = jnp.einsum("ecf,efd->ecd", active, full_out, preferred_element_type=jnp.float32)
    expert_low = (slot_gate[:, :, None] * result).astype(jnp.bfloat16)
    combined = jnp.einsum("ect,ecd->td", dispatch, expert_low, preferred_element_type=jnp.float32)
    output = (hidden_one + combined).astype(jnp.bfloat16)
    regathered = (
        lax.all_gather(w_qkv, ("dp", "seq"), axis=0, tiled=True),
        lax.all_gather(w_attn, ("dp", "seq"), axis=0, tiled=True),
        lax.all_gather(w_expert_in, ("dp", "seq"), axis=1, tiled=True),
        lax.all_gather(w_expert_out, ("dp", "seq"), axis=1, tiled=True),
    )
    back_qkv, back_attn, back_in, back_out = regathered
    grad_out_low = cotangent[0]
    grad_slots = jnp.einsum(
        "ect,td->ecd", dispatch, grad_out_low, preferred_element_type=jnp.float32
    )
    grad_result = (slot_gate[:, :, None] * grad_slots).astype(jnp.bfloat16)
    grad_w_out = jnp.einsum("ecf,ecd->efd", active, grad_result, preferred_element_type=jnp.float32)
    grad_active = jnp.einsum(
        "ecd,efd->ecf", grad_result, back_out, preferred_element_type=jnp.float32
    )
    unused_value, gelu_pull = jax.vjp(jax.nn.gelu, pre_act)
    grad_pre = gelu_pull(grad_active)[0].astype(jnp.bfloat16)
    grad_w_in = jnp.einsum("ecd,ecf->edf", entered, grad_pre, preferred_element_type=jnp.float32)
    grad_entered = jnp.einsum(
        "ecf,edf->ecd", grad_pre, back_in, preferred_element_type=jnp.float32
    ).astype(jnp.bfloat16)
    grad_normed_two = jnp.einsum(
        "ect,ecd->td", dispatch, grad_entered, preferred_element_type=jnp.float32
    )
    grad_hidden_norm, grad_gain_two = norm_back(grad_normed_two, scaled_two, factor_two, gain_two)
    grad_hidden = grad_out_low.astype(jnp.float32) + grad_hidden_norm
    branch_low = grad_hidden.astype(jnp.bfloat16)
    grad_w_attn = lax.dot_general(
        mixed_low, branch_low, (((0,), (0,)), ((), ())), preferred_element_type=jnp.float32
    )
    grad_mixed = lax.dot_general(
        branch_low, back_attn, (((1,), (1,)), ((), ())), preferred_element_type=jnp.float32
    ).astype(jnp.bfloat16)
    grad_mixed_heads = grad_mixed.reshape(row_count, head_count, head_size)
    row_delta = jnp.sum(grad_mixed_heads.astype(jnp.float32) * mixed_full, axis=-1).T

    def score_grads(pieces):
        prob_full = jnp.where(pieces[1], jnp.exp(pieces[0] - log_total[:, :, None]), 0.0)
        grad_prob = jnp.einsum(
            "qhd,khd->hqk", grad_mixed_heads, pieces[3], preferred_element_type=jnp.float32
        )
        grad_score = (prob_full * (grad_prob - row_delta[:, :, None])).astype(jnp.bfloat16)
        return (prob_full.astype(jnp.bfloat16), grad_score)

    start_query = jnp.zeros((row_count, head_count, head_size), jnp.float32)
    start_table = jnp.zeros((head_count, BUCKETS), jnp.float32)

    def back_step(block_index, running):
        grad_query, grad_key_all, grad_value_all, grad_table = running
        pieces = block_scores(block_index)
        prob_low, grad_score = score_grads(pieces)
        grad_query = (
            grad_query
            + jnp.einsum("hqk,khd->qhd", grad_score, pieces[2], preferred_element_type=jnp.float32)
            * score_scale
        )
        key_part = (
            jnp.einsum("hqk,qhd->khd", grad_score, query_heads, preferred_element_type=jnp.float32)
            * score_scale
        ).reshape(key_block, model_width)
        value_part = jnp.einsum(
            "hqk,qhd->khd", prob_low, grad_mixed_heads, preferred_element_type=jnp.float32
        ).reshape(key_block, model_width)
        grad_key_all = lax.dynamic_update_slice_in_dim(grad_key_all, key_part, pieces[5], 0)
        grad_value_all = lax.dynamic_update_slice_in_dim(grad_value_all, value_part, pieces[5], 0)
        grad_table = grad_table + table_part(grad_score, edges_np, pieces[4])
        return (grad_query, grad_key_all, grad_value_all, grad_table)

    start_back = (
        start_query,
        jnp.zeros((length, model_width), jnp.float32),
        jnp.zeros((length, model_width), jnp.float32),
        start_table,
    )
    grad_query, grad_key_all, grad_value_all, grad_table = lax.fori_loop(
        0, block_count, back_step, start_back
    )
    grad_keys, grad_values = (
        lax.psum_scatter(
            grad_key_all.astype(jnp.bfloat16), "seq", scatter_dimension=0, tiled=True
        ).astype(jnp.float32),
        lax.psum_scatter(
            grad_value_all.astype(jnp.bfloat16), "seq", scatter_dimension=0, tiled=True
        ).astype(jnp.float32),
    )
    grad_proj = jnp.concatenate(
        [
            grad_query.reshape(row_count, model_width).astype(jnp.bfloat16),
            grad_keys.astype(jnp.bfloat16),
            grad_values.astype(jnp.bfloat16),
        ],
        axis=1,
    )
    grad_w_qkv = lax.dot_general(
        normed_one, grad_proj, (((0,), (0,)), ((), ())), preferred_element_type=jnp.float32
    )
    grad_normed_one = lax.dot_general(
        grad_proj, back_qkv, (((1,), (1,)), ((), ())), preferred_element_type=jnp.float32
    )
    grad_input_norm, grad_gain_one = norm_back(grad_normed_one, scaled_one, factor_one, gain_one)
    grad_inputs = grad_hidden + grad_input_norm
    table_total, gain_one_total, gain_two_total = lax.psum(
        (grad_table, grad_gain_one, grad_gain_two), ("dp", "seq")
    )
    shares = (
        lax.psum_scatter(grad_w_qkv, ("dp", "seq"), scatter_dimension=0, tiled=True),
        lax.psum_scatter(grad_w_attn, ("dp", "seq"), scatter_dimension=0, tiled=True),
        lax.psum_scatter(grad_w_in, ("dp", "seq"), scatter_dimension=1, tiled=True),
        lax.psum_scatter(grad_w_out, ("dp", "seq"), scatter_dimension=1, tiled=True),
    )
    return (
        output[None],
        grad_inputs[None],
        gain_one_total,
        shares[0],
        shares[1],
        table_total,
        gain_two_total,
        shares[2],
        shares[3],
    )


def rows_solution(mesh):
    return jax.shard_map(
        body,
        mesh=mesh,
        in_specs=(
            P("dp", "seq", None),
            P("dp", "seq", None),
            P("dp", "seq"),
            P("dp", "seq"),
            P("dp", "seq", None),
            P("dp", "seq", None),
            P(),
            P(("dp", "seq"), None),
            P(("dp", "seq"), None),
            P(),
            P(),
            P(None, ("dp", "seq"), None),
            P(None, ("dp", "seq"), None),
        ),
        out_specs=(
            P("dp", "seq", None),
            P("dp", "seq", None),
            P(),
            P(("dp", "seq"), None),
            P(("dp", "seq"), None),
            P(),
            P(),
            P(None, ("dp", "seq"), None),
            P(None, ("dp", "seq"), None),
        ),
        check_vma=False,
    )


F32 = jnp.float32
BF16 = jnp.bfloat16
ROWS = 128
EXT = 128
TAB_AT = 256
AXES = ("z", "y", "x", "c")
MIB = 1024 * 1024
BYTES_US = 3690000


def swap(value, axis, step=1):
    size = lax.axis_size(axis)
    return lax.ppermute(value, axis, [(i, i ^ step) for i in range(size)])


def after(value, *earlier):
    return lax.optimization_barrier((value, earlier))[0]


def gather_seq(value):
    along_x = swap(value, "x")
    return value, along_x, swap(value, "c"), swap(along_x, "c")


def reduce_seq(keep, send):
    rows = keep.shape[0] // 2
    pair = keep + swap(send, "c").astype(F32)
    return pair[:rows] + swap(pair[rows:].astype(BF16), "x").astype(F32)


def mm(a, b):
    return lax.dot_general(a, b, (((1,), (0,)), ((), ())), preferred_element_type=F32)


def mm_t(a, b):
    return lax.dot_general(a, b, (((1,), (1,)), ((), ())), preferred_element_type=F32)


def t_mm(a, b):
    return lax.dot_general(a, b, (((0,), (0,)), ((), ())), preferred_element_type=F32)


SLOTS = (0, 2, 1, 3)


def slot_rows(slot, me):
    block = jnp.bitwise_xor(me, SLOTS[slot])
    return pl.ds(pl.multiple_of(block * ROWS, ROWS), ROWS)


def tile_distance(offset):
    row = lax.broadcasted_iota(jnp.int32, (ROWS, ROWS), 0)
    col = lax.broadcasted_iota(jnp.int32, (ROWS, ROWS), 1)
    return offset + row - col


def fill_bias(bias_ref, tab_ref, heads):
    edges = [int(e) for e in bucket_edges()]
    for near in range(2):
        distance = tile_distance(near * ROWS)
        tiles = [jnp.full((ROWS, ROWS), tab_ref[h, 0], F32) for h in range(heads)]
        for b, edge in enumerate(edges):
            above = distance >= edge
            tiles = [jnp.where(above, tab_ref[h, b + 1], tiles[h]) for h in range(heads)]
        for h in range(heads):
            bias_ref[near * heads + h] = tiles[h]


def read_marks(xs_ref, width, blocks):
    seg_cols, info_rows = [], []
    for i in range(blocks):
        marks = xs_ref[i * ROWS : (i + 1) * ROWS, width : width + EXT].astype(F32)
        seg_cols.append(marks[:, 0:1])
        info_rows.append(marks.T[1:2, :])
    return seg_cols, info_rows


def mask_tiles(i, seg_cols, info_rows):
    tiles = []
    for j in range(i + 1):
        seen = info_rows[j] == seg_cols[i]
        if j == i:
            distance = tile_distance(0)
            seen = (distance == 0) | ((distance > 0) & seen)
        tiles.append(jnp.where(seen, 0.0, -1e30))
    return tiles


def add_tiles(i, h, heads, masks, bias_ref, tab_ref):
    tiles = []
    for j in range(i + 1):
        if i - j < 2:
            tiles.append(masks[j] + bias_ref[(i - j) * heads + h])
        else:
            tiles.append(masks[j] + tab_ref[h, BUCKETS - 1])
    return jnp.concatenate(tiles, axis=1) if len(tiles) > 1 else tiles[0]


def copies(pairs, sem_ref):
    return [pltpu.make_async_copy(a, b, sem_ref.at[n]) for n, (a, b) in enumerate(pairs)]


def attend_kernel(
    me_ref,
    place_ref,
    tab_ref,
    x0_ref,
    x1_ref,
    x2_ref,
    x3_ref,
    gain_ref,
    *refs,
):
    w_refs = refs[:2]
    mixed_ref = refs[2]
    home = refs[3:8]
    kept = refs[8:13]
    blocks_ref, bias_ref, sem_ref = refs[13:]
    xs_ref, n1_ref, wq_ref, qkv_ref, lse_ref = kept
    out = copies(zip(kept, home), sem_ref)
    me, place = me_ref[0], place_ref[0]
    width = gain_ref.shape[1]
    third = wq_ref.shape[1] // 3
    heads = tab_ref.shape[0]
    size = third // heads
    blocks = xs_ref.shape[0] // ROWS
    devices, shard = blocks_ref.shape[0], blocks_ref.shape[1]
    scale = size ** (-0.5)
    fill_bias(bias_ref, tab_ref, heads)
    for slot, x_ref in enumerate((x0_ref, x1_ref, x2_ref, x3_ref)):
        rows = slot_rows(slot, me)
        xs_ref[rows, :] = x_ref[...]
        x = x_ref[:, :width].astype(F32)
        factor = lax.rsqrt(jnp.mean(x * x, axis=-1, keepdims=True) + 1e-06)
        n1_ref[rows, :] = (x * factor * gain_ref[...]).astype(BF16)
    out[0].start()
    out[1].start()
    for n, w_ref in enumerate(w_refs):
        y = jnp.bitwise_xor(jnp.bitwise_and(place, 1), n)
        for i in range(devices // 2):
            blocks_ref[(2 * (i // blocks) + y) * blocks + i % blocks] = w_ref[i]
    for i in range(devices):
        wq_ref[i * shard : (i + 1) * shard, :] = blocks_ref[i]
    out[2].start()
    qkv_ref[...] = mm(n1_ref[...], wq_ref[...]).astype(BF16)
    out[3].start()
    seg_cols, info_rows = read_marks(xs_ref, width, blocks)
    lane = lax.broadcasted_iota(jnp.int32, (ROWS, EXT), 1)
    for i in range(blocks):
        masks = mask_tiles(i, seg_cols, info_rows)
        span = (i + 1) * ROWS
        rows = slice(i * ROWS, span)
        outs = []
        lse = jnp.zeros((ROWS, EXT), F32)
        for h in range(heads):
            q = qkv_ref[rows, h * size : (h + 1) * size]
            k = qkv_ref[0:span, third + h * size : third + (h + 1) * size]
            v = qkv_ref[0:span, 2 * third + h * size : 2 * third + (h + 1) * size]
            scores = mm_t(q, k) * scale + add_tiles(i, h, heads, masks, bias_ref, tab_ref)
            top = jnp.max(scores, axis=-1, keepdims=True)
            weight = jnp.exp(scores - top)
            total = jnp.sum(weight, axis=-1, keepdims=True)
            prob = (weight * (1.0 / total)).astype(BF16)
            outs.append(mm(prob, v))
            lse = jnp.where(lane == h, top + jnp.log(total), lse)
        mixed_ref[rows, :] = jnp.concatenate(outs, axis=1).astype(BF16)
        lse_ref[rows, :] = lse
    out[4].start()
    for copy in out:
        copy.wait()


def project_kernel(me_ref, mixed_ref, watt_ref, keep_ref, send_ref):
    me = me_ref[0]
    for slot in range(len(SLOTS)):
        part = mm(mixed_ref[slot_rows(slot, me), :], watt_ref[...])
        if slot < 2:
            keep_ref[slot * ROWS : (slot + 1) * ROWS, :] = part
        else:
            send_ref[(slot - 2) * ROWS : (slot - 1) * ROWS, :] = part.astype(BF16)


def attend_back_kernel(
    me_ref,
    place_ref,
    tab_ref,
    b0_ref,
    b1_ref,
    b2_ref,
    b3_ref,
    watt_ref,
    gain_two_ref,
    *refs,
):
    home = refs[:6]
    wkeep_ref, wsend_ref, keep_ref, send_ref = refs[6:10]
    kept = refs[10:16]
    bias_ref, dm_ref, dk_ref, dv_ref, proj_ref, gtab_ref, small_ref, grad_ref, sem_ref = refs[16:]
    xs_ref, n1_ref, wq_ref, qkv_ref, lse_ref, mixed_ref = kept
    fetch = copies(zip(home, kept), sem_ref)
    for copy in fetch:
        copy.start()
    me = me_ref[0]
    width = watt_ref.shape[1]
    third = wq_ref.shape[1] // 3
    heads = tab_ref.shape[0]
    size = third // heads
    blocks = xs_ref.shape[0] // ROWS
    scale = size ** (-0.5)
    fill_bias(bias_ref, tab_ref, heads)
    for slot, b_ref in enumerate((b0_ref, b1_ref, b2_ref, b3_ref)):
        dm_ref[slot_rows(slot, me), :] = mm_t(b_ref[...], watt_ref[...]).astype(BF16)
    for copy in fetch:
        copy.wait()
    seg_cols, info_rows = read_marks(xs_ref, width, blocks)
    dk_ref[...] = jnp.zeros_like(dk_ref)
    dv_ref[...] = jnp.zeros_like(dv_ref)
    near = [[jnp.zeros((ROWS, ROWS), F32) for _ in range(heads)] for _ in range(2)]
    far = [jnp.zeros((1, ROWS), F32) for _ in range(heads)]
    for i in range(blocks):
        masks = mask_tiles(i, seg_cols, info_rows)
        span = (i + 1) * ROWS
        rows = slice(i * ROWS, span)
        for h in range(heads):
            own = slice(h * size, (h + 1) * size)
            q = qkv_ref[rows, own]
            k = qkv_ref[0:span, third + h * size : third + (h + 1) * size]
            v = qkv_ref[0:span, 2 * third + h * size : 2 * third + (h + 1) * size]
            dm = dm_ref[rows, own]
            scores = mm_t(q, k) * scale + add_tiles(i, h, heads, masks, bias_ref, tab_ref)
            prob = jnp.exp(scores - lse_ref[rows, h : h + 1])
            grad_prob = mm_t(dm, v)
            delta = jnp.sum(prob * grad_prob, axis=-1, keepdims=True)
            grad_score = (prob * (grad_prob - delta)).astype(BF16)
            proj_ref[rows, own] = (mm(grad_score, k) * scale).astype(BF16)
            dk_ref[0:span, own] += t_mm(grad_score, q)
            dv_ref[0:span, own] += t_mm(prob.astype(BF16), dm)
            for j in range(i + 1):
                tile = grad_score[:, j * ROWS : (j + 1) * ROWS].astype(F32)
                if i - j < 2:
                    near[i - j][h] = near[i - j][h] + tile
                else:
                    far[h] = far[h] + jnp.sum(tile, axis=0, keepdims=True)
    proj_ref[:, third : 2 * third] = (dk_ref[...] * scale).astype(BF16)
    proj_ref[:, 2 * third :] = dv_ref[...].astype(BF16)
    gtab_ref[...] = jnp.zeros_like(gtab_ref)
    edges = [int(e) for e in bucket_edges()]
    buckets = []
    for n in range(2):
        distance = tile_distance(n * ROWS)
        count = jnp.zeros((ROWS, ROWS), jnp.int32)
        for edge in edges:
            count = count + (distance >= edge).astype(jnp.int32)
        buckets.append(count)
    for b in range(BUCKETS):
        picks = [buckets[n] == b for n in range(2)]
        for h in range(heads):
            line = jnp.sum(
                jnp.where(picks[0], near[0][h], 0.0) + jnp.where(picks[1], near[1][h], 0.0),
                axis=0,
                keepdims=True,
            )
            if b == BUCKETS - 1:
                line = line + far[h]
            gtab_ref[h * BUCKETS + b : h * BUCKETS + b + 1, :] = line
    gain = jnp.zeros((1, width), F32)
    for slot in range(blocks):
        rows = slot_rows(slot, me)
        x = xs_ref[rows, :width].astype(F32)
        factor = lax.rsqrt(jnp.mean(x * x, axis=-1, keepdims=True) + 1e-06)
        part = mm_t(proj_ref[rows, :], wq_ref[...])
        if slot < 2:
            keep_ref[slot * ROWS : (slot + 1) * ROWS, :] = part
        else:
            send_ref[(slot - 2) * ROWS : (slot - 1) * ROWS, :] = part.astype(BF16)
        gain = gain + jnp.sum(part * (x * factor), axis=0, keepdims=True)
    wide = 3 * third
    table = jnp.sum(gtab_ref[...].T, axis=0, keepdims=True)
    small_ref[...] = jnp.zeros_like(small_ref)
    for n, value in enumerate((gain, gain_two_ref[...])):
        for m, piece in enumerate(halves(value)):
            small_ref[4 * n + 2 * m : 4 * n + 2 * m + 1, :] = piece[:, :wide]
            small_ref[4 * n + 2 * m + 1 : 4 * n + 2 * m + 2, : width - wide] = piece[:, wide:]
    for m, piece in enumerate(halves(table)):
        small_ref[2 * m + 1 : 2 * m + 2, TAB_AT : TAB_AT + EXT] = piece
    small = small_ref[...].astype(BF16)
    grad = t_mm(n1_ref[...], proj_ref[...])
    att = 0.0
    for slot, b_ref in enumerate((b0_ref, b1_ref, b2_ref, b3_ref)):
        att = att + t_mm(mixed_ref[slot_rows(slot, me), :], b_ref[...])
    groups, rows = grad_ref.shape[0], grad_ref.shape[1]
    shard = third // groups
    main = width // groups
    for n in range(groups):
        grad_ref[n, :main, :] = grad[n * main : (n + 1) * main, :]
        piece = att[n * shard : (n + 1) * shard, :]
        grad_ref[n, main : main + shard, :] = piece[:, :wide]
        for m in range(3):
            grad_ref[n, main + shard :, m * third : (m + 1) * third] = piece[
                m * 8 : (m + 1) * 8, wide:
            ]
    own = jnp.bitwise_and(place_ref[0], 1)
    for z in range(groups // 2):
        wkeep_ref[z * rows : (z + 1) * rows, :] = grad_ref[2 * z + own]
        wsend_ref[z * rows : (z + 1) * rows, :] = grad_ref[2 * z + 1 - own].astype(BF16)
    wkeep_ref[groups // 2 * rows :, :] = small.astype(F32)
    wsend_ref[groups // 2 * rows :, :] = small


def halves(value):
    high = value.astype(BF16).astype(F32)
    return high, value - high


def split_small(rows):
    pieces = []
    for n in range(2):
        pieces += halves(rows[4 * n : 4 * n + 2] + rows[4 * n + 2 : 4 * n + 4])
    return jnp.concatenate(pieces, axis=0).astype(BF16)


def fold_y_kernel(place_ref, keep_ref, got_ref, own_ref, *refs):
    sends, block_ref = refs[:-1], refs[-1]
    count, rows = block_ref.shape[0], block_ref.shape[1]
    total = keep_ref[...] + got_ref[...].astype(F32)
    for z in range(count):
        block_ref[z] = total[z * rows : (z + 1) * rows, :]
    small = split_small(total[count * rows :, :])
    me = jnp.right_shift(place_ref[0], 1)
    own_ref[:rows, :] = block_ref[me]
    own_ref[rows:, :] = small.astype(F32)
    for k, send_ref in enumerate(sends):
        send_ref[:rows, :] = block_ref[jnp.bitwise_xor(me, k + 1)].astype(BF16)
        send_ref[rows:, :] = small


def fold_z_kernel(me_ref, own_ref, *refs):
    gots, att_ref, keep_ref, sends, block_ref = refs[:3], refs[3], refs[4], refs[5:-1], refs[-1]
    count, shard, wide = block_ref.shape
    third = wide // 3
    total = (own_ref[...] + gots[0][...].astype(F32)) + (
        gots[1][...].astype(F32) + gots[2][...].astype(F32)
    )
    for s in range(count):
        block_ref[s] = total[s * shard : (s + 1) * shard, :]
    main = count * shard
    att_ref[:, :wide] = total[main : main + shard, :].astype(BF16)
    rest = total[main + shard : main + shard + 8, :]
    att_ref[:, wide:] = jnp.concatenate(
        [rest[:, m * third : (m + 1) * third] for m in range(3)], axis=0
    ).astype(BF16)
    small = split_small(total[main + shard + 8 :, :])
    keep_ref[:shard, :] = block_ref[me_ref[0]]
    keep_ref[shard:, :] = small.astype(F32)
    for k, send_ref in enumerate(sends):
        send_ref[:shard, :] = block_ref[jnp.bitwise_xor(me_ref[0], SLOTS[k + 1])].astype(BF16)
        send_ref[shard:, :] = small


def fold_seq_kernel(me_ref, *refs):
    pieces, gwq_ref, one_ref, two_ref, tab_ref, block_ref, table_ref = (
        refs[:4],
        *refs[4:],
    )
    parts, shard = block_ref.shape[0], block_ref.shape[1]
    wide = block_ref.shape[2]
    width = one_ref.shape[1]
    third = wide // 3
    values = [piece[...].astype(F32) for piece in pieces]
    for slot, value in enumerate(values):
        s = jnp.bitwise_xor(me_ref[0], SLOTS[slot])
        block_ref[s] = value[:shard]
        table_ref[s] = jnp.broadcast_to(
            (value[shard + 1 : shard + 2] + value[shard + 3 : shard + 4])[
                :, TAB_AT : TAB_AT + EXT
            ],
            (8, EXT),
        )
    for s in range(parts):
        for n in range(3):
            at = n * width + s * third
            gwq_ref[:, at : at + third] = block_ref[s, :, n * third : (n + 1) * third]
        tab_ref[s : s + 1, :] = table_ref[s, 0:1, :]
    small = (values[0][shard:] + values[1][shard:]) + (values[2][shard:] + values[3][shard:])
    for n, out_ref in enumerate((one_ref, two_ref)):
        out_ref[:, :wide] = small[4 * n : 4 * n + 1] + small[4 * n + 2 : 4 * n + 3]
        rest = small[4 * n + 1 : 4 * n + 2] + small[4 * n + 3 : 4 * n + 4]
        out_ref[:, wide:] = rest[:, : width - wide]


def qkv_send_kernel(w_ref, send_ref):
    count, shard, wide = send_ref.shape
    third = wide // 3
    width = w_ref.shape[1] // 3
    parts = width // third
    for p in range(parts):
        for n in range(3):
            at = n * width + p * third
            piece = w_ref[:, at : at + third]
            for i in range(p, count, parts):
                send_ref[i, :, n * third : (n + 1) * third] = piece


def in_send_kernel(w_ref, send_ref):
    devices, shard, wide = send_ref.shape
    experts = w_ref.shape[0]
    own = wide // experts
    for i in range(devices):
        for e in range(experts):
            send_ref[i, :, e * own : (e + 1) * own] = w_ref[e, :, i * own : (i + 1) * own]


def in_last_kernel(got_ref, grad_ref):
    devices, shard, wide = got_ref.shape
    experts = grad_ref.shape[0]
    own = wide // experts
    for i in range(devices):
        for e in range(experts):
            grad_ref[e, :, i * own : (i + 1) * own] = got_ref[
                i, :, e * own : (e + 1) * own
            ].astype(F32)


def expert_kernel(
    xa_ref,
    xb_ref,
    ga_ref,
    gb_ref,
    w1a_ref,
    w1b_ref,
    w2a_ref,
    w2b_ref,
    pick_ref,
    act_home,
    pre_home,
    keep_ref,
    send_ref,
    x_ref,
    g_ref,
    act_ref,
    pre_ref,
    sem_ref,
):
    rows, width = xa_ref.shape
    half = w1a_ref.shape[1]
    tile_cols = 256
    root = math.sqrt(2.0 / math.pi)
    x_ref[:rows, :] = xa_ref[...]
    x_ref[rows:, :] = xb_ref[...]
    g_ref[:rows, :] = ga_ref[...]
    g_ref[rows:, :] = gb_ref[...]

    def tile(t, carry):
        cols = pl.ds(pl.multiple_of(t * tile_cols, tile_cols), tile_cols)
        for side, (w1_ref, w2_ref) in enumerate(((w1a_ref, w2a_ref), (w1b_ref, w2b_ref))):
            out_cols = pl.ds(pl.multiple_of(side * half + t * tile_cols, tile_cols), tile_cols)
            choose = mm(g_ref[:, width:], pick_ref[:, cols])
            v = mm(x_ref[...], w1_ref[:, cols])
            square = v * v
            curve = jnp.tanh(root * v * (1.0 + 0.044715 * square))
            part = 0.5 * (1.0 + curve)
            slope = part + 0.5 * v * (1.0 - curve * curve) * (
                root * (1.0 + 3 * 0.044715 * square)
            )
            act_ref[:, out_cols] = (choose * (v * part)).astype(BF16)
            grad_act = mm_t(g_ref[:, :width], w2_ref[cols, :])
            grad_pre = (choose * grad_act * slope).astype(BF16)
            pre_ref[:, out_cols] = grad_pre
        return carry

    lax.fori_loop(0, half // tile_cols, tile, 0)
    home = copies([(act_ref, act_home), (pre_ref, pre_home)], sem_ref)
    for copy in home:
        copy.start()
    grad_x = mm_t(pre_ref[:, :half], w1a_ref[...]) + mm_t(pre_ref[:, half:], w1b_ref[...])
    keep_ref[...] = grad_x[:rows, :]
    send_ref[...] = grad_x[rows:, :].astype(BF16)
    for copy in home:
        copy.wait()


def expert_out_kernel(count, w2a_ref, w2b_ref, *refs):
    acts, keep_ref, send_ref, act_ref, sem_ref = refs[:count], *refs[count:]
    rows = keep_ref.shape[1]
    half = w2a_ref.shape[0]
    fetch = copies([(act, act_ref.at[k]) for k, act in enumerate(acts)], sem_ref)
    for copy in fetch:
        copy.start()
    for k in range(count):
        fetch[k].wait()
        out = mm(act_ref[k, :, :half], w2a_ref[...]) + mm(act_ref[k, :, half:], w2b_ref[...])
        keep_ref[k] = out[:rows]
        send_ref[k] = out[rows:].astype(BF16)


def in_grad_kernel(count, *refs):
    xs, pres = refs[: 2 * count], refs[2 * count : 3 * count]
    own_ref, far_ref, xt_ref, pre_ref, sem_ref = refs[3 * count :]
    rows = xs[0].shape[0]
    half = own_ref.shape[1]
    step = 256
    fetch = copies(
        [(p, pre_ref.at[pl.ds(k * 2 * rows, 2 * rows)]) for k, p in enumerate(pres)], sem_ref
    )
    for copy in fetch:
        copy.start()
    for k in range(2 * count):
        xt_ref[:, k * rows : (k + 1) * rows] = xs[k][...].T
    for copy in fetch:
        copy.wait()

    def tile(t, carry):
        cols = pl.ds(pl.multiple_of(t * step, step), step)
        cols_far = pl.ds(pl.multiple_of(half + t * step, step), step)
        far_ref[:, cols] = mm(xt_ref[...], pre_ref[:, cols_far]).astype(BF16)
        own_ref[:, cols] = mm(xt_ref[...], pre_ref[:, cols])
        return carry

    lax.fori_loop(0, half // step, tile, 0)


def out_grad_kernel(count, *refs):
    gs, acts = refs[: 2 * count], refs[2 * count : 3 * count]
    own_ref, far_ref, g_ref, act_ref, sem_ref = refs[3 * count :]
    rows = gs[0].shape[0]
    half, width = own_ref.shape
    step = 256
    pairs = [(a, act_ref.at[pl.ds(k * 2 * rows, 2 * rows)]) for k, a in enumerate(acts)]
    for n, g in enumerate(gs):
        pairs.append((g, g_ref.at[pl.ds(n * rows, rows)]))
    fetch = copies(pairs, sem_ref)
    for copy in fetch:
        copy.start()
    for copy in fetch:
        copy.wait()

    def tile(t, carry):
        cols = pl.ds(pl.multiple_of(t * step, step), step)
        cols_far = pl.ds(pl.multiple_of(half + t * step, step), step)
        far_ref[cols, :] = t_mm(act_ref[:, cols_far], g_ref[:, :width]).astype(BF16)
        own_ref[cols, :] = t_mm(act_ref[:, cols], g_ref[:, :width])
        return carry

    lax.fori_loop(0, half // step, tile, 0)


def call(kernel, outs, args, us, scratch=(), scalars=0, far=(), home=(), mib=60):
    smem = pl.BlockSpec(memory_space=pltpu.SMEM)
    vmem = pl.BlockSpec(memory_space=pltpu.VMEM)
    hbm = pl.BlockSpec(memory_space=pltpu.HBM)
    return pl.pallas_call(
        kernel,
        out_shape=[jax.ShapeDtypeStruct(shape, dtype) for shape, dtype in outs],
        in_specs=[smem] * scalars
        + [hbm if n in far else vmem for n in range(scalars, len(args))],
        out_specs=[hbm if n in home else vmem for n in range(len(outs))],
        scratch_shapes=list(scratch),
        compiler_params=pltpu.CompilerParams(vmem_limit_bytes=mib * MIB),
        cost_estimate=pl.CostEstimate(
            flops=0, bytes_accessed=int(us * BYTES_US), transcendentals=0
        ),
    )(*args)


def head_body(
    tokens,
    cotangent,
    segment_ids,
    pad_mask,
    routes,
    gate_weights,
    gain_one,
    w_qkv,
    w_attn,
    rel_table,
    gain_two,
    w_expert_in,
    w_expert_out,
):
    x_low = tokens[0]
    g_low = cotangent[0]
    rows, width = x_low.shape
    size_z, size_y, size_x, size_c = (lax.axis_size(a) for a in AXES)
    parts = size_x * size_c
    devices = size_z * size_y * parts
    me = lax.axis_index(("x", "c"))
    head_count = rel_table.shape[0]
    heads = head_count // parts
    third = width // parts
    length = rows * parts
    experts, shard, ff = w_expert_in.shape
    ff_own = ff // devices
    me_arr = me.astype(jnp.int32).reshape(1)

    seg = segment_ids[0]
    info = jnp.where(pad_mask[0] == 1, seg, -1)
    marks = jnp.stack([seg, info], axis=1).astype(BF16)
    x_ext = jnp.concatenate([x_low, jnp.pad(marks, ((0, 0), (0, EXT - 2)))], axis=1)
    x_slots = gather_seq(x_ext)

    groups = devices // parts
    across = [(i, i ^ 3) for i in range(parts)]
    to_part = [((i % groups) * parts + i // groups) for i in range(devices)]
    expert_ids = jnp.arange(experts, dtype=jnp.int32)
    choose = jnp.sum(
        gate_weights[0][:, :, None] * (routes[0][:, :, None] == expert_ids).astype(F32), axis=1
    )
    choose_hi = choose.astype(BF16)
    choose_lo = (choose - choose_hi.astype(F32)).astype(BF16)
    g_ext = jnp.concatenate(
        [g_low, choose_hi, choose_lo, jnp.zeros((rows, EXT - 2 * experts), BF16)], axis=1
    )
    g_own = [g_ext] + [swap(g_ext, "z", k) for k in range(1, size_z)]
    g_far = [swap(g, "y") for g in g_own]

    q_send = call(
        qkv_send_kernel,
        [((devices // 2, shard, 3 * third), BF16)],
        [w_qkv],
        us=1,
        mib=8,
    )[0]
    q_own = lax.all_to_all(q_send, ("z", "x", "c"), 0, 0, tiled=True)

    att_one = lax.ppermute(w_attn, AXES, [(i, to_part[i]) for i in range(devices)])
    z_index = lax.axis_index("z")
    y_index = lax.axis_index("y")
    att_z = jnp.zeros((size_z, shard, width), BF16)
    for k in range(size_z):
        piece = att_one if k == 0 else swap(att_one, "z", k)
        att_z = lax.dynamic_update_slice_in_dim(
            att_z, piece[None], jnp.bitwise_xor(z_index, k), 0
        )
    att_y = swap(att_z, "y")
    watt = jnp.where(
        y_index == 0, jnp.stack([att_z, att_y], axis=1), jnp.stack([att_y, att_z], axis=1)
    ).reshape(third, width)

    w2_own = w_expert_out.reshape(experts * ff_own, width)
    w2_x = swap(w2_own, "x")
    w2a = jnp.concatenate([w2_own, w2_x], axis=0)
    w2b = swap(w2a, "c")
    q_own = after(q_own, att_z, x_slots, w2_x)
    q_far = swap(q_own, "y")

    in_send = call(
        in_send_kernel,
        [((devices, shard, experts * ff_own), BF16)],
        [w_expert_in],
        us=1.2,
        mib=16,
    )[0]
    in_send = after(in_send, q_own)
    w1_own = lax.all_to_all(in_send, AXES, 0, 0, tiled=True).reshape(width, experts * ff_own)

    w1_x = swap(w1_own, "x")

    place_arr = lax.axis_index(("z", "y")).astype(jnp.int32).reshape(1)

    table = lax.dynamic_slice_in_dim(rel_table, me * heads, heads, 0).astype(F32)
    half = length // 2
    kept = [
        ((length, width + EXT), BF16),
        ((length, width), BF16),
        ((width, 3 * third), BF16),
        ((length, 3 * third), BF16),
        ((length, EXT), F32),
    ]
    kept_scratch = [pltpu.VMEM(shape, dtype) for shape, dtype in kept]
    mixed, *saved = call(
        attend_kernel,
        [((length, third), BF16), *kept],
        [me_arr, place_arr, table, *x_slots, gain_one.reshape(1, width), q_own, q_far],
        scratch=[
            *kept_scratch,
            pltpu.VMEM((devices, shard, 3 * third), BF16),
            pltpu.VMEM((2 * heads, ROWS, ROWS), F32),
            pltpu.SemaphoreType.DMA((5,)),
        ],
        scalars=3,
        home=range(1, 6),
        us=8,
        mib=60,
    )
    saved = [*saved, mixed]
    keep, send = call(
        project_kernel,
        [((half, width), F32), ((half, width), BF16)],
        [me_arr, after(mixed, g_own), watt],
        scalars=1,
        us=1,
        mib=16,
    )
    inputs = x_low.astype(F32)
    hidden_one = after(inputs, w1_own) + reduce_seq(keep, send)
    scaled_two, factor_two = norm_stats(hidden_one)
    normed_two = (scaled_two * gain_two).astype(BF16)

    ff_two = parts * experts * ff_own
    pick_np = np.zeros((EXT, ff_two // 2), np.float32)
    for col in range(ff_two // 2):
        e = col // ff_own % experts
        pick_np[[e, experts + e], col] = 1.0
    pick = jnp.asarray(pick_np, BF16)
    pair = 2 * rows
    x_own = [normed_two] + [swap(normed_two, "z", k) for k in range(1, size_z)]
    x_far = [swap(after(x, g_far, x_own[2]) if k == 1 else x, "y") for k, x in enumerate(x_own)]
    w1a = jnp.concatenate([after(w1_own, x_far[1]), after(w1_x, x_far[1])], axis=1)
    w1b = swap(w1a, "c")
    order = [*range(1, size_z), 0]
    acts, pres, keeps, gots, backs, far_back = {}, {}, {}, {}, {}, {}
    for n, k in enumerate(order):
        earlier = [acts[order[n - 1]]] if n else []
        if n >= 2:
            earlier.append(backs[order[n - 2]])
        if n >= 3:
            earlier.append(far_back[order[n - 3]])
        x_here = after(x_own[k], *earlier)
        act, pre, dx_keep, dx_send = call(
            expert_kernel,
            [
                ((pair, ff_two), BF16),
                ((pair, ff_two), BF16),
                ((rows, width), F32),
                ((rows, width), BF16),
            ],
            [x_here, x_far[k], g_own[k], g_far[k], w1a, w1b, w2a, w2b, pick],
            scratch=[
                pltpu.VMEM((pair, width), BF16),
                pltpu.VMEM((pair, width + EXT), BF16),
                pltpu.VMEM((pair, ff_two), BF16),
                pltpu.VMEM((pair, ff_two), BF16),
                pltpu.SemaphoreType.DMA((2,)),
            ],
            home=(0, 1),
            mib=20,
        us=5.5,
        )
        acts[k], pres[k], keeps[k] = act, pre, dx_keep
        gots[k] = swap(dx_send, "y")
        backs[k] = dx_keep + gots[k].astype(F32)
        if k:
            far_back[k] = swap(backs[k].astype(BF16), "z", k)
    acts, pres = [acts[k] for k in range(size_z)], [pres[k] for k in range(size_z)]
    ready = [keeps[order[-1]], backs[order[-2]], far_back[order[-3]]]

    ff_half = ff_two // 2
    out_keep, out_send = call(
        functools.partial(expert_out_kernel, size_z),
        [((size_z, rows, width), F32), ((size_z, rows, width), BF16)],
        [w2a, w2b, after(acts[0], *ready), *acts[1:]],
        scratch=[
            pltpu.VMEM((size_z, pair, ff_two), BF16),
            pltpu.SemaphoreType.DMA((size_z,)),
        ],
        far=range(2, 2 + size_z),
        us=4.4,
        mib=24,
    )
    in_own, in_far = call(
        functools.partial(in_grad_kernel, size_z),
        [((width, ff_half), F32), ((width, ff_half), BF16)],
        [*[x for both in zip(x_own, x_far) for x in both], *pres[:-1], after(pres[-1], out_send)],
        scratch=[
            pltpu.VMEM((width, size_z * pair), BF16),
            pltpu.VMEM((size_z * pair, ff_two), BF16),
            pltpu.SemaphoreType.DMA((size_z,)),
        ],
        far=range(2 * size_z, 3 * size_z),
        us=6,
        mib=24,
    )
    grad_normed_two = after(backs[0], in_far)
    for k in range(1, size_z):
        grad_normed_two = grad_normed_two + far_back[k].astype(F32)

    grad_hidden_norm, gain_two_part = norm_back(grad_normed_two, scaled_two, factor_two, gain_two)
    grad_hidden = g_low.astype(F32) + grad_hidden_norm
    branch_low = grad_hidden.astype(BF16)
    branch = gather_seq(branch_low)

    quarter = ff_half // 2
    in_c = after(in_own, branch_low) + swap(in_far, "c").astype(F32)
    in_x_got = swap(after(in_c[:, quarter:].astype(BF16), branch[1]), "x")
    out_y = out_keep + swap(out_send, "y").astype(F32)
    extra = 8
    wide = 3 * third
    rows_y = parts * shard + shard * width // wide
    w_keep, w_send, gno_keep, gno_send = call(
        attend_back_kernel,
        [
            ((size_z * rows_y + extra, wide), F32),
            ((size_z * rows_y + extra, wide), BF16),
            ((half, width), F32),
            ((half, width), BF16),
        ],
        [
            me_arr,
            place_arr,
            table,
            *branch,
            watt,
            after(gain_two_part.reshape(1, width), out_y, in_c),
            *saved,
        ],
        scratch=[
            *kept_scratch,
            pltpu.VMEM((length, third), BF16),
            pltpu.VMEM((2 * heads, ROWS, ROWS), F32),
            pltpu.VMEM((length, third), BF16),
            pltpu.VMEM((length, third), F32),
            pltpu.VMEM((length, third), F32),
            pltpu.VMEM((length, wide), BF16),
            pltpu.VMEM((EXT, ROWS), F32),
            pltpu.VMEM((extra, wide), F32),
            pltpu.VMEM((groups, rows_y, wide), F32),
            pltpu.SemaphoreType.DMA((6,)),
        ],
        scalars=3,
        far=range(9, 15),
        us=10,
        mib=60,
    )
    out_z = [swap(out_y[k].astype(BF16), "z", k) for k in range(1, size_z)]
    w_send = after(w_send, in_x_got, out_z)
    in_x = after(in_c[:, :quarter], w_send) + in_x_got.astype(F32)
    in_x_low = in_x.astype(BF16).reshape(devices, shard, quarter)
    in_got = lax.all_to_all(in_x_low, AXES, 0, 0, tiled=True)
    combined = after(out_y[0], w_send)
    for got in out_z:
        combined = combined + got.astype(F32)
    output = (hidden_one + combined).astype(BF16)
    first_act = after(acts[0], w_send)
    out_own, out_far = call(
        functools.partial(out_grad_kernel, size_z),
        [((ff_half, width), F32), ((ff_half, width), BF16)],
        [*[g for both in zip(g_own, g_far) for g in both], first_act, *acts[1:]],
        scratch=[
            pltpu.VMEM((size_z * pair, width + EXT), BF16),
            pltpu.VMEM((size_z * pair, ff_two), BF16),
            pltpu.SemaphoreType.DMA((3 * size_z,)),
        ],
        far=range(3 * size_z),
        us=6.5,
        mib=24,
    )
    z_keep, *z_sends = call(
        fold_y_kernel,
        [((rows_y + extra, wide), F32)] + [((rows_y + extra, wide), BF16)] * (size_z - 1),
        [place_arr, after(w_keep, out_far), swap(w_send, "y")],
        scratch=[pltpu.VMEM((size_z, rows_y, wide), F32)],
        scalars=1,
        mib=12,
        us=1,
    )
    out_c = out_own + swap(out_far, "c").astype(F32)
    out_x_got = swap(out_c[quarter:].astype(BF16), "x")
    att_share, s_keep, *s_sends = call(
        fold_z_kernel,
        [((shard, width), BF16), ((shard + extra, wide), F32)]
        + [((shard + extra, wide), BF16)] * (parts - 1),
        [me_arr, after(z_keep, out_x_got), *[swap(piece, "z", k + 1) for k, piece in enumerate(z_sends)]],
        scratch=[pltpu.VMEM((parts, shard, wide), F32)],
        scalars=1,
        mib=12,
        us=1,
    )
    grad_w_qkv, one_sum, two_sum, table_sum = call(
        fold_seq_kernel,
        [
            ((shard, 3 * width), F32),
            ((1, width), F32),
            ((1, width), F32),
            ((parts, EXT), F32),
        ],
        [
            me_arr,
            s_keep,
            swap(s_sends[0], "x"),
            swap(s_sends[1], "c"),
            lax.ppermute(s_sends[2], ("x", "c"), across),
        ],
        scratch=[
            pltpu.VMEM((parts, shard, wide), F32),
            pltpu.VMEM((parts, 8, EXT), F32),
        ],
        scalars=1,
        mib=12,
        us=1,
    )

    grad_normed_one = reduce_seq(after(gno_keep, z_keep), after(gno_send, z_keep))
    scaled_one, factor_one = norm_stats(inputs)
    grad_input_norm, unused_gain = norm_back(grad_normed_one, scaled_one, factor_one, gain_one)
    grad_inputs = grad_hidden + grad_input_norm

    grad_w_in = call(
        in_last_kernel, [((experts, shard, ff), F32)], [in_got], us=1.3, mib=16
    )[0]
    grad_w_out = (out_c[:quarter] + out_x_got.astype(F32)).reshape(experts, ff_own, width)

    grad_w_attn = lax.ppermute(
        att_share, AXES, [(to_part[i], i) for i in range(devices)]
    ).astype(F32)
    return (
        output[None],
        grad_inputs[None],
        one_sum[0],
        grad_w_qkv,
        grad_w_attn,
        table_sum[:, : heads * BUCKETS].reshape(head_count, BUCKETS),
        two_sum[0],
        grad_w_in,
        grad_w_out,
    )


def heads_fit(mesh):
    return mesh.shape["seq"] == 4 and mesh.shape["dp"] == 8


def solution(mesh):
    if not heads_fit(mesh):
        return rows_solution(mesh)
    grid = Mesh(mesh.devices.reshape(mesh.shape["dp"] // 2, 2, mesh.shape["seq"] // 2, 2), AXES)
    by_token = P(("z", "y"), ("x", "c"))
    by_row = P(AXES, None)
    by_second = P(None, AXES, None)
    return jax.shard_map(
        head_body,
        mesh=grid,
        in_specs=(
            by_token,
            by_token,
            by_token,
            by_token,
            by_token,
            by_token,
            P(),
            by_row,
            by_row,
            P(),
            P(),
            by_second,
            by_second,
        ),
        out_specs=(
            by_token,
            by_token,
            P(),
            by_row,
            by_row,
            P(),
            P(),
            by_second,
            by_second,
        ),
        check_vma=False,
    )
```

```python
import functools
import math

import jax
import jax.numpy as jnp
import numpy as np
from jax import lax
from jax.experimental import pallas as pl
from jax.experimental.pallas import tpu as pltpu
from jax.sharding import Mesh
from jax.sharding import PartitionSpec as P

BUCKETS = 32
MAX_DIST = 128
CAP = 96


def bucket_edges():
    exact_span = BUCKETS // 2
    distance = np.arange(1, 8 * MAX_DIST + 1)
    widened = np.maximum(distance, exact_span) / exact_span
    spread = exact_span + (np.log(widened) / np.log(MAX_DIST / exact_span) * exact_span).astype(
        np.int64
    )
    bucket_of = np.where(distance < exact_span, distance, np.minimum(spread, BUCKETS - 1))
    return np.array(
        [distance[np.argmax(bucket_of >= target)] for target in range(1, BUCKETS)], dtype=np.int32
    )


def norm_stats(values):
    factor = lax.rsqrt(jnp.mean(values * values, axis=-1, keepdims=True) + 1e-06)
    return (values * factor, factor)


def norm_back(grad_normed, scaled, factor, gain_vec):
    grad_scaled = grad_normed * gain_vec
    inner_mean = jnp.mean(grad_scaled * scaled, axis=-1, keepdims=True)
    return (factor * (grad_scaled - scaled * inner_mean), jnp.sum(grad_normed * scaled, axis=0))


def make_onehot(distance, edges_np):
    bucket_of = jnp.sum((distance[:, :, None] >= edges_np).astype(jnp.int32), axis=-1)
    return (bucket_of[:, :, None] == jnp.arange(BUCKETS, dtype=jnp.int32)).astype(jnp.bfloat16)


def block_bias(table_low, edges_np, distance):
    far_away = jnp.min(distance) >= int(edges_np[-1])

    def block_detailed(unused):
        return jnp.einsum(
            "qkb,hb->hqk",
            make_onehot(distance, edges_np),
            table_low,
            preferred_element_type=jnp.float32,
        )

    def block_constant(unused):
        last_col = table_low[:, BUCKETS - 1].astype(jnp.float32)
        return jnp.broadcast_to(last_col[:, None, None], (table_low.shape[0],) + distance.shape)

    return lax.cond(far_away, block_constant, block_detailed, 0)


def table_part(grad_low, edges_np, distance):
    far_away = jnp.min(distance) >= int(edges_np[-1])

    def table_detailed(unused):
        return jnp.einsum(
            "hqk,qkb->hb",
            grad_low,
            make_onehot(distance, edges_np),
            preferred_element_type=jnp.float32,
        )

    def table_constant(unused):
        totals = jnp.sum(grad_low, axis=(1, 2), dtype=jnp.float32)
        return totals[:, None] * (jnp.arange(BUCKETS) == BUCKETS - 1).astype(jnp.float32)

    return lax.cond(far_away, table_constant, table_detailed, 0)


def body(
    tokens,
    cotangent,
    segment_ids,
    pad_mask,
    routes,
    gate_weights,
    gain_one,
    w_qkv,
    w_attn,
    rel_table,
    gain_two,
    w_expert_in,
    w_expert_out,
):
    gathered = (
        lax.all_gather(w_qkv, ("dp", "seq"), axis=0, tiled=True),
        lax.all_gather(w_attn, ("dp", "seq"), axis=0, tiled=True),
        lax.all_gather(w_expert_in, ("dp", "seq"), axis=1, tiled=True),
        lax.all_gather(w_expert_out, ("dp", "seq"), axis=1, tiled=True),
    )
    full_qkv, full_attn, full_in, full_out = gathered
    inputs = tokens[0].astype(jnp.float32)
    row_count, model_width = inputs.shape
    head_count = rel_table.shape[0]
    head_size = model_width // head_count
    score_scale = head_size ** (-0.5)
    seg_local = segment_ids[0]
    seq_index = lax.axis_index("seq")
    length = row_count * lax.axis_size("seq")
    key_block = math.gcd(length, 512)
    query_pos = seq_index * row_count + jnp.arange(row_count, dtype=jnp.int32)
    block_count = ((seq_index + 1) * row_count + key_block - 1) // key_block
    edges_np = bucket_edges()
    scaled_one, factor_one = norm_stats(inputs)
    normed_one = (scaled_one * gain_one).astype(jnp.bfloat16)
    project = jnp.dot(normed_one, full_qkv, preferred_element_type=jnp.float32)
    queries = project[:, :model_width].astype(jnp.bfloat16)
    keys_local = project[:, model_width : 2 * model_width].astype(jnp.bfloat16)
    values_local = project[:, 2 * model_width :].astype(jnp.bfloat16)
    info_local = jnp.where(pad_mask[0] == 1, seg_local, -1)
    keys_all, values_all, info_all, seg_all = (
        lax.all_gather(keys_local, "seq", axis=0, tiled=True),
        lax.all_gather(values_local, "seq", axis=0, tiled=True),
        lax.all_gather(info_local, "seq", axis=0, tiled=True),
        lax.all_gather(seg_local, "seq", axis=0, tiled=True),
    )
    query_heads = queries.reshape(row_count, head_count, head_size)

    def block_scores(block_index):
        key_start = block_index * key_block
        key_heads = lax.dynamic_slice_in_dim(keys_all, key_start, key_block, 0).reshape(
            key_block, head_count, head_size
        )
        value_heads = lax.dynamic_slice_in_dim(values_all, key_start, key_block, 0).reshape(
            key_block, head_count, head_size
        )
        info_block = lax.dynamic_slice_in_dim(info_all, key_start, key_block, 0)
        key_pos = key_start + jnp.arange(key_block, dtype=jnp.int32)
        distance = query_pos[:, None] - key_pos[None, :]
        allowed = (distance >= 0) & ((info_block[None, :] == seg_local[:, None]) | (distance == 0))
        raw_scores = (
            jnp.einsum("qhd,khd->hqk", query_heads, key_heads, preferred_element_type=jnp.float32)
            * score_scale
        )
        raw_scores = raw_scores + block_bias(rel_table, edges_np, distance)
        return (
            jnp.where(allowed[None], raw_scores, -1e30),
            allowed[None],
            key_heads,
            value_heads,
            distance,
            key_start,
        )

    def max_step(block_index, running):
        top_score, row_total = running
        pieces = block_scores(block_index)
        new_top = jnp.maximum(top_score, jnp.max(pieces[0], axis=-1))
        exponent = jnp.where(pieces[1], jnp.exp(pieces[0] - new_top[:, :, None]), 0.0)
        return (new_top, row_total * jnp.exp(top_score - new_top) + jnp.sum(exponent, axis=-1))

    start_top = jnp.full((head_count, row_count), -1e30, jnp.float32)
    start_total = jnp.zeros((head_count, row_count), jnp.float32)
    top_score, row_total = lax.fori_loop(0, block_count, max_step, (start_top, start_total))
    log_total = top_score + jnp.log(row_total)

    def out_step(block_index, mixed_acc):
        pieces = block_scores(block_index)
        prob_low = jnp.where(pieces[1], jnp.exp(pieces[0] - log_total[:, :, None]), 0.0).astype(
            jnp.bfloat16
        )
        return mixed_acc + jnp.einsum(
            "hqk,khd->qhd", prob_low, pieces[3], preferred_element_type=jnp.float32
        )

    mixed_full = lax.fori_loop(
        0, block_count, out_step, jnp.zeros((row_count, head_count, head_size), jnp.float32)
    )
    mixed_low = mixed_full.reshape(row_count, model_width).astype(jnp.bfloat16)
    hidden_one = inputs + jnp.dot(mixed_low, full_attn, preferred_element_type=jnp.float32)
    scaled_two, factor_two = norm_stats(hidden_one)
    normed_two = (scaled_two * gain_two).astype(jnp.bfloat16)
    route_local = routes[0]
    expert_count = w_expert_in.shape[0]
    top_count = route_local.shape[1]
    flat_routes = route_local.reshape(-1)
    expert_hot = (flat_routes[:, None] == jnp.arange(expert_count, dtype=jnp.int32)).astype(
        jnp.int32
    )
    earlier = jnp.cumsum(expert_hot, axis=0) - expert_hot
    slot_index = jnp.sum(earlier * expert_hot, axis=1)
    slot_float = (
        (slot_index[:, None] == jnp.arange(CAP, dtype=jnp.int32))
        .astype(jnp.float32)
        .reshape(row_count, top_count, CAP)
    )
    expert_float = expert_hot.astype(jnp.float32).reshape(row_count, top_count, expert_count)
    dispatch = jnp.einsum(
        "tke,tkc->ect",
        expert_float.astype(jnp.bfloat16),
        slot_float.astype(jnp.bfloat16),
        preferred_element_type=jnp.float32,
    ).astype(jnp.bfloat16)
    slot_gate = jnp.einsum(
        "tke,tkc,tk->ec", expert_float, slot_float, gate_weights[0], precision=lax.Precision.HIGHEST
    )
    entered = jnp.einsum(
        "ect,td->ecd", dispatch, normed_two, preferred_element_type=jnp.float32
    ).astype(jnp.bfloat16)
    pre_act = jnp.einsum("ecd,edf->ecf", entered, full_in, preferred_element_type=jnp.float32)
    active = jax.nn.gelu(pre_act).astype(jnp.bfloat16)
    result = jnp.einsum("ecf,efd->ecd", active, full_out, preferred_element_type=jnp.float32)
    expert_low = (slot_gate[:, :, None] * result).astype(jnp.bfloat16)
    combined = jnp.einsum("ect,ecd->td", dispatch, expert_low, preferred_element_type=jnp.float32)
    output = (hidden_one + combined).astype(jnp.bfloat16)
    regathered = (
        lax.all_gather(w_qkv, ("dp", "seq"), axis=0, tiled=True),
        lax.all_gather(w_attn, ("dp", "seq"), axis=0, tiled=True),
        lax.all_gather(w_expert_in, ("dp", "seq"), axis=1, tiled=True),
        lax.all_gather(w_expert_out, ("dp", "seq"), axis=1, tiled=True),
    )
    back_qkv, back_attn, back_in, back_out = regathered
    grad_out_low = cotangent[0]
    grad_slots = jnp.einsum(
        "ect,td->ecd", dispatch, grad_out_low, preferred_element_type=jnp.float32
    )
    grad_result = (slot_gate[:, :, None] * grad_slots).astype(jnp.bfloat16)
    grad_w_out = jnp.einsum("ecf,ecd->efd", active, grad_result, preferred_element_type=jnp.float32)
    grad_active = jnp.einsum(
        "ecd,efd->ecf", grad_result, back_out, preferred_element_type=jnp.float32
    )
    unused_value, gelu_pull = jax.vjp(jax.nn.gelu, pre_act)
    grad_pre = gelu_pull(grad_active)[0].astype(jnp.bfloat16)
    grad_w_in = jnp.einsum("ecd,ecf->edf", entered, grad_pre, preferred_element_type=jnp.float32)
    grad_entered = jnp.einsum(
        "ecf,edf->ecd", grad_pre, back_in, preferred_element_type=jnp.float32
    ).astype(jnp.bfloat16)
    grad_normed_two = jnp.einsum(
        "ect,ecd->td", dispatch, grad_entered, preferred_element_type=jnp.float32
    )
    grad_hidden_norm, grad_gain_two = norm_back(grad_normed_two, scaled_two, factor_two, gain_two)
    grad_hidden = grad_out_low.astype(jnp.float32) + grad_hidden_norm
    branch_low = grad_hidden.astype(jnp.bfloat16)
    grad_w_attn = lax.dot_general(
        mixed_low, branch_low, (((0,), (0,)), ((), ())), preferred_element_type=jnp.float32
    )
    grad_mixed = lax.dot_general(
        branch_low, back_attn, (((1,), (1,)), ((), ())), preferred_element_type=jnp.float32
    ).astype(jnp.bfloat16)
    grad_mixed_heads = grad_mixed.reshape(row_count, head_count, head_size)
    row_delta = jnp.sum(grad_mixed_heads.astype(jnp.float32) * mixed_full, axis=-1).T

    def score_grads(pieces):
        prob_full = jnp.where(pieces[1], jnp.exp(pieces[0] - log_total[:, :, None]), 0.0)
        grad_prob = jnp.einsum(
            "qhd,khd->hqk", grad_mixed_heads, pieces[3], preferred_element_type=jnp.float32
        )
        grad_score = (prob_full * (grad_prob - row_delta[:, :, None])).astype(jnp.bfloat16)
        return (prob_full.astype(jnp.bfloat16), grad_score)

    start_query = jnp.zeros((row_count, head_count, head_size), jnp.float32)
    start_table = jnp.zeros((head_count, BUCKETS), jnp.float32)

    def back_step(block_index, running):
        grad_query, grad_key_all, grad_value_all, grad_table = running
        pieces = block_scores(block_index)
        prob_low, grad_score = score_grads(pieces)
        grad_query = (
            grad_query
            + jnp.einsum("hqk,khd->qhd", grad_score, pieces[2], preferred_element_type=jnp.float32)
            * score_scale
        )
        key_part = (
            jnp.einsum("hqk,qhd->khd", grad_score, query_heads, preferred_element_type=jnp.float32)
            * score_scale
        ).reshape(key_block, model_width)
        value_part = jnp.einsum(
            "hqk,qhd->khd", prob_low, grad_mixed_heads, preferred_element_type=jnp.float32
        ).reshape(key_block, model_width)
        grad_key_all = lax.dynamic_update_slice_in_dim(grad_key_all, key_part, pieces[5], 0)
        grad_value_all = lax.dynamic_update_slice_in_dim(grad_value_all, value_part, pieces[5], 0)
        grad_table = grad_table + table_part(grad_score, edges_np, pieces[4])
        return (grad_query, grad_key_all, grad_value_all, grad_table)

    start_back = (
        start_query,
        jnp.zeros((length, model_width), jnp.float32),
        jnp.zeros((length, model_width), jnp.float32),
        start_table,
    )
    grad_query, grad_key_all, grad_value_all, grad_table = lax.fori_loop(
        0, block_count, back_step, start_back
    )
    grad_keys, grad_values = (
        lax.psum_scatter(
            grad_key_all.astype(jnp.bfloat16), "seq", scatter_dimension=0, tiled=True
        ).astype(jnp.float32),
        lax.psum_scatter(
            grad_value_all.astype(jnp.bfloat16), "seq", scatter_dimension=0, tiled=True
        ).astype(jnp.float32),
    )
    grad_proj = jnp.concatenate(
        [
            grad_query.reshape(row_count, model_width).astype(jnp.bfloat16),
            grad_keys.astype(jnp.bfloat16),
            grad_values.astype(jnp.bfloat16),
        ],
        axis=1,
    )
    grad_w_qkv = lax.dot_general(
        normed_one, grad_proj, (((0,), (0,)), ((), ())), preferred_element_type=jnp.float32
    )
    grad_normed_one = lax.dot_general(
        grad_proj, back_qkv, (((1,), (1,)), ((), ())), preferred_element_type=jnp.float32
    )
    grad_input_norm, grad_gain_one = norm_back(grad_normed_one, scaled_one, factor_one, gain_one)
    grad_inputs = grad_hidden + grad_input_norm
    table_total, gain_one_total, gain_two_total = lax.psum(
        (grad_table, grad_gain_one, grad_gain_two), ("dp", "seq")
    )
    shares = (
        lax.psum_scatter(grad_w_qkv, ("dp", "seq"), scatter_dimension=0, tiled=True),
        lax.psum_scatter(grad_w_attn, ("dp", "seq"), scatter_dimension=0, tiled=True),
        lax.psum_scatter(grad_w_in, ("dp", "seq"), scatter_dimension=1, tiled=True),
        lax.psum_scatter(grad_w_out, ("dp", "seq"), scatter_dimension=1, tiled=True),
    )
    return (
        output[None],
        grad_inputs[None],
        gain_one_total,
        shares[0],
        shares[1],
        table_total,
        gain_two_total,
        shares[2],
        shares[3],
    )


def rows_solution(mesh):
    return jax.shard_map(
        body,
        mesh=mesh,
        in_specs=(
            P("dp", "seq", None),
            P("dp", "seq", None),
            P("dp", "seq"),
            P("dp", "seq"),
            P("dp", "seq", None),
            P("dp", "seq", None),
            P(),
            P(("dp", "seq"), None),
            P(("dp", "seq"), None),
            P(),
            P(),
            P(None, ("dp", "seq"), None),
            P(None, ("dp", "seq"), None),
        ),
        out_specs=(
            P("dp", "seq", None),
            P("dp", "seq", None),
            P(),
            P(("dp", "seq"), None),
            P(("dp", "seq"), None),
            P(),
            P(),
            P(None, ("dp", "seq"), None),
            P(None, ("dp", "seq"), None),
        ),
        check_vma=False,
    )


F32 = jnp.float32
BF16 = jnp.bfloat16
ROWS = 128
EXT = 128
TAB_AT = 256
AXES = ("z", "y", "x", "c")
MIB = 1024 * 1024
BYTES_US = 3690000


def swap(value, axis, step=1):
    size = lax.axis_size(axis)
    return lax.ppermute(value, axis, [(i, i ^ step) for i in range(size)])


def after(value, *earlier):
    return lax.optimization_barrier((value, earlier))[0]


def gather_seq(value):
    along_x = swap(value, "x")
    return value, along_x, swap(value, "c"), swap(along_x, "c")


def reduce_seq(keep, send):
    rows = keep.shape[0] // 2
    pair = keep + swap(send, "c").astype(F32)
    return pair[:rows] + swap(pair[rows:].astype(BF16), "x").astype(F32)


def mm(a, b):
    return lax.dot_general(a, b, (((1,), (0,)), ((), ())), preferred_element_type=F32)


def mm_t(a, b):
    return lax.dot_general(a, b, (((1,), (1,)), ((), ())), preferred_element_type=F32)


def t_mm(a, b):
    return lax.dot_general(a, b, (((0,), (0,)), ((), ())), preferred_element_type=F32)


SLOTS = (0, 2, 1, 3)


def slot_rows(slot, me):
    block = jnp.bitwise_xor(me, SLOTS[slot])
    return pl.ds(pl.multiple_of(block * ROWS, ROWS), ROWS)


def tile_distance(offset):
    row = lax.broadcasted_iota(jnp.int32, (ROWS, ROWS), 0)
    col = lax.broadcasted_iota(jnp.int32, (ROWS, ROWS), 1)
    return offset + row - col


def fill_bias(bias_ref, tab_ref, heads):
    edges = [int(e) for e in bucket_edges()]
    for near in range(2):
        distance = tile_distance(near * ROWS)
        tiles = [jnp.full((ROWS, ROWS), tab_ref[h, 0], F32) for h in range(heads)]
        for b, edge in enumerate(edges):
            above = distance >= edge
            tiles = [jnp.where(above, tab_ref[h, b + 1], tiles[h]) for h in range(heads)]
        for h in range(heads):
            bias_ref[near * heads + h] = tiles[h]


def read_marks(xs_ref, width, blocks):
    seg_cols, info_rows = [], []
    for i in range(blocks):
        marks = xs_ref[i * ROWS : (i + 1) * ROWS, width : width + EXT].astype(F32)
        seg_cols.append(marks[:, 0:1])
        info_rows.append(marks.T[1:2, :])
    return seg_cols, info_rows


def mask_tiles(i, seg_cols, info_rows):
    tiles = []
    for j in range(i + 1):
        seen = info_rows[j] == seg_cols[i]
        if j == i:
            distance = tile_distance(0)
            seen = (distance == 0) | ((distance > 0) & seen)
        tiles.append(jnp.where(seen, 0.0, -1e30))
    return tiles


def add_tiles(i, h, heads, masks, bias_ref, tab_ref):
    tiles = []
    for j in range(i + 1):
        if i - j < 2:
            tiles.append(masks[j] + bias_ref[(i - j) * heads + h])
        else:
            tiles.append(masks[j] + tab_ref[h, BUCKETS - 1])
    return jnp.concatenate(tiles, axis=1) if len(tiles) > 1 else tiles[0]


def copies(pairs, sem_ref):
    return [pltpu.make_async_copy(a, b, sem_ref.at[n]) for n, (a, b) in enumerate(pairs)]


def attend_kernel(
    me_ref,
    place_ref,
    tab_ref,
    x0_ref,
    x1_ref,
    x2_ref,
    x3_ref,
    gain_ref,
    *refs,
):
    w_refs = refs[:2]
    mixed_ref = refs[2]
    home = refs[3:8]
    kept = refs[8:13]
    blocks_ref, bias_ref, sem_ref = refs[13:]
    xs_ref, n1_ref, wq_ref, qkv_ref, lse_ref = kept
    out = copies(zip(kept, home), sem_ref)
    me, place = me_ref[0], place_ref[0]
    width = gain_ref.shape[1]
    third = wq_ref.shape[1] // 3
    heads = tab_ref.shape[0]
    size = third // heads
    blocks = xs_ref.shape[0] // ROWS
    devices, shard = blocks_ref.shape[0], blocks_ref.shape[1]
    scale = size ** (-0.5)
    fill_bias(bias_ref, tab_ref, heads)
    for slot, x_ref in enumerate((x0_ref, x1_ref, x2_ref, x3_ref)):
        rows = slot_rows(slot, me)
        xs_ref[rows, :] = x_ref[...]
        x = x_ref[:, :width].astype(F32)
        factor = lax.rsqrt(jnp.mean(x * x, axis=-1, keepdims=True) + 1e-06)
        n1_ref[rows, :] = (x * factor * gain_ref[...]).astype(BF16)
    out[0].start()
    out[1].start()
    for n, w_ref in enumerate(w_refs):
        y = jnp.bitwise_xor(jnp.bitwise_and(place, 1), n)
        for i in range(devices // 2):
            blocks_ref[(2 * (i // blocks) + y) * blocks + i % blocks] = w_ref[i]
    for i in range(devices):
        wq_ref[i * shard : (i + 1) * shard, :] = blocks_ref[i]
    out[2].start()
    qkv_ref[...] = mm(n1_ref[...], wq_ref[...]).astype(BF16)
    out[3].start()
    seg_cols, info_rows = read_marks(xs_ref, width, blocks)
    lane = lax.broadcasted_iota(jnp.int32, (ROWS, EXT), 1)
    for i in range(blocks):
        masks = mask_tiles(i, seg_cols, info_rows)
        span = (i + 1) * ROWS
        rows = slice(i * ROWS, span)
        outs = []
        lse = jnp.zeros((ROWS, EXT), F32)
        for h in range(heads):
            q = qkv_ref[rows, h * size : (h + 1) * size]
            k = qkv_ref[0:span, third + h * size : third + (h + 1) * size]
            v = qkv_ref[0:span, 2 * third + h * size : 2 * third + (h + 1) * size]
            scores = mm_t(q, k) * scale + add_tiles(i, h, heads, masks, bias_ref, tab_ref)
            top = jnp.max(scores, axis=-1, keepdims=True)
            weight = jnp.exp(scores - top)
            total = jnp.sum(weight, axis=-1, keepdims=True)
            prob = (weight * (1.0 / total)).astype(BF16)
            outs.append(mm(prob, v))
            lse = jnp.where(lane == h, top + jnp.log(total), lse)
        mixed_ref[rows, :] = jnp.concatenate(outs, axis=1).astype(BF16)
        lse_ref[rows, :] = lse
    out[4].start()
    for copy in out:
        copy.wait()


def project_kernel(me_ref, mixed_ref, watt_ref, keep_ref, send_ref):
    me = me_ref[0]
    for slot in range(len(SLOTS)):
        part = mm(mixed_ref[slot_rows(slot, me), :], watt_ref[...])
        if slot < 2:
            keep_ref[slot * ROWS : (slot + 1) * ROWS, :] = part
        else:
            send_ref[(slot - 2) * ROWS : (slot - 1) * ROWS, :] = part.astype(BF16)


def attend_back_kernel(
    me_ref,
    place_ref,
    tab_ref,
    b0_ref,
    b1_ref,
    b2_ref,
    b3_ref,
    watt_ref,
    gain_two_ref,
    *refs,
):
    home = refs[:6]
    wkeep_ref, wsend_ref, keep_ref, send_ref = refs[6:10]
    kept = refs[10:16]
    bias_ref, dm_ref, dk_ref, dv_ref, proj_ref, gtab_ref, small_ref, grad_ref, sem_ref = refs[16:]
    xs_ref, n1_ref, wq_ref, qkv_ref, lse_ref, mixed_ref = kept
    fetch = copies(zip(home, kept), sem_ref)
    for copy in fetch:
        copy.start()
    me = me_ref[0]
    width = watt_ref.shape[1]
    third = wq_ref.shape[1] // 3
    heads = tab_ref.shape[0]
    size = third // heads
    blocks = xs_ref.shape[0] // ROWS
    scale = size ** (-0.5)
    fill_bias(bias_ref, tab_ref, heads)
    for slot, b_ref in enumerate((b0_ref, b1_ref, b2_ref, b3_ref)):
        dm_ref[slot_rows(slot, me), :] = mm_t(b_ref[...], watt_ref[...]).astype(BF16)
    for copy in fetch:
        copy.wait()
    seg_cols, info_rows = read_marks(xs_ref, width, blocks)
    dk_ref[...] = jnp.zeros_like(dk_ref)
    dv_ref[...] = jnp.zeros_like(dv_ref)
    near = [[jnp.zeros((ROWS, ROWS), F32) for _ in range(heads)] for _ in range(2)]
    far = [jnp.zeros((1, ROWS), F32) for _ in range(heads)]
    for i in range(blocks):
        masks = mask_tiles(i, seg_cols, info_rows)
        span = (i + 1) * ROWS
        rows = slice(i * ROWS, span)
        for h in range(heads):
            own = slice(h * size, (h + 1) * size)
            q = qkv_ref[rows, own]
            k = qkv_ref[0:span, third + h * size : third + (h + 1) * size]
            v = qkv_ref[0:span, 2 * third + h * size : 2 * third + (h + 1) * size]
            dm = dm_ref[rows, own]
            scores = mm_t(q, k) * scale + add_tiles(i, h, heads, masks, bias_ref, tab_ref)
            prob = jnp.exp(scores - lse_ref[rows, h : h + 1])
            grad_prob = mm_t(dm, v)
            delta = jnp.sum(prob * grad_prob, axis=-1, keepdims=True)
            grad_score = (prob * (grad_prob - delta)).astype(BF16)
            proj_ref[rows, own] = (mm(grad_score, k) * scale).astype(BF16)
            dk_ref[0:span, own] += t_mm(grad_score, q)
            dv_ref[0:span, own] += t_mm(prob.astype(BF16), dm)
            for j in range(i + 1):
                tile = grad_score[:, j * ROWS : (j + 1) * ROWS].astype(F32)
                if i - j < 2:
                    near[i - j][h] = near[i - j][h] + tile
                else:
                    far[h] = far[h] + jnp.sum(tile, axis=0, keepdims=True)
    proj_ref[:, third : 2 * third] = (dk_ref[...] * scale).astype(BF16)
    proj_ref[:, 2 * third :] = dv_ref[...].astype(BF16)
    gtab_ref[...] = jnp.zeros_like(gtab_ref)
    edges = [int(e) for e in bucket_edges()]
    buckets = []
    for n in range(2):
        distance = tile_distance(n * ROWS)
        count = jnp.zeros((ROWS, ROWS), jnp.int32)
        for edge in edges:
            count = count + (distance >= edge).astype(jnp.int32)
        buckets.append(count)
    for b in range(BUCKETS):
        picks = [buckets[n] == b for n in range(2)]
        for h in range(heads):
            line = jnp.sum(
                jnp.where(picks[0], near[0][h], 0.0) + jnp.where(picks[1], near[1][h], 0.0),
                axis=0,
                keepdims=True,
            )
            if b == BUCKETS - 1:
                line = line + far[h]
            gtab_ref[h * BUCKETS + b : h * BUCKETS + b + 1, :] = line
    gain = jnp.zeros((1, width), F32)
    for slot in range(blocks):
        rows = slot_rows(slot, me)
        x = xs_ref[rows, :width].astype(F32)
        factor = lax.rsqrt(jnp.mean(x * x, axis=-1, keepdims=True) + 1e-06)
        part = mm_t(proj_ref[rows, :], wq_ref[...])
        if slot < 2:
            keep_ref[slot * ROWS : (slot + 1) * ROWS, :] = part
        else:
            send_ref[(slot - 2) * ROWS : (slot - 1) * ROWS, :] = part.astype(BF16)
        gain = gain + jnp.sum(part * (x * factor), axis=0, keepdims=True)
    wide = 3 * third
    table = jnp.sum(gtab_ref[...].T, axis=0, keepdims=True)
    small_ref[...] = jnp.zeros_like(small_ref)
    for n, value in enumerate((gain, gain_two_ref[...])):
        for m, piece in enumerate(halves(value)):
            small_ref[4 * n + 2 * m : 4 * n + 2 * m + 1, :] = piece[:, :wide]
            small_ref[4 * n + 2 * m + 1 : 4 * n + 2 * m + 2, : width - wide] = piece[:, wide:]
    for m, piece in enumerate(halves(table)):
        small_ref[2 * m + 1 : 2 * m + 2, TAB_AT : TAB_AT + EXT] = piece
    small = small_ref[...].astype(BF16)
    grad = t_mm(n1_ref[...], proj_ref[...])
    att = 0.0
    for slot, b_ref in enumerate((b0_ref, b1_ref, b2_ref, b3_ref)):
        att = att + t_mm(mixed_ref[slot_rows(slot, me), :], b_ref[...])
    groups, rows = grad_ref.shape[0], grad_ref.shape[1]
    shard = third // groups
    main = width // groups
    for n in range(groups):
        grad_ref[n, :main, :] = grad[n * main : (n + 1) * main, :]
        piece = att[n * shard : (n + 1) * shard, :]
        grad_ref[n, main : main + shard, :] = piece[:, :wide]
        for m in range(3):
            grad_ref[n, main + shard :, m * third : (m + 1) * third] = piece[
                m * 8 : (m + 1) * 8, wide:
            ]
    own = jnp.bitwise_and(place_ref[0], 1)
    for z in range(groups // 2):
        wkeep_ref[z * rows : (z + 1) * rows, :] = grad_ref[2 * z + own]
        wsend_ref[z * rows : (z + 1) * rows, :] = grad_ref[2 * z + 1 - own].astype(BF16)
    wkeep_ref[groups // 2 * rows :, :] = small.astype(F32)
    wsend_ref[groups // 2 * rows :, :] = small


def halves(value):
    high = value.astype(BF16).astype(F32)
    return high, value - high


def split_small(rows):
    pieces = []
    for n in range(2):
        pieces += halves(rows[4 * n : 4 * n + 2] + rows[4 * n + 2 : 4 * n + 4])
    return jnp.concatenate(pieces, axis=0).astype(BF16)


def fold_y_kernel(place_ref, keep_ref, got_ref, own_ref, *refs):
    sends, block_ref = refs[:-1], refs[-1]
    count, rows = block_ref.shape[0], block_ref.shape[1]
    total = keep_ref[...] + got_ref[...].astype(F32)
    for z in range(count):
        block_ref[z] = total[z * rows : (z + 1) * rows, :]
    small = split_small(total[count * rows :, :])
    me = jnp.right_shift(place_ref[0], 1)
    own_ref[:rows, :] = block_ref[me]
    own_ref[rows:, :] = small.astype(F32)
    for k, send_ref in enumerate(sends):
        send_ref[:rows, :] = block_ref[jnp.bitwise_xor(me, k + 1)].astype(BF16)
        send_ref[rows:, :] = small


def fold_z_kernel(me_ref, own_ref, *refs):
    gots, att_ref, keep_ref, sends, block_ref = refs[:3], refs[3], refs[4], refs[5:-1], refs[-1]
    count, shard, wide = block_ref.shape
    third = wide // 3
    total = (own_ref[...] + gots[0][...].astype(F32)) + (
        gots[1][...].astype(F32) + gots[2][...].astype(F32)
    )
    for s in range(count):
        block_ref[s] = total[s * shard : (s + 1) * shard, :]
    main = count * shard
    att_ref[:, :wide] = total[main : main + shard, :].astype(BF16)
    rest = total[main + shard : main + shard + 8, :]
    att_ref[:, wide:] = jnp.concatenate(
        [rest[:, m * third : (m + 1) * third] for m in range(3)], axis=0
    ).astype(BF16)
    small = split_small(total[main + shard + 8 :, :])
    keep_ref[:shard, :] = block_ref[me_ref[0]]
    keep_ref[shard:, :] = small.astype(F32)
    for k, send_ref in enumerate(sends):
        send_ref[:shard, :] = block_ref[jnp.bitwise_xor(me_ref[0], SLOTS[k + 1])].astype(BF16)
        send_ref[shard:, :] = small


def fold_seq_kernel(me_ref, *refs):
    pieces, gwq_ref, one_ref, two_ref, tab_ref, block_ref, table_ref = (
        refs[:4],
        *refs[4:],
    )
    parts, shard = block_ref.shape[0], block_ref.shape[1]
    wide = block_ref.shape[2]
    width = one_ref.shape[1]
    third = wide // 3
    values = [piece[...].astype(F32) for piece in pieces]
    for slot, value in enumerate(values):
        s = jnp.bitwise_xor(me_ref[0], SLOTS[slot])
        block_ref[s] = value[:shard]
        table_ref[s] = jnp.broadcast_to(
            (value[shard + 1 : shard + 2] + value[shard + 3 : shard + 4])[
                :, TAB_AT : TAB_AT + EXT
            ],
            (8, EXT),
        )
    for s in range(parts):
        for n in range(3):
            at = n * width + s * third
            gwq_ref[:, at : at + third] = block_ref[s, :, n * third : (n + 1) * third]
        tab_ref[s : s + 1, :] = table_ref[s, 0:1, :]
    small = (values[0][shard:] + values[1][shard:]) + (values[2][shard:] + values[3][shard:])
    for n, out_ref in enumerate((one_ref, two_ref)):
        out_ref[:, :wide] = small[4 * n : 4 * n + 1] + small[4 * n + 2 : 4 * n + 3]
        rest = small[4 * n + 1 : 4 * n + 2] + small[4 * n + 3 : 4 * n + 4]
        out_ref[:, wide:] = rest[:, : width - wide]


def qkv_send_kernel(w_ref, send_ref):
    count, shard, wide = send_ref.shape
    third = wide // 3
    width = w_ref.shape[1] // 3
    parts = width // third
    for p in range(parts):
        for n in range(3):
            at = n * width + p * third
            piece = w_ref[:, at : at + third]
            for i in range(p, count, parts):
                send_ref[i, :, n * third : (n + 1) * third] = piece


def in_send_kernel(w_ref, send_ref):
    devices, shard, wide = send_ref.shape
    experts = w_ref.shape[0]
    own = wide // experts
    for i in range(devices):
        for e in range(experts):
            send_ref[i, :, e * own : (e + 1) * own] = w_ref[e, :, i * own : (i + 1) * own]


def in_last_kernel(got_ref, grad_ref):
    devices, shard, wide = got_ref.shape
    experts = grad_ref.shape[0]
    own = wide // experts
    for i in range(devices):
        for e in range(experts):
            grad_ref[e, :, i * own : (i + 1) * own] = got_ref[
                i, :, e * own : (e + 1) * own
            ].astype(F32)


def expert_kernel(
    xa_ref,
    xb_ref,
    ga_ref,
    gb_ref,
    w1a_ref,
    w1b_ref,
    w2a_ref,
    w2b_ref,
    pick_ref,
    act_home,
    pre_home,
    keep_ref,
    send_ref,
    x_ref,
    g_ref,
    act_ref,
    pre_ref,
    sem_ref,
):
    rows, width = xa_ref.shape
    half = w1a_ref.shape[1]
    tile_cols = 256
    root = math.sqrt(2.0 / math.pi)
    x_ref[:rows, :] = xa_ref[...]
    x_ref[rows:, :] = xb_ref[...]
    g_ref[:rows, :] = ga_ref[...]
    g_ref[rows:, :] = gb_ref[...]

    def tile(t, carry):
        cols = pl.ds(pl.multiple_of(t * tile_cols, tile_cols), tile_cols)
        for side, (w1_ref, w2_ref) in enumerate(((w1a_ref, w2a_ref), (w1b_ref, w2b_ref))):
            out_cols = pl.ds(pl.multiple_of(side * half + t * tile_cols, tile_cols), tile_cols)
            choose = mm(g_ref[:, width:], pick_ref[:, cols])
            v = mm(x_ref[...], w1_ref[:, cols])
            square = v * v
            curve = jnp.tanh(root * v * (1.0 + 0.044715 * square))
            part = 0.5 * (1.0 + curve)
            slope = part + 0.5 * v * (1.0 - curve * curve) * (
                root * (1.0 + 3 * 0.044715 * square)
            )
            act_ref[:, out_cols] = (choose * (v * part)).astype(BF16)
            grad_act = mm_t(g_ref[:, :width], w2_ref[cols, :])
            grad_pre = (choose * grad_act * slope).astype(BF16)
            pre_ref[:, out_cols] = grad_pre
        return carry

    lax.fori_loop(0, half // tile_cols, tile, 0)
    home = copies([(act_ref, act_home), (pre_ref, pre_home)], sem_ref)
    for copy in home:
        copy.start()
    grad_x = mm_t(pre_ref[:, :half], w1a_ref[...]) + mm_t(pre_ref[:, half:], w1b_ref[...])
    keep_ref[...] = grad_x[:rows, :]
    send_ref[...] = grad_x[rows:, :].astype(BF16)
    for copy in home:
        copy.wait()


def expert_out_kernel(count, w2a_ref, w2b_ref, *refs):
    acts, keep_ref, send_ref, act_ref, sem_ref = refs[:count], *refs[count:]
    rows = keep_ref.shape[1]
    half = w2a_ref.shape[0]
    fetch = copies([(act, act_ref.at[k]) for k, act in enumerate(acts)], sem_ref)
    for copy in fetch:
        copy.start()
    for k in range(count):
        fetch[k].wait()
        out = mm(act_ref[k, :, :half], w2a_ref[...]) + mm(act_ref[k, :, half:], w2b_ref[...])
        keep_ref[k] = out[:rows]
        send_ref[k] = out[rows:].astype(BF16)


def in_grad_kernel(count, *refs):
    xs, pres = refs[: 2 * count], refs[2 * count : 3 * count]
    own_ref, far_ref, xt_ref, pre_ref, sem_ref = refs[3 * count :]
    rows = xs[0].shape[0]
    half = own_ref.shape[1]
    step = 256
    fetch = copies(
        [(p, pre_ref.at[pl.ds(k * 2 * rows, 2 * rows)]) for k, p in enumerate(pres)], sem_ref
    )
    for copy in fetch:
        copy.start()
    for k in range(2 * count):
        xt_ref[:, k * rows : (k + 1) * rows] = xs[k][...].T
    for copy in fetch:
        copy.wait()

    def tile(t, carry):
        cols = pl.ds(pl.multiple_of(t * step, step), step)
        cols_far = pl.ds(pl.multiple_of(half + t * step, step), step)
        far_ref[:, cols] = mm(xt_ref[...], pre_ref[:, cols_far]).astype(BF16)
        own_ref[:, cols] = mm(xt_ref[...], pre_ref[:, cols])
        return carry

    lax.fori_loop(0, half // step, tile, 0)


def out_grad_kernel(count, *refs):
    gs, acts = refs[: 2 * count], refs[2 * count : 3 * count]
    own_ref, far_ref, g_ref, act_ref, sem_ref = refs[3 * count :]
    rows = gs[0].shape[0]
    half, width = own_ref.shape
    step = 256
    pairs = [(a, act_ref.at[pl.ds(k * 2 * rows, 2 * rows)]) for k, a in enumerate(acts)]
    for n, g in enumerate(gs):
        pairs.append((g, g_ref.at[pl.ds(n * rows, rows)]))
    fetch = copies(pairs, sem_ref)
    for copy in fetch:
        copy.start()
    for copy in fetch:
        copy.wait()

    def tile(t, carry):
        cols = pl.ds(pl.multiple_of(t * step, step), step)
        cols_far = pl.ds(pl.multiple_of(half + t * step, step), step)
        far_ref[cols, :] = t_mm(act_ref[:, cols_far], g_ref[:, :width]).astype(BF16)
        own_ref[cols, :] = t_mm(act_ref[:, cols], g_ref[:, :width])
        return carry

    lax.fori_loop(0, half // step, tile, 0)


def call(kernel, outs, args, us, scratch=(), scalars=0, far=(), home=(), mib=60):
    smem = pl.BlockSpec(memory_space=pltpu.SMEM)
    vmem = pl.BlockSpec(memory_space=pltpu.VMEM)
    hbm = pl.BlockSpec(memory_space=pltpu.HBM)
    return pl.pallas_call(
        kernel,
        out_shape=[jax.ShapeDtypeStruct(shape, dtype) for shape, dtype in outs],
        in_specs=[smem] * scalars
        + [hbm if n in far else vmem for n in range(scalars, len(args))],
        out_specs=[hbm if n in home else vmem for n in range(len(outs))],
        scratch_shapes=list(scratch),
        compiler_params=pltpu.CompilerParams(vmem_limit_bytes=mib * MIB),
        cost_estimate=pl.CostEstimate(
            flops=0, bytes_accessed=int(us * BYTES_US), transcendentals=0
        ),
    )(*args)


def head_body(
    tokens,
    cotangent,
    segment_ids,
    pad_mask,
    routes,
    gate_weights,
    gain_one,
    w_qkv,
    w_attn,
    rel_table,
    gain_two,
    w_expert_in,
    w_expert_out,
):
    x_low = tokens[0]
    g_low = cotangent[0]
    rows, width = x_low.shape
    size_z, size_y, size_x, size_c = (lax.axis_size(a) for a in AXES)
    parts = size_x * size_c
    devices = size_z * size_y * parts
    me = lax.axis_index(("x", "c"))
    head_count = rel_table.shape[0]
    heads = head_count // parts
    third = width // parts
    length = rows * parts
    experts, shard, ff = w_expert_in.shape
    ff_own = ff // devices
    me_arr = me.astype(jnp.int32).reshape(1)

    seg = segment_ids[0]
    info = jnp.where(pad_mask[0] == 1, seg, -1)
    marks = jnp.stack([seg, info], axis=1).astype(BF16)
    x_ext = jnp.concatenate([x_low, jnp.pad(marks, ((0, 0), (0, EXT - 2)))], axis=1)
    x_slots = gather_seq(x_ext)

    groups = devices // parts
    across = [(i, i ^ 3) for i in range(parts)]
    to_part = [((i % groups) * parts + i // groups) for i in range(devices)]
    expert_ids = jnp.arange(experts, dtype=jnp.int32)
    choose = jnp.sum(
        gate_weights[0][:, :, None] * (routes[0][:, :, None] == expert_ids).astype(F32), axis=1
    )
    choose_hi = choose.astype(BF16)
    choose_lo = (choose - choose_hi.astype(F32)).astype(BF16)
    g_ext = jnp.concatenate(
        [g_low, choose_hi, choose_lo, jnp.zeros((rows, EXT - 2 * experts), BF16)], axis=1
    )
    g_own = [g_ext] + [swap(g_ext, "z", k) for k in range(1, size_z)]
    g_far = [swap(g, "y") for g in g_own]

    q_send = call(
        qkv_send_kernel,
        [((devices // 2, shard, 3 * third), BF16)],
        [w_qkv],
        us=1,
        mib=8,
    )[0]
    q_own = lax.all_to_all(q_send, ("z", "x", "c"), 0, 0, tiled=True)

    att_one = lax.ppermute(w_attn, AXES, [(i, to_part[i]) for i in range(devices)])
    z_index = lax.axis_index("z")
    y_index = lax.axis_index("y")
    att_z = jnp.zeros((size_z, shard, width), BF16)
    for k in range(size_z):
        piece = att_one if k == 0 else swap(att_one, "z", k)
        att_z = lax.dynamic_update_slice_in_dim(
            att_z, piece[None], jnp.bitwise_xor(z_index, k), 0
        )
    att_y = swap(att_z, "y")
    watt = jnp.where(
        y_index == 0, jnp.stack([att_z, att_y], axis=1), jnp.stack([att_y, att_z], axis=1)
    ).reshape(third, width)

    w2_own = w_expert_out.reshape(experts * ff_own, width)
    w2_x = swap(w2_own, "x")
    w2a = jnp.concatenate([w2_own, w2_x], axis=0)
    w2b = swap(w2a, "c")
    q_own = after(q_own, att_z, x_slots, w2_x)
    q_far = swap(q_own, "y")

    in_send = call(
        in_send_kernel,
        [((devices, shard, experts * ff_own), BF16)],
        [w_expert_in],
        us=1.2,
        mib=16,
    )[0]
    in_send = after(in_send, q_own)
    w1_own = lax.all_to_all(in_send, AXES, 0, 0, tiled=True).reshape(width, experts * ff_own)

    w1_x = swap(w1_own, "x")

    place_arr = lax.axis_index(("z", "y")).astype(jnp.int32).reshape(1)

    table = lax.dynamic_slice_in_dim(rel_table, me * heads, heads, 0).astype(F32)
    half = length // 2
    kept = [
        ((length, width + EXT), BF16),
        ((length, width), BF16),
        ((width, 3 * third), BF16),
        ((length, 3 * third), BF16),
        ((length, EXT), F32),
    ]
    kept_scratch = [pltpu.VMEM(shape, dtype) for shape, dtype in kept]
    mixed, *saved = call(
        attend_kernel,
        [((length, third), BF16), *kept],
        [me_arr, place_arr, table, *x_slots, gain_one.reshape(1, width), q_own, q_far],
        scratch=[
            *kept_scratch,
            pltpu.VMEM((devices, shard, 3 * third), BF16),
            pltpu.VMEM((2 * heads, ROWS, ROWS), F32),
            pltpu.SemaphoreType.DMA((5,)),
        ],
        scalars=3,
        home=range(1, 6),
        us=8,
        mib=60,
    )
    saved = [*saved, mixed]
    keep, send = call(
        project_kernel,
        [((half, width), F32), ((half, width), BF16)],
        [me_arr, after(mixed, g_own), watt],
        scalars=1,
        us=1,
        mib=16,
    )
    inputs = x_low.astype(F32)
    hidden_one = after(inputs, w1_own) + reduce_seq(keep, send)
    scaled_two, factor_two = norm_stats(hidden_one)
    normed_two = (scaled_two * gain_two).astype(BF16)

    ff_two = parts * experts * ff_own
    pick_np = np.zeros((EXT, ff_two // 2), np.float32)
    for col in range(ff_two // 2):
        e = col // ff_own % experts
        pick_np[[e, experts + e], col] = 1.0
    pick = jnp.asarray(pick_np, BF16)
    pair = 2 * rows
    x_own = [normed_two] + [swap(normed_two, "z", k) for k in range(1, size_z)]
    x_far = [swap(after(x, g_far, x_own[2]) if k == 1 else x, "y") for k, x in enumerate(x_own)]
    w1a = jnp.concatenate([after(w1_own, x_far[1]), after(w1_x, x_far[1])], axis=1)
    w1b = swap(w1a, "c")
    order = [*range(1, size_z), 0]
    acts, pres, keeps, gots, backs, far_back = {}, {}, {}, {}, {}, {}
    for n, k in enumerate(order):
        earlier = [acts[order[n - 1]]] if n else []
        if n >= 2:
            earlier.append(backs[order[n - 2]])
        if n >= 3:
            earlier.append(far_back[order[n - 3]])
        x_here = after(x_own[k], *earlier)
        act, pre, dx_keep, dx_send = call(
            expert_kernel,
            [
                ((pair, ff_two), BF16),
                ((pair, ff_two), BF16),
                ((rows, width), F32),
                ((rows, width), BF16),
            ],
            [x_here, x_far[k], g_own[k], g_far[k], w1a, w1b, w2a, w2b, pick],
            scratch=[
                pltpu.VMEM((pair, width), BF16),
                pltpu.VMEM((pair, width + EXT), BF16),
                pltpu.VMEM((pair, ff_two), BF16),
                pltpu.VMEM((pair, ff_two), BF16),
                pltpu.SemaphoreType.DMA((2,)),
            ],
            home=(0, 1),
            mib=20,
        us=5.5,
        )
        acts[k], pres[k], keeps[k] = act, pre, dx_keep
        gots[k] = swap(dx_send, "y")
        backs[k] = dx_keep + gots[k].astype(F32)
        if k:
            far_back[k] = swap(backs[k].astype(BF16), "z", k)
    acts, pres = [acts[k] for k in range(size_z)], [pres[k] for k in range(size_z)]
    ready = [keeps[order[-1]], backs[order[-2]]]

    ff_half = ff_two // 2
    out_keep, out_send = call(
        functools.partial(expert_out_kernel, size_z),
        [((size_z, rows, width), F32), ((size_z, rows, width), BF16)],
        [w2a, w2b, after(acts[0], *ready), *acts[1:]],
        scratch=[
            pltpu.VMEM((size_z, pair, ff_two), BF16),
            pltpu.SemaphoreType.DMA((size_z,)),
        ],
        far=range(2, 2 + size_z),
        us=4.4,
        mib=24,
    )
    in_own, in_far = call(
        functools.partial(in_grad_kernel, size_z),
        [((width, ff_half), F32), ((width, ff_half), BF16)],
        [*[x for both in zip(x_own, x_far) for x in both], *pres[:-1], after(pres[-1], out_send)],
        scratch=[
            pltpu.VMEM((width, size_z * pair), BF16),
            pltpu.VMEM((size_z * pair, ff_two), BF16),
            pltpu.SemaphoreType.DMA((size_z,)),
        ],
        far=range(2 * size_z, 3 * size_z),
        us=6,
        mib=24,
    )
    grad_normed_two = after(backs[0], in_far)
    for k in range(1, size_z):
        grad_normed_two = grad_normed_two + far_back[k].astype(F32)

    grad_hidden_norm, gain_two_part = norm_back(grad_normed_two, scaled_two, factor_two, gain_two)
    grad_hidden = g_low.astype(F32) + grad_hidden_norm
    branch_low = grad_hidden.astype(BF16)
    branch = gather_seq(branch_low)

    quarter = ff_half // 2
    in_c = after(in_own, branch_low) + swap(in_far, "c").astype(F32)
    in_x_got = swap(after(in_c[:, quarter:].astype(BF16), branch[1]), "x")
    out_y = out_keep + swap(out_send, "y").astype(F32)
    extra = 8
    wide = 3 * third
    rows_y = parts * shard + shard * width // wide
    w_keep, w_send, gno_keep, gno_send = call(
        attend_back_kernel,
        [
            ((size_z * rows_y + extra, wide), F32),
            ((size_z * rows_y + extra, wide), BF16),
            ((half, width), F32),
            ((half, width), BF16),
        ],
        [
            me_arr,
            place_arr,
            table,
            *branch,
            watt,
            after(gain_two_part.reshape(1, width), out_y, in_c),
            *saved,
        ],
        scratch=[
            *kept_scratch,
            pltpu.VMEM((length, third), BF16),
            pltpu.VMEM((2 * heads, ROWS, ROWS), F32),
            pltpu.VMEM((length, third), BF16),
            pltpu.VMEM((length, third), F32),
            pltpu.VMEM((length, third), F32),
            pltpu.VMEM((length, wide), BF16),
            pltpu.VMEM((EXT, ROWS), F32),
            pltpu.VMEM((extra, wide), F32),
            pltpu.VMEM((groups, rows_y, wide), F32),
            pltpu.SemaphoreType.DMA((6,)),
        ],
        scalars=3,
        far=range(9, 15),
        us=10,
        mib=60,
    )
    out_z = [swap(out_y[k].astype(BF16), "z", k) for k in range(1, size_z)]
    w_send = after(w_send, in_x_got, out_z)
    in_x = after(in_c[:, :quarter], w_send) + in_x_got.astype(F32)
    in_x_low = in_x.astype(BF16).reshape(devices, shard, quarter)
    in_got = lax.all_to_all(in_x_low, AXES, 0, 0, tiled=True)
    combined = after(out_y[0], w_send)
    for got in out_z:
        combined = combined + got.astype(F32)
    output = (hidden_one + combined).astype(BF16)
    first_act = after(acts[0], w_send)
    out_own, out_far = call(
        functools.partial(out_grad_kernel, size_z),
        [((ff_half, width), F32), ((ff_half, width), BF16)],
        [*[g for both in zip(g_own, g_far) for g in both], first_act, *acts[1:]],
        scratch=[
            pltpu.VMEM((size_z * pair, width + EXT), BF16),
            pltpu.VMEM((size_z * pair, ff_two), BF16),
            pltpu.SemaphoreType.DMA((3 * size_z,)),
        ],
        far=range(3 * size_z),
        us=6.5,
        mib=24,
    )
    z_keep, *z_sends = call(
        fold_y_kernel,
        [((rows_y + extra, wide), F32)] + [((rows_y + extra, wide), BF16)] * (size_z - 1),
        [place_arr, after(w_keep, out_far), swap(w_send, "y")],
        scratch=[pltpu.VMEM((size_z, rows_y, wide), F32)],
        scalars=1,
        mib=12,
        us=1,
    )
    out_c = out_own + swap(out_far, "c").astype(F32)
    out_x_got = swap(out_c[quarter:].astype(BF16), "x")
    att_share, s_keep, *s_sends = call(
        fold_z_kernel,
        [((shard, width), BF16), ((shard + extra, wide), F32)]
        + [((shard + extra, wide), BF16)] * (parts - 1),
        [me_arr, after(z_keep, out_x_got), *[swap(piece, "z", k + 1) for k, piece in enumerate(z_sends)]],
        scratch=[pltpu.VMEM((parts, shard, wide), F32)],
        scalars=1,
        mib=12,
        us=1,
    )
    grad_w_qkv, one_sum, two_sum, table_sum = call(
        fold_seq_kernel,
        [
            ((shard, 3 * width), F32),
            ((1, width), F32),
            ((1, width), F32),
            ((parts, EXT), F32),
        ],
        [
            me_arr,
            s_keep,
            swap(s_sends[0], "x"),
            swap(s_sends[1], "c"),
            lax.ppermute(s_sends[2], ("x", "c"), across),
        ],
        scratch=[
            pltpu.VMEM((parts, shard, wide), F32),
            pltpu.VMEM((parts, 8, EXT), F32),
        ],
        scalars=1,
        mib=12,
        us=1,
    )

    grad_normed_one = reduce_seq(after(gno_keep, z_keep), after(gno_send, z_keep))
    scaled_one, factor_one = norm_stats(inputs)
    grad_input_norm, unused_gain = norm_back(grad_normed_one, scaled_one, factor_one, gain_one)
    grad_inputs = grad_hidden + grad_input_norm

    grad_w_in = call(
        in_last_kernel, [((experts, shard, ff), F32)], [after(in_got, out_c)], us=1.3, mib=16
    )[0]
    grad_w_out = (out_c[:quarter] + out_x_got.astype(F32)).reshape(experts, ff_own, width)

    grad_w_attn = lax.ppermute(
        att_share, AXES, [(to_part[i], i) for i in range(devices)]
    ).astype(F32)
    return (
        output[None],
        grad_inputs[None],
        one_sum[0],
        grad_w_qkv,
        grad_w_attn,
        table_sum[:, : heads * BUCKETS].reshape(head_count, BUCKETS),
        two_sum[0],
        grad_w_in,
        grad_w_out,
    )


def heads_fit(mesh):
    return mesh.shape["seq"] == 4 and mesh.shape["dp"] == 8


def solution(mesh):
    if not heads_fit(mesh):
        return rows_solution(mesh)
    grid = Mesh(mesh.devices.reshape(mesh.shape["dp"] // 2, 2, mesh.shape["seq"] // 2, 2), AXES)
    by_token = P(("z", "y"), ("x", "c"))
    by_row = P(AXES, None)
    by_second = P(None, AXES, None)
    return jax.shard_map(
        head_body,
        mesh=grid,
        in_specs=(
            by_token,
            by_token,
            by_token,
            by_token,
            by_token,
            by_token,
            P(),
            by_row,
            by_row,
            P(),
            P(),
            by_second,
            by_second,
        ),
        out_specs=(
            by_token,
            by_token,
            P(),
            by_row,
            by_row,
            P(),
            P(),
            by_second,
            by_second,
        ),
        check_vma=False,
    )
```
